32 devices in a mesh: depth: 4 (over y, core), image: 8 (over z, x).
Axes of the slice: x: 2, y: 2, z: 4, core: 2. Of those that a mesh axis runs over, the one named last changes fastest.
Arguments:
- populations: float32 [19, 128, 128, 128], P(None, 'depth', 'image'), may hold values from 0 to 0.4, as said below
- transfer: float32 [8, 5, 8], P('image'), may hold values from 0.1 to 1
- direction: int32 [8], P('image'), may hold values from 0 to 1
Outputs:
- final_populations: float32 [19, 128, 128, 128], P(None, 'depth', 'image')
- vorticity: bfloat16 [128, 128, 128], P('depth', 'image')
- images: float32 [8, 4, 128, 128], P('image', None, 'depth')
The draws below stay inside these ranges and needn't reach their ends.
Inputs may be any that keep to these rules, and one draw needn't show every extreme that they name: `populations`: each population is positive, its lattice weight times a density near one with a perturbation by a rough flow of small speed. `direction`: 0 views from the side of small x, 1 from the side of large x.
All inputs are finite; a program needn't handle non-finite values.
Results may differ from the reference program's by a relative error of at most 0.001.
Values may be sent and summed in bfloat16 or wider, within the bound.
A program may use at most 128 MiB of HBM per device.

```python
import jax
import jax.numpy as jnp
from jax import lax

NZ = 128
STEPS = 4
TF_BUMPS = 8
NX = 128
NY = 128
TFS = 8


lattice_velocities = ((0, 0, 0), (1, 0, 0), (-1, 0, 0), (0, 1, 0), (0, -1, 0), (0, 0, 1), (0, 0, -1), (1, 1, 0), (-1, -1, 0), (1, -1, 0), (-1, 1, 0), (1, 0, 1), (-1, 0, -1), (1, 0, -1), (-1, 0, 1), (0, 1, 1), (0, -1, -1), (0, 1, -1), (0, -1, 1))


lattice_weights = (1.0 / 3.0,) + (1.0 / 18.0,) * 6 + (1.0 / 36.0,) * 12


def draw_populations(key, part):
    flow_key = jax.random.fold_in(key, 11)
    noise_key = jax.random.fold_in(key, 23)
    flow = jnp.clip(0.05 * jax.random.normal(flow_key, (3, NX, NY, NZ), jnp.float32), -0.12, 0.12)
    noise = jax.random.uniform(noise_key, (19, NX, NY, NZ), jnp.float32, -0.1, 0.1)
    pieces = []
    for number in range(19):
        project = jnp.zeros((NX, NY, NZ), jnp.float32)
        for axis_index in range(3):
            factor = lattice_velocities[number][axis_index]
            if factor != 0:
                project = project + factor * flow[axis_index]
        pieces.append(lattice_weights[number] * (1.0 + 3.0 * project + noise[number]))
    return jnp.stack(pieces).astype(jnp.float32)


def place_ends(drawn, rng, least, top_value):
    longest = drawn.shape.index(max(drawn.shape))
    spots = []
    for shift in (0, 1):
        where = [jax.random.randint(jax.random.fold_in(rng, axis), (), 0, length) for axis, length in enumerate(drawn.shape)]
        where[longest] = (where[longest] + shift) % drawn.shape[longest]
        spots.append(tuple(where))
    return drawn.at[spots[0]].set(least).at[spots[1]].set(top_value)


def level_of(rng, shape, split, least, top_value):
    loudness, own = 1.0, jax.random.fold_in(rng, 6)
    for dim, parts in split:
        heights = jnp.exp(jax.random.uniform(jax.random.fold_in(own, dim), (parts,), jnp.float32, least / len(split), top_value / len(split)))
        loudness = loudness * jnp.repeat(heights, shape[dim] // parts).reshape([-1 if axis == dim else 1 for axis in range(len(shape))])
    return loudness


def setup_inputs(seed: int = 0) -> dict:
    splits = jax.random.split(jax.random.key(seed), 4)
    return {
        "populations": draw_populations(jax.random.fold_in(splits[3], 71), 0),
        "transfer": jnp.clip(0.1 + 0.9 * jax.random.uniform(splits[1], (TFS, 5, TF_BUMPS), jnp.float32) ** level_of(splits[1], (TFS, 5, TF_BUMPS), ((0, 8),), -0.2, 0.2), 0.1, 1.0),
        "direction": place_ends(jax.random.randint(splits[2], (TFS,), 0, 2), jax.random.fold_in(splits[2], 1), 0, 1).astype(jnp.int32),
    }


lattice_velocities = ((0, 0, 0), (1, 0, 0), (-1, 0, 0), (0, 1, 0), (0, -1, 0), (0, 0, 1), (0, 0, -1), (1, 1, 0), (-1, -1, 0), (1, -1, 0), (-1, 1, 0), (1, 0, 1), (-1, 0, -1), (1, 0, -1), (-1, 0, 1), (0, 1, 1), (0, -1, -1), (0, 1, -1), (0, -1, 1))
lattice_weights = (1.0 / 3.0,) + (1.0 / 18.0,) * 6 + (1.0 / 36.0,) * 12
relaxation = 1.25
bump_width = 0.15
level_offset = 0.05

def moments(field):
    density = field[0]
    for number in range(1, 19):
        density = density + field[number]
    components = []
    for axis_index in range(3):
        total = jnp.zeros_like(density)
        for number in range(19):
            factor = lattice_velocities[number][axis_index]
            if factor != 0:
                total = total + factor * field[number]
        components.append(total / density)
    return (density, components)

def collide(field):
    density, flow = moments(field)
    squared = flow[0] * flow[0] + flow[1] * flow[1] + flow[2] * flow[2]
    result = []
    for number in range(19):
        project = jnp.zeros_like(density)
        for axis_index in range(3):
            factor = lattice_velocities[number][axis_index]
            if factor != 0:
                project = project + factor * flow[axis_index]
        equilibrium = lattice_weights[number] * density * (1.0 + 3.0 * project + 4.5 * project * project - 1.5 * squared)
        result.append(field[number] - relaxation * (field[number] - equilibrium))
    return result

def slope(values, axis_index):
    return (jnp.roll(values, -1, axis_index) - jnp.roll(values, 1, axis_index)) * 0.5

def reference(populations, transfer, direction):
    field = populations
    for turn_index in range(STEPS):
        collided = collide(field)
        field = jnp.stack([jnp.roll(collided[number], lattice_velocities[number], axis=(0, 1, 2)) for number in range(19)])
    density, flow = moments(field)
    spin_x = slope(flow[2], 1) - slope(flow[1], 2)
    spin_y = slope(flow[0], 2) - slope(flow[2], 0)
    spin_z = slope(flow[1], 0) - slope(flow[0], 1)
    vorticity = jnp.sqrt(spin_x * spin_x + spin_y * spin_y + spin_z * spin_z).astype(jnp.bfloat16)
    level = vorticity.astype(jnp.float32)
    level = level / (level + level_offset)

    def render_one(pair):
        params, flip = pair
        extinction = jnp.zeros_like(level)
        emission = [jnp.zeros_like(level) for channel in range(3)]
        for bump_index in range(TF_BUMPS):
            bump = jnp.exp(-jnp.square((level - params[0, bump_index]) / bump_width))
            extinction = extinction + params[1, bump_index] * bump
            for channel in range(3):
                emission[channel] = emission[channel] + params[2 + channel, bump_index] * bump
        optical = extinction / NX
        inclusive = jnp.cumsum(optical, axis=0)
        total = inclusive[-1]
        front = jnp.where(flip == 1, total[None] - inclusive, inclusive - optical)
        weight = jnp.exp(-front) * (1.0 - jnp.exp(-optical))
        colors = [lax.optimization_barrier(jnp.sum(weight * emission[channel], axis=0)) for channel in range(3)]
        return jnp.stack(colors + [1.0 - jnp.exp(-total)])
    images = lax.map(render_one, (transfer, direction))
    return (field, vorticity, images)
```

```python
import functools
import math

import jax
import jax.numpy as jnp
from jax import lax
from jax.experimental import pallas as pl
from jax.experimental.pallas import tpu as pltpu
from jax.sharding import PartitionSpec as P

STEPS = 4
MESH = pl.DeviceIdType.MESH

lattice_velocities = (
    (0, 0, 0),
    (1, 0, 0),
    (-1, 0, 0),
    (0, 1, 0),
    (0, -1, 0),
    (0, 0, 1),
    (0, 0, -1),
    (1, 1, 0),
    (-1, -1, 0),
    (1, -1, 0),
    (-1, 1, 0),
    (1, 0, 1),
    (-1, 0, -1),
    (1, 0, -1),
    (-1, 0, 1),
    (0, 1, 1),
    (0, -1, -1),
    (0, 1, -1),
    (0, -1, 1),
)
relaxation = 1.25
bump_width = 0.15
level_offset = 0.05
LOG2E = math.log2(math.e)
SCALE = math.sqrt(LOG2E) / bump_width

COUNT = len(lattice_velocities)
ORDER = (
    [n for n in range(COUNT) if lattice_velocities[n][0] == 1]
    + [n for n in range(COUNT) if lattice_velocities[n][0] == -1]
    + [n for n in range(COUNT) if lattice_velocities[n][0] == 0]
)
SLOT = {number: place for place, number in enumerate(ORDER)}
UP_Y = [n for n in range(COUNT) if lattice_velocities[n][1] == 1]
DOWN_Y = [n for n in range(COUNT) if lattice_velocities[n][1] == -1]
CROSS = len(UP_Y)
CORNERS = [n for n in range(COUNT) if lattice_velocities[n][0] and lattice_velocities[n][1]]
PAIRS = [(n, n + 1) for n in range(1, COUNT, 2)]
LOW = 8
ROWS = 8
CODED = 16
STEP = 16384.0


def add_all(values):
    while len(values) > 1:
        paired = [a + b for a, b in zip(values[0::2], values[1::2])]
        values = paired + ([values[-1]] if len(values) % 2 else [])
    return values[0]


def moments(field):
    diffs = {}
    sums = [field[0]]
    for plus, minus in PAIRS:
        sums.append(field[plus] + field[minus])
        diffs[plus] = field[plus] - field[minus]
    momentum = []
    for axis in range(3):
        total = diffs[1 + 2 * axis]
        for plus, _ in PAIRS[3:]:
            factor = lattice_velocities[plus][axis]
            if factor == 1:
                total = total + diffs[plus]
            elif factor == -1:
                total = total - diffs[plus]
        momentum.append(total)
    return add_all(sums), momentum


def collide(field):
    density, momentum = moments(field)
    inverse = 1.0 / density
    square = momentum[0] * momentum[0] + momentum[1] * momentum[1] + momentum[2] * momentum[2]
    even = density - 1.5 * (square * inverse)
    keep = 1.0 - relaxation
    result = [keep * field[0] + (relaxation / 3.0) * even] + [None] * (COUNT - 1)
    parts = {}
    for divisor in (18.0, 36.0):
        parts[divisor] = ((relaxation / divisor) * even, (relaxation * 4.5 / divisor) * inverse)
    for plus, minus in PAIRS:
        project = None
        for axis in range(3):
            factor = lattice_velocities[plus][axis]
            if factor:
                if project is None:
                    project = momentum[axis]
                elif factor == 1:
                    project = project + momentum[axis]
                else:
                    project = project - momentum[axis]
        divisor = 18.0 if plus < 7 else 36.0
        base, curve = parts[divisor]
        symmetric = base + curve * (project * project)
        odd = (3.0 * relaxation / divisor) * project
        result[plus] = keep * field[plus] + (symmetric + odd)
        result[minus] = keep * field[minus] + (symmetric - odd)
    return result


def weight_of(number):
    return 1.0 / (18.0 if number < 7 else 36.0)


def encode(value, unit):
    steps = jnp.round(value * (STEP / unit) - STEP)
    return jnp.clip(steps, -2.0 * STEP, 2.0 * STEP - 1.0).astype(jnp.int32).astype(jnp.int16)


def decode(code, unit):
    return code.astype(jnp.int32).astype(jnp.float32) * (unit / STEP) + unit


def kernel(
    sizes,
    f_hbm,
    par,
    direct,
    F,
    vort,
    img,
    A,
    B,
    E,
    SY,
    RY,
    SQ,
    RQ,
    SC,
    RC,
    U,
    VS,
    VR,
    L,
    G,
    PC,
    PA,
    PS,
    PR,
    in_sem,
    halo_s,
    halo_r,
    flow_s,
    flow_r,
    pa_s,
    pa_r,
    pr_s,
    pr_r,
):
    nd, ni, X, W, NZ, bumps = sizes
    d = lax.axis_index("depth")
    i = lax.axis_index("image")
    halves = W // ROWS
    ratio = ni // nd
    chunks = 4
    step_x = X // chunks

    loads = [
        pltpu.make_async_copy(
            f_hbm.at[:, pl.ds(c * step_x, step_x)],
            F.at[:, pl.ds(c * step_x, step_x)],
            in_sem.at[c],
        )
        for c in range(chunks)
    ]
    for copy in loads:
        copy.start()

    barrier = pltpu.get_barrier_semaphore()
    everyone = nd * ni
    me = d * ni + i

    def greet(offset, carry):
        other = lax.rem(me + offset, everyone)
        pl.semaphore_signal(
            barrier,
            inc=1,
            device_id={"depth": other // ni, "image": lax.rem(other, ni)},
            device_id_type=MESH,
        )
        return carry

    lax.fori_loop(1, everyone, greet, 0)

    ray = X * nd
    lane = lax.broadcasted_iota(jnp.int32, (8, NZ), 1)
    entries = jnp.full((8, NZ), direct[0].astype(jnp.float32), jnp.float32)
    for k in range(bumps):
        for kind in range(5):
            factor = SCALE if kind == 0 else (LOG2E / ray if kind == 1 else 1.0)
            entries = jnp.where(lane == kind * bumps + k, par[kind, 0, k] * factor, entries)
    gain = pltpu.roll(entries, bumps, 1)
    shift = gain * gain - jnp.log2(entries)
    ratios = entries / gain
    for kind in (3, 4):
        ratios = jnp.where(
            lane < kind * bumps, ratios, entries / pltpu.roll(entries, (kind - 1) * bumps, 1)
        )
    table = jnp.where(lane < 2 * bumps, shift, ratios)
    table = jnp.where(lane < bumps, 2.0 * entries, table)
    PC[i] = jnp.where(lane < 5 * bumps, table, entries)[0:1]

    def to(cx, cy):
        return {"depth": lax.rem(d + cx + nd, nd), "image": lax.rem(i + cy + ni, ni)}

    def remote(src, dst, send, recv, target):
        return pltpu.make_async_remote_copy(
            src_ref=src,
            dst_ref=dst,
            send_sem=send,
            recv_sem=recv,
            device_id=target,
            device_id_type=MESH,
        )

    starts = list(range(1, W - 1 - ROWS, ROWS)) + [W - 1 - ROWS]
    edge_rows = (0, W - 1)
    outward = (DOWN_Y, UP_Y)
    inward = (UP_Y, DOWN_Y)

    def pack(b, x, start, values):
        if start == 1:
            for number in DOWN_Y:
                E[b, 0, SLOT[number], pl.ds(ROWS + x, 1), :] = values[number][0:1]
        if start == W - 1 - ROWS:
            for number in UP_Y:
                E[b, 1, SLOT[number], pl.ds(ROWS + x, 1), :] = values[number][ROWS - 1 : ROWS]

    def streamed(S, x, start):
        field = []
        for number in range(COUNT):
            cx, cy, cz = lattice_velocities[number]
            value = S[SLOT[number], x + 1 - cx, pl.ds(LOW + start - cy, ROWS), :]
            if cz:
                value = pltpu.roll(value, cz % NZ, 1)
            field.append(value)
        return field

    def edge_streamed(b, side, x):
        field = []
        for number in range(COUNT):
            cx, _, cz = lattice_velocities[number]
            rows = slice(ROWS + x - cx, 2 * ROWS + x - cx)
            if number in inward[side]:
                value = RY[b, side, inward[side].index(number), rows, :]
            else:
                value = E[b, side, SLOT[number], rows, :]
            if cz:
                value = pltpu.roll(value, cz % NZ, 1)
            field.append(value)
        return field

    def update(S, D, b, x):
        for start in starts:
            values = collide(streamed(S, x, start))
            for number in range(COUNT):
                D[SLOT[number], x + 1, pl.ds(LOW + start, ROWS), :] = values[number]
            pack(b, x, start, values)

    def put_edges(D, b, side, x, values):
        row = LOW + edge_rows[side]
        for number in range(COUNT):
            cx, cy, _ = lattice_velocities[number]
            value = values[number]
            if number in inward[side]:
                for r in range(ROWS):
                    D[SLOT[number], x + r + 1, row : row + 1, :] = value[r : r + 1]
                continue
            if cy == 0:
                E[b, side, SLOT[number], ROWS + x : 2 * ROWS + x, :] = value
            else:
                SY[side, outward[side].index(number), x : x + ROWS, :] = value
            if cx == 1 and x == X - ROWS:
                D[SLOT[number], X, row : row + 1, :] = value[ROWS - 1 : ROWS]
            if cx == -1 and x == 0:
                D[SLOT[number], 1, row : row + 1, :] = value[0:1]

    inner = pl.ds(LOW, W)

    def exchange(D, turn, columns=None):
        slot = turn % 2
        for k, number in enumerate(CORNERS):
            cx, cy, _ = lattice_velocities[number]
            side = 1 if cy == 1 else 0
            edge = X - 1 if cx == 1 else 0
            SC[k] = SY[side, outward[side].index(number), edge : edge + 1, :]
        copies = []

        def add(src, dst, target, leave=None, land=None):
            k = len(copies) + 2
            leave, land = (k, k) if leave is None else (leave, land)
            copies.append(remote(src, dst, halo_s.at[turn, leave], halo_r.at[turn, land], target))
            copies[-1].start()

        for k, number in enumerate(CORNERS):
            cx, cy, _ = lattice_velocities[number]
            add(SC.at[k], RC.at[slot, k], to(cx, cy))
        for side in range(2):
            for j, number in enumerate(outward[side]):
                for x in range(0, X, CODED):
                    rows = slice(x, x + CODED)
                    SQ[side, j, rows, :] = encode(SY[side, j, rows, :], weight_of(number))
        far = lax.rem(i, 2)
        for side in (far, 1 - far):
            step = {"depth": d, "image": lax.rem(i + 2 * side - 1 + ni, ni)}
            add(SQ.at[side], RQ.at[slot, 1 - side], step, side, 1 - side)
        if columns is not None:
            for x in (0, X - 1):
                columns(x, 0)
        add(D.at[pl.ds(0, CROSS), X, inner], D.at[pl.ds(0, CROSS), 0, inner], to(1, 0))
        add(D.at[pl.ds(CROSS, CROSS), 1, inner], D.at[pl.ds(CROSS, CROSS), X + 1, inner], to(-1, 0))
        return copies

    def finish(copies, D, turn):
        slot = turn % 2
        for copy in copies:
            copy.wait()
        for side in range(2):
            for j, number in enumerate(inward[side]):
                for x in range(0, X, CODED):
                    value = decode(RQ[slot, side, j, x : x + CODED, :], weight_of(number))
                    RY[slot, side, j, ROWS + x : ROWS + x + CODED, :] = value
        for number in range(COUNT):
            cx, cy, _ = lattice_velocities[number]
            if cx == 0:
                continue
            plane, place = (0, ROWS - 1) if cx == 1 else (X + 1, ROWS + X)
            for side in range(2):
                if number in inward[side]:
                    k = CORNERS.index(number)
                    j = inward[side].index(number)
                    RY[slot, side, j, place : place + 1, :] = RC[slot, k]
                else:
                    row = LOW + edge_rows[side] - cy
                    E[slot, side, SLOT[number], place : place + 1, :] = D[
                        SLOT[number], plane, row : row + 1, :
                    ]

    def first(x, carry):
        for h in range(halves):
            field = [F[number, x, pl.ds(ROWS * h, ROWS), :] for number in range(COUNT)]
            values = collide(field)
            for number in range(COUNT):
                A[SLOT[number], x + 1, pl.ds(LOW + ROWS * h, ROWS), :] = values[number]
            for side, edge in ((0, 0), (1, ROWS - 1)):
                if h != (0 if side == 0 else halves - 1):
                    continue
                near = 1 if side == 0 else ROWS - 2
                for number in range(COUNT):
                    if lattice_velocities[number][1] == 0:
                        E[0, side, SLOT[number], pl.ds(ROWS + x, 1), :] = values[number][
                            edge : edge + 1
                        ]
                for j, number in enumerate(outward[side]):
                    SY[side, j, pl.ds(x, 1), :] = values[number][edge : edge + 1]
                    E[0, side, SLOT[number], pl.ds(ROWS + x, 1), :] = values[number][
                        near : near + 1
                    ]
        return carry

    for c in range(chunks):
        loads[c].wait()
        lax.fori_loop(c * step_x, (c + 1) * step_x, first, 0)

    pl.semaphore_wait(barrier, everyone - 1)
    shares = [
        remote(PC.at[i], PC.at[i], pa_s.at[o], pa_r.at[o], to(0, o)) for o in range(1, ni)
    ]
    copies = exchange(A, 0)
    for copy in shares:
        copy.start()

    source, target = A, B
    for turn in range(1, STEPS):

        def middle(x, carry, source=source, target=target, turn=turn):
            update(source, target, turn % 2, x)
            return carry

        lax.fori_loop(1, X - 1, middle, 0)
        finish(copies, source, turn - 1)
        for side in range(2):
            for x in range(0, X, ROWS):
                put_edges(target, turn % 2, side, x, collide(edge_streamed((turn - 1) % 2, side, x)))
        copies = exchange(target, turn, middle)
        source, target = target, source

    def flow_of(field):
        density, momentum = moments(field)
        inverse = 1.0 / density
        return [momentum[axis] * inverse for axis in (1, 2, 0)]

    def last(x, carry):
        for start in starts:
            field = streamed(source, x, start)
            for number in range(COUNT):
                F[number, x, pl.ds(start, ROWS), :] = field[number]
            for place, value in enumerate(flow_of(field)):
                U[place, x + 1, pl.ds(LOW + start, ROWS), :] = value
        return carry

    lax.fori_loop(1, X - 1, last, 0)
    finish(copies, source, STEPS - 1)
    for x in (0, X - 1):
        last(x, 0)
    for side in range(2):
        row = edge_rows[side]
        for x in range(0, X, ROWS):
            field = edge_streamed((STEPS - 1) % 2, side, x)
            flow = flow_of(field)
            for place, value in enumerate(flow):
                for r in range(ROWS):
                    U[place, x + r + 1, LOW + row : LOW + row + 1, :] = value[r : r + 1]
            VS[side, 0, x : x + ROWS, :] = flow[1]
            VS[side, 1, x : x + ROWS, :] = flow[2]
    flows = [
        remote(VS.at[1], VR.at[1], flow_s.at[0], flow_r.at[0], to(0, 1)),
        remote(VS.at[0], VR.at[0], flow_s.at[1], flow_r.at[1], to(0, -1)),
        remote(
            U.at[pl.ds(0, 2), X, inner],
            U.at[pl.ds(0, 2), 0, inner],
            flow_s.at[2],
            flow_r.at[2],
            to(1, 0),
        ),
        remote(
            U.at[pl.ds(0, 2), 1, inner],
            U.at[pl.ds(0, 2), X + 1, inner],
            flow_s.at[3],
            flow_r.at[3],
            to(-1, 0),
        ),
    ]
    for copy in flows:
        copy.start()
    for side in range(2):
        row = edge_rows[side]
        for x in range(0, X, ROWS):
            field = edge_streamed((STEPS - 1) % 2, side, x)
            for number in range(COUNT):
                for r in range(ROWS):
                    F[number, x + r, row : row + 1, :] = field[number][r : r + 1]
    for copy in shares:
        copy.wait()

    def expand(m, carry):
        for block in range(PA.shape[1] // 8):
            line = lax.broadcasted_iota(jnp.int32, (8, NZ), 0) + 8 * block
            chosen = jnp.where(lane == line, jnp.broadcast_to(PC[m], (8, NZ)), 0.0)
            value = jnp.sum(chosen, axis=1, keepdims=True)
            PA[m, pl.ds(8 * block, 8), :] = jnp.broadcast_to(value, (8, NZ))
        return carry

    lax.fori_loop(0, ni, expand, 0, unroll=2)
    for copy in flows:
        copy.wait()

    def flow_rows(x, carry):
        for place, j in ((1, 0), (2, 1)):
            U[place, x + 1, pl.ds(LOW - 1, 1), :] = VR[1, j, pl.ds(x, 1), :]
            U[place, x + 1, pl.ds(LOW + W, 1), :] = VR[0, j, pl.ds(x, 1), :]
        return carry

    lax.fori_loop(0, X, flow_rows, 0)

    def spin(x, carry):
        def across_x(place):
            return (U[place, x + 2, inner, :] - U[place, x, inner, :]) * 0.5

        def across_y(place):
            above = U[place, x + 1, pl.ds(LOW + 1, W), :]
            return (above - U[place, x + 1, pl.ds(LOW - 1, W), :]) * 0.5

        def across_z(place):
            value = U[place, x + 1, inner, :]
            return (pltpu.roll(value, NZ - 1, 1) - pltpu.roll(value, 1, 1)) * 0.5

        spin_x = across_y(1) - across_z(0)
        spin_y = across_z(2) - across_x(1)
        spin_z = across_x(0) - across_y(2)
        size = jnp.sqrt(spin_x * spin_x + spin_y * spin_y + spin_z * spin_z)
        rounded = size.astype(jnp.bfloat16)
        vort[x] = rounded
        value = rounded.astype(jnp.float32)
        level = (value / (value + level_offset)) * SCALE
        L[x] = level
        G[x] = jnp.exp2(-(level * level))
        return carry

    lax.fori_loop(0, X, spin, 0, unroll=2)

    owner = i // ratio
    mine = d * ratio + lax.rem(i, ratio)

    def row(m, r):
        return jnp.broadcast_to(PA[m, pl.ds(r, 1), :], (ROWS, NZ))

    def blend(backward, through, colors, local_through, local_colors):
        fade = jnp.where(backward, local_through, 1.0)
        lit = jnp.where(backward, 1.0, through)
        mixed = [color * fade + lit * local for color, local in zip(colors, local_colors)]
        return through * local_through, mixed

    def piece(o, m):
        return remote(
            PS.at[m],
            PR.at[mine],
            pr_s.at[o],
            pr_r.at[mine],
            {"depth": owner, "image": m},
        )

    def render(o, carry):
        m = lax.rem(i + 1 + o, ni)
        backward = row(m, 5 * bumps) > 0.5
        sign = jnp.where(backward, 1.0, -1.0)

        def along(x, state):
            new = []
            levels = [L[x, pl.ds(ROWS * h, ROWS), :] for h in range(halves)]
            totals = [[None] * 4 for h in range(halves)]
            for k in range(bumps):
                centre = row(m, k)
                shift = row(m, bumps + k)
                gains = [row(m, (1 + j) * bumps + k) for j in range(1, 4)]
                for h in range(halves):
                    bump = jnp.exp2(levels[h] * centre - shift)
                    for j in range(4):
                        term = gains[j - 1] * bump if j else bump
                        totals[h][j] = term if k == 0 else totals[h][j] + term
            for h in range(halves):
                signed, seen, *colors = state[5 * h : 5 * h + 5]
                common = G[x, pl.ds(ROWS * h, ROWS), :]
                signed = signed + totals[h][0] * (common * sign)
                now = jnp.exp2(signed)
                weight = (seen - now) * common
                colors = [color + weight * total for color, total in zip(colors, totals[h][1:])]
                new += [signed, now, *colors]
            return tuple(new)

        zero = jnp.zeros((ROWS, NZ), jnp.float32)
        start = (zero, jnp.ones((ROWS, NZ), jnp.float32), zero, zero, zero) * halves
        state = lax.fori_loop(0, X, along, start, unroll=2)
        for h in range(halves):
            signed, seen, *colors = state[5 * h : 5 * h + 5]
            through = jnp.where(backward, jnp.exp2(-signed), seen)
            factor = jnp.where(backward, -through, 1.0)
            for j, value in enumerate([color * factor for color in colors] + [through]):
                PS[m, j, pl.ds(ROWS * h, ROWS), :] = value
        local_target = jnp.logical_and(owner == d, m == i)

        @pl.when(local_target)
        def _():
            PR[mine] = PS[m]

        @pl.when(jnp.logical_not(local_target))
        def _():
            piece(o, m).start()

        return carry

    lax.fori_loop(0, ni, render, 0)

    def sent(o, carry):
        m = lax.rem(i + 1 + o, ni)

        @pl.when(jnp.logical_not(jnp.logical_and(owner == d, m == i)))
        def _():
            piece(o, m).wait_send()

        return carry

    def arrived(slot, carry):
        @pl.when(jnp.logical_not(jnp.logical_and(owner == d, slot == mine)))
        def _():
            remote(
                PS.at[0], PR.at[slot], pr_s.at[0], pr_r.at[slot], {"depth": d, "image": i}
            ).wait_recv()

        return carry

    lax.fori_loop(0, nd * ratio, arrived, 0)
    backward = row(i, 5 * bumps) > 0.5
    for part in range(ratio):
        for h in range(halves):
            rows = pl.ds(ROWS * h, ROWS)
            through = jnp.ones((ROWS, NZ), jnp.float32)
            colors = [jnp.zeros((ROWS, NZ), jnp.float32)] * 3
            for slab in range(nd):
                slot = slab * ratio + part
                local = [PR[slot, j, rows, :] for j in range(4)]
                through, colors = blend(backward, through, colors, local[3], local[:3])
            for j, value in enumerate(colors + [1.0 - through]):
                img[0, j, pl.ds(part * W + ROWS * h, ROWS), :] = value
    lax.fori_loop(0, ni, sent, 0)


def put_out(pieces, F, vort, img, F_out, vort_out, img_out, sems):
    step = F.shape[1] // pieces
    copies = [
        pltpu.make_async_copy(
            F.at[:, pl.ds(c * step, step)], F_out.at[:, pl.ds(c * step, step)], sems.at[c]
        )
        for c in range(pieces)
    ]
    copies.append(pltpu.make_async_copy(vort, vort_out, sems.at[pieces]))
    copies.append(pltpu.make_async_copy(img, img_out, sems.at[pieces + 1]))
    for copy in copies:
        copy.start()
    for copy in copies:
        copy.wait()


def on_device(populations, transfer, direction):
    nd, ni = lax.axis_size("depth"), lax.axis_size("image")
    count, X, W, NZ = populations.shape
    bumps = transfer.shape[2]
    assert transfer.shape[0] == 1 and ni % nd == 0 and W % ROWS == 0 and W >= 2 * ROWS and X % CODED == 0
    sizes = (nd, ni, X, W, NZ, bumps)
    ratio = ni // nd
    padded = W + 2 * ROWS
    f32 = jnp.float32
    table = -(-(5 * bumps + 1) // 8) * 8
    dma = pltpu.SemaphoreType.DMA
    results = pl.pallas_call(
        functools.partial(kernel, sizes),
        out_shape=(
            pltpu.VMEM(populations.shape, f32),
            pltpu.VMEM((X, W, NZ), jnp.bfloat16),
            pltpu.VMEM((1, 4, ratio * W, NZ), f32),
        ),
        in_specs=[
            pl.BlockSpec(memory_space=pl.ANY),
            pl.BlockSpec(memory_space=pltpu.SMEM),
            pl.BlockSpec(memory_space=pltpu.SMEM),
        ],
        out_specs=(
            pl.BlockSpec(memory_space=pltpu.VMEM),
            pl.BlockSpec(memory_space=pltpu.VMEM),
            pl.BlockSpec(memory_space=pltpu.VMEM),
        ),
        scratch_shapes=[
            pltpu.VMEM((COUNT, X + 2, padded, NZ), f32),
            pltpu.VMEM((COUNT, X + 2, padded, NZ), f32),
            pltpu.VMEM((2, 2, COUNT, X + 2 * ROWS, NZ), f32),
            pltpu.VMEM((2, CROSS, X, NZ), f32),
            pltpu.VMEM((2, 2, CROSS, X + 2 * ROWS, NZ), f32),
            pltpu.VMEM((2, CROSS, X, NZ), jnp.int16),
            pltpu.VMEM((2, 2, CROSS, X, NZ), jnp.int16),
            pltpu.VMEM((4, 1, NZ), f32),
            pltpu.VMEM((2, 4, 1, NZ), f32),
            pltpu.VMEM((3, X + 2, padded, NZ), f32),
            pltpu.VMEM((2, 2, X, NZ), f32),
            pltpu.VMEM((2, 2, X, NZ), f32),
            pltpu.VMEM((X, W, NZ), f32),
            pltpu.VMEM((X, W, NZ), f32),
            pltpu.VMEM((ni, 1, NZ), f32),
            pltpu.VMEM((ni, table, NZ), f32),
            pltpu.VMEM((ni, 4, W, NZ), f32),
            pltpu.VMEM((nd * ratio, 4, W, NZ), f32),
            dma((4,)),
            dma((STEPS, 10)),
            dma((STEPS, 10)),
            dma((4,)),
            dma((4,)),
            dma((ni,)),
            dma((ni,)),
            dma((ni,)),
            dma((nd * ratio,)),
        ],
        compiler_params=pltpu.CompilerParams(
            collective_id=0, has_side_effects=True, vmem_limit_bytes=56 << 20
        ),
    )(populations, transfer.transpose(1, 0, 2), direction)
    pieces = 4
    return pl.pallas_call(
        functools.partial(put_out, pieces),
        out_shape=tuple(jax.ShapeDtypeStruct(r.shape, r.dtype) for r in results),
        in_specs=[pl.BlockSpec(memory_space=pltpu.VMEM)] * 3,
        out_specs=(pl.BlockSpec(memory_space=pl.ANY),) * 3,
        scratch_shapes=[dma((pieces + 2,))],
        compiler_params=pltpu.CompilerParams(vmem_limit_bytes=1 << 20),
    )(*results)


def solution(mesh):
    in_specs = (P(None, "depth", "image", None), P("image", None, None), P("image"))
    out_specs = (
        P(None, "depth", "image", None),
        P("depth", "image", None),
        P("image", None, "depth", None),
    )
    return jax.shard_map(
        on_device, mesh=mesh, in_specs=in_specs, out_specs=out_specs, check_vma=False
    )
```

```python
import functools
import math

import jax
import jax.numpy as jnp
from jax import lax
from jax.experimental import pallas as pl
from jax.experimental.pallas import tpu as pltpu
from jax.sharding import PartitionSpec as P

STEPS = 4
MESH = pl.DeviceIdType.MESH

lattice_velocities = (
    (0, 0, 0),
    (1, 0, 0),
    (-1, 0, 0),
    (0, 1, 0),
    (0, -1, 0),
    (0, 0, 1),
    (0, 0, -1),
    (1, 1, 0),
    (-1, -1, 0),
    (1, -1, 0),
    (-1, 1, 0),
    (1, 0, 1),
    (-1, 0, -1),
    (1, 0, -1),
    (-1, 0, 1),
    (0, 1, 1),
    (0, -1, -1),
    (0, 1, -1),
    (0, -1, 1),
)
relaxation = 1.25
bump_width = 0.15
level_offset = 0.05
LOG2E = math.log2(math.e)
SCALE = math.sqrt(LOG2E) / bump_width

COUNT = len(lattice_velocities)
ORDER = (
    [n for n in range(COUNT) if lattice_velocities[n][0] == 1]
    + [n for n in range(COUNT) if lattice_velocities[n][0] == -1]
    + [n for n in range(COUNT) if lattice_velocities[n][0] == 0]
)
SLOT = {number: place for place, number in enumerate(ORDER)}
UP_Y = [n for n in range(COUNT) if lattice_velocities[n][1] == 1]
DOWN_Y = [n for n in range(COUNT) if lattice_velocities[n][1] == -1]
CROSS = len(UP_Y)
CORNERS = [n for n in range(COUNT) if lattice_velocities[n][0] and lattice_velocities[n][1]]
PAIRS = [(n, n + 1) for n in range(1, COUNT, 2)]
LOW = 8
ROWS = 8
CODED = 16
STEP = 16384.0
PART_UNITS = ((32768.0, 5.0 / 6.0), (65536.0, 0.0), (65536.0, 0.0))


def add_all(values):
    while len(values) > 1:
        paired = [a + b for a, b in zip(values[0::2], values[1::2])]
        values = paired + ([values[-1]] if len(values) % 2 else [])
    return values[0]


def moments(field):
    diffs = {}
    sums = [field[0]]
    for plus, minus in PAIRS:
        sums.append(field[plus] + field[minus])
        diffs[plus] = field[plus] - field[minus]
    momentum = []
    for axis in range(3):
        total = diffs[1 + 2 * axis]
        for plus, _ in PAIRS[3:]:
            factor = lattice_velocities[plus][axis]
            if factor == 1:
                total = total + diffs[plus]
            elif factor == -1:
                total = total - diffs[plus]
        momentum.append(total)
    return add_all(sums), momentum


def collide(field):
    density, momentum = moments(field)
    inverse = 1.0 / density
    square = momentum[0] * momentum[0] + momentum[1] * momentum[1] + momentum[2] * momentum[2]
    even = density - 1.5 * (square * inverse)
    keep = 1.0 - relaxation
    result = [keep * field[0] + (relaxation / 3.0) * even] + [None] * (COUNT - 1)
    parts = {}
    for divisor in (18.0, 36.0):
        parts[divisor] = ((relaxation / divisor) * even, (relaxation * 4.5 / divisor) * inverse)
    for plus, minus in PAIRS:
        project = None
        for axis in range(3):
            factor = lattice_velocities[plus][axis]
            if factor:
                if project is None:
                    project = momentum[axis]
                elif factor == 1:
                    project = project + momentum[axis]
                else:
                    project = project - momentum[axis]
        divisor = 18.0 if plus < 7 else 36.0
        base, curve = parts[divisor]
        symmetric = base + curve * (project * project)
        odd = (3.0 * relaxation / divisor) * project
        result[plus] = keep * field[plus] + (symmetric + odd)
        result[minus] = keep * field[minus] + (symmetric - odd)
    return result


def weight_of(number):
    return 1.0 / (18.0 if number < 7 else 36.0)


def encode(value, unit):
    steps = jnp.round(value * (STEP / unit) - STEP)
    return jnp.clip(steps, -2.0 * STEP, 2.0 * STEP - 1.0).astype(jnp.int32).astype(jnp.int16)


def decode(code, unit):
    return code.astype(jnp.int32).astype(jnp.float32) * (unit / STEP) + unit


def kernel(
    sizes,
    f_hbm,
    par,
    direct,
    F,
    vort,
    img,
    A,
    B,
    E,
    SY,
    RY,
    SQ,
    RQ,
    SC,
    RC,
    U,
    PYS,
    PYR,
    PXS,
    PXR,
    CS,
    CR,
    L,
    G,
    PC,
    PA,
    PS,
    PR,
    in_sem,
    halo_s,
    halo_r,
    part_s,
    part_r,
    pa_s,
    pa_r,
    pr_s,
    pr_r,
):
    nd, ni, X, W, NZ, bumps = sizes
    d = lax.axis_index("depth")
    i = lax.axis_index("image")
    halves = W // ROWS
    ratio = ni // nd
    chunks = 4
    step_x = X // chunks

    loads = [
        pltpu.make_async_copy(
            f_hbm.at[:, pl.ds(c * step_x, step_x)],
            F.at[:, pl.ds(c * step_x, step_x)],
            in_sem.at[c],
        )
        for c in range(chunks)
    ]
    for copy in loads:
        copy.start()

    barrier = pltpu.get_barrier_semaphore()
    everyone = nd * ni
    me = d * ni + i

    def greet(offset, carry):
        other = lax.rem(me + offset, everyone)
        pl.semaphore_signal(
            barrier,
            inc=1,
            device_id={"depth": other // ni, "image": lax.rem(other, ni)},
            device_id_type=MESH,
        )
        return carry

    lax.fori_loop(1, everyone, greet, 0)

    ray = X * nd
    lane = lax.broadcasted_iota(jnp.int32, (8, NZ), 1)
    entries = jnp.full((8, NZ), direct[0].astype(jnp.float32), jnp.float32)
    for k in range(bumps):
        for kind in range(5):
            factor = SCALE if kind == 0 else (LOG2E / ray if kind == 1 else 1.0)
            entries = jnp.where(lane == kind * bumps + k, par[kind, 0, k] * factor, entries)
    gain = pltpu.roll(entries, bumps, 1)
    shift = gain * gain - jnp.log2(entries)
    ratios = entries / gain
    for kind in (3, 4):
        ratios = jnp.where(
            lane < kind * bumps, ratios, entries / pltpu.roll(entries, (kind - 1) * bumps, 1)
        )
    table = jnp.where(lane < 2 * bumps, shift, ratios)
    table = jnp.where(lane < bumps, 2.0 * entries, table)
    PC[i] = jnp.where(lane < 5 * bumps, table, entries)[0:1]

    def to(cx, cy):
        return {"depth": lax.rem(d + cx + nd, nd), "image": lax.rem(i + cy + ni, ni)}

    def remote(src, dst, send, recv, target):
        return pltpu.make_async_remote_copy(
            src_ref=src,
            dst_ref=dst,
            send_sem=send,
            recv_sem=recv,
            device_id=target,
            device_id_type=MESH,
        )

    starts = list(range(1, W - 1 - ROWS, ROWS)) + [W - 1 - ROWS]
    edge_rows = (0, W - 1)
    outward = (DOWN_Y, UP_Y)
    inward = (UP_Y, DOWN_Y)

    def pack(b, x, start, values):
        if start == 1:
            for number in DOWN_Y:
                E[b, 0, SLOT[number], pl.ds(ROWS + x, 1), :] = values[number][0:1]
        if start == W - 1 - ROWS:
            for number in UP_Y:
                E[b, 1, SLOT[number], pl.ds(ROWS + x, 1), :] = values[number][ROWS - 1 : ROWS]

    def streamed(S, x, start):
        field = []
        for number in range(COUNT):
            cx, cy, cz = lattice_velocities[number]
            value = S[SLOT[number], x + 1 - cx, pl.ds(LOW + start - cy, ROWS), :]
            if cz:
                value = pltpu.roll(value, cz % NZ, 1)
            field.append(value)
        return field

    def edge_streamed(b, side, x):
        field = []
        for number in range(COUNT):
            cx, _, cz = lattice_velocities[number]
            rows = slice(ROWS + x - cx, 2 * ROWS + x - cx)
            if number in inward[side]:
                value = RY[b, side, inward[side].index(number), rows, :]
            else:
                value = E[b, side, SLOT[number], rows, :]
            if cz:
                value = pltpu.roll(value, cz % NZ, 1)
            field.append(value)
        return field

    def update(S, D, b, x):
        for start in starts:
            values = collide(streamed(S, x, start))
            for number in range(COUNT):
                D[SLOT[number], x + 1, pl.ds(LOW + start, ROWS), :] = values[number]
            pack(b, x, start, values)

    def put_edges(D, b, side, x, values):
        row = LOW + edge_rows[side]
        for number in range(COUNT):
            cx, cy, _ = lattice_velocities[number]
            value = values[number]
            if number in inward[side]:
                for r in range(ROWS):
                    D[SLOT[number], x + r + 1, row : row + 1, :] = value[r : r + 1]
                continue
            if cy == 0:
                E[b, side, SLOT[number], ROWS + x : 2 * ROWS + x, :] = value
            else:
                SY[side, outward[side].index(number), ROWS + x : 2 * ROWS + x, :] = value
            if cx == 1 and x == X - ROWS:
                D[SLOT[number], X, row : row + 1, :] = value[ROWS - 1 : ROWS]
            if cx == -1 and x == 0:
                D[SLOT[number], 1, row : row + 1, :] = value[0:1]

    inner = pl.ds(LOW, W)

    def collect(terms, axes):
        groups = {}
        for number, value in terms:
            velocity = lattice_velocities[number]
            sums = groups.setdefault(velocity[2], [None] * 3)
            for place, factor in enumerate([1] + [velocity[axis] for axis in axes]):
                if factor:
                    value_now = value if factor == 1 else -value
                    sums[place] = value_now if sums[place] is None else sums[place] + value_now
        totals = [None] * 3
        for cz, sums in groups.items():
            turned = [v if v is None or cz == 0 else pltpu.roll(v, cz % NZ, 1) for v in sums]
            if 2 in axes:
                turned[1 + axes.index(2)] = None if cz == 0 else cz * turned[0]
            for place in range(3):
                if turned[place] is not None:
                    old = totals[place]
                    totals[place] = turned[place] if old is None else old + turned[place]
        return totals

    def planes_of(side, number):
        edge, inside = ((0, 1), (X - 1, X - 2))[side]
        cx = lattice_velocities[number][0]
        if cx == 0:
            return edge
        return inside if cx == 2 * side - 1 else None

    def fill_rows(D, b):
        zero = jnp.zeros((1, NZ), jnp.float32)
        for side in range(2):
            for number in range(COUNT):
                plane = planes_of(side, number)
                if plane is None:
                    continue
                cy = lattice_velocities[number][1]
                if cy:
                    row = LOW - 1 if cy == 1 else LOW + W
                    D[SLOT[number], plane + 1, row : row + 1, :] = zero
                    continue
                for y, row in enumerate(edge_rows):
                    value = E[b, y, SLOT[number], ROWS + plane : ROWS + plane + 1, :]
                    D[SLOT[number], plane + 1, LOW + row : LOW + row + 1, :] = value

    def send_parts(D, b):
        line = lax.broadcasted_iota(jnp.int32, (CODED, NZ), 0)
        for k, corner in enumerate(CORNERS):
            cx, cy, _ = lattice_velocities[corner]
            side = 1 if cy == 1 else 0
            edge = ROWS + (X - 1 if cx == 1 else 0)
            for place, cz in enumerate((0, 1, -1)):
                number = lattice_velocities.index((cx, 0, cz))
                upper = E[b, side, SLOT[number], edge : edge + 1, :]
                number = outward[side].index(lattice_velocities.index((0, cy, cz)))
                lower = SY[side, number, edge : edge + 1, :]
                if cz == 0:
                    upper = upper + E[b, side, SLOT[corner], edge : edge + 1, :]
                    near = edge - cx
                    lower = lower + SY[side, outward[side].index(corner), near : near + 1, :]
                CS[k, 2 * place : 2 * place + 1, :] = upper
                CS[k, 2 * place + 1 : 2 * place + 2, :] = lower
        for side in range(2):
            for x in range(0, X, CODED):
                terms = []
                for number in range(COUNT):
                    if number in inward[side]:
                        continue
                    cx = lattice_velocities[number][0]
                    start = ROWS + x - cx
                    value = E[b, side, SLOT[number], start : start + CODED, :]
                    if cx == 1 and x == 0:
                        value = jnp.where(line == 0, 0.0, value)
                    if cx == -1 and x == X - CODED:
                        value = jnp.where(line == CODED - 1, 0.0, value)
                    terms.append((number, value))
                for place, value in enumerate(collect(terms, (2, 0))):
                    unit, centre = PART_UNITS[place]
                    steps = jnp.clip(jnp.round((value - centre) * unit), -32768.0, 32767.0)
                    code = steps.astype(jnp.int32).astype(jnp.int16)
                    PYS[side, place, x : x + CODED, :] = code
        for side in range(2):
            for h in range(halves):
                terms = []
                for number in range(COUNT):
                    plane = planes_of(side, number)
                    if plane is None:
                        continue
                    rows = pl.ds(LOW + ROWS * h - lattice_velocities[number][1], ROWS)
                    terms.append((number, D[SLOT[number], plane + 1, rows, :]))
                for place, value in enumerate(collect(terms, (1, 2))):
                    PXS[side, place, ROWS * h : ROWS * h + ROWS, :] = value
        parts = []
        for k, corner in enumerate(CORNERS):
            cx, cy, _ = lattice_velocities[corner]
            parts.append(remote(CS.at[k], CR.at[k], part_s.at[k], part_r.at[k], to(cx, cy)))
        far = lax.rem(i, 2)
        for side in (far, 1 - far):
            step = {"depth": d, "image": lax.rem(i + 2 * side - 1 + ni, ni)}
            parts.append(
                remote(
                    PYS.at[side], PYR.at[1 - side], part_s.at[4 + side], part_r.at[5 - side], step
                )
            )
        for side in range(2):
            parts.append(
                remote(
                    PXS.at[side],
                    PXR.at[1 - side],
                    part_s.at[6 + side],
                    part_r.at[7 - side],
                    to(2 * side - 1, 0),
                )
            )
        for part in parts:
            part.start()
        return parts

    def ghosts(D, slot):
        line = lax.broadcasted_iota(jnp.int32, (ROWS, NZ), 0)
        meet = {}
        for k, corner in enumerate(CORNERS):
            after = pltpu.roll(CR[k], 1, 1)
            before = pltpu.roll(CR[k], NZ - 1, 1)
            plain = CR[k]
            for y in range(2):
                up, down = after[2 + y : 3 + y], before[4 + y : 5 + y]
                meet[lattice_velocities[corner][:2], y] = (plain[y : y + 1] + up + down, up - down)
        for y in range(2):
            for number in outward[y]:
                cx = lattice_velocities[number][0]
                if cx:
                    place, plane = (ROWS - 1, 0) if cx == 1 else (ROWS + X, X + 1)
                    row = LOW + edge_rows[y]
                    SY[y, outward[y].index(number), place : place + 1, :] = D[
                        SLOT[number], plane, row : row + 1, :
                    ]
        for k, corner in enumerate(CORNERS):
            cx, cy, _ = lattice_velocities[corner]
            y = 0 if cy == 1 else 1
            plane, place = (X, ROWS + X - 1) if cx == 1 else (1, ROWS)
            row = LOW - 1 if cy == 1 else LOW + W
            D[SLOT[corner], plane, row : row + 1, :] = RY[
                slot, y, inward[y].index(corner), place : place + 1, :
            ]
        for side in range(2):
            from_x = 1 - 2 * side
            plane = X if side else 1
            for h in range(halves):
                terms = []
                for number in range(COUNT):
                    if lattice_velocities[number][0] == -from_x:
                        rows = pl.ds(LOW + ROWS * h - lattice_velocities[number][1], ROWS)
                        terms.append((number, D[SLOT[number], plane, rows, :]))
                sums = collect(terms, (1, 2))
                for place in range(3):
                    sums[place] = sums[place] + PXR[side, place, ROWS * h : ROWS * h + ROWS, :]
                for at, from_y, wanted in ((0, 1, 0), (ROWS - 1, -1, halves - 1)):
                    if h == wanted:
                        mass, along_z = meet[(from_x, from_y), 1]
                        for place, more in enumerate((mass, from_y * mass, along_z)):
                            sums[place] = jnp.where(line == at, sums[place] + more, sums[place])
                inverse = 1.0 / sums[0]
                for place in range(2):
                    U[place, (X + 1) * side, pl.ds(LOW + ROWS * h, ROWS), :] = (
                        sums[1 + place] * inverse
                    )
        for side in range(2):
            from_y = 1 - 2 * side
            row = LOW + W if side else LOW - 1
            for x in range(0, X, ROWS):
                terms = []
                for j, number in enumerate(outward[side]):
                    start = ROWS + x - lattice_velocities[number][0]
                    terms.append((number, SY[side, j, start : start + ROWS, :]))
                sums = collect(terms, (2, 0))
                for place in range(3):
                    unit, centre = PART_UNITS[place]
                    code = PYR[side, place, x // CODED * CODED : x // CODED * CODED + CODED, :]
                    value = code.astype(jnp.int32).astype(jnp.float32) * (1.0 / unit) + centre
                    sums[place] = sums[place] + value[x % CODED : x % CODED + ROWS]
                for at, from_x, wanted in ((0, 1, 0), (ROWS - 1, -1, X - ROWS)):
                    if x == wanted:
                        mass, along_z = meet[(from_x, from_y), 0]
                        for place, more in enumerate((mass, along_z, from_x * mass)):
                            sums[place] = jnp.where(line == at, sums[place] + more, sums[place])
                inverse = 1.0 / sums[0]
                for place in range(2):
                    value = sums[1 + place] * inverse
                    for r in range(ROWS):
                        U[1 + place, x + r + 1, row : row + 1, :] = value[r : r + 1]

    def exchange(D, turn, columns=None):
        slot = turn % 2
        for k, number in enumerate(CORNERS):
            cx, cy, _ = lattice_velocities[number]
            side = 1 if cy == 1 else 0
            edge = X - 1 if cx == 1 else 0
            SC[k] = SY[side, outward[side].index(number), ROWS + edge : ROWS + edge + 1, :]
        copies = []

        def add(src, dst, target, leave=None, land=None):
            k = len(copies) + 2
            leave, land = (k, k) if leave is None else (leave, land)
            copies.append(remote(src, dst, halo_s.at[turn, leave], halo_r.at[turn, land], target))
            copies[-1].start()

        for k, number in enumerate(CORNERS):
            cx, cy, _ = lattice_velocities[number]
            add(SC.at[k], RC.at[slot, k], to(cx, cy))
        for side in range(2):
            for j, number in enumerate(outward[side]):
                for x in range(0, X, CODED):
                    value = SY[side, j, ROWS + x : ROWS + x + CODED, :]
                    SQ[side, j, x : x + CODED, :] = encode(value, weight_of(number))
        far = lax.rem(i, 2)
        for side in (far, 1 - far):
            step = {"depth": d, "image": lax.rem(i + 2 * side - 1 + ni, ni)}
            add(SQ.at[side], RQ.at[slot, 1 - side], step, side, 1 - side)
        if columns is not None:
            for x in (0, X - 1):
                columns(x, 0)
        if turn == STEPS - 1:
            fill_rows(D, turn % 2)
        add(D.at[pl.ds(0, CROSS), X, inner], D.at[pl.ds(0, CROSS), 0, inner], to(1, 0))
        add(D.at[pl.ds(CROSS, CROSS), 1, inner], D.at[pl.ds(CROSS, CROSS), X + 1, inner], to(-1, 0))
        if turn == STEPS - 1:
            copies += send_parts(D, turn % 2)
        return copies

    def finish(copies, D, turn):
        slot = turn % 2
        for copy in copies:
            copy.wait()
        for side in range(2):
            for j, number in enumerate(inward[side]):
                for x in range(0, X, CODED):
                    value = decode(RQ[slot, side, j, x : x + CODED, :], weight_of(number))
                    RY[slot, side, j, ROWS + x : ROWS + x + CODED, :] = value
        for number in range(COUNT):
            cx, cy, _ = lattice_velocities[number]
            if cx == 0:
                continue
            plane, place = (0, ROWS - 1) if cx == 1 else (X + 1, ROWS + X)
            for side in range(2):
                if number in inward[side]:
                    k = CORNERS.index(number)
                    j = inward[side].index(number)
                    RY[slot, side, j, place : place + 1, :] = RC[slot, k]
                else:
                    row = LOW + edge_rows[side] - cy
                    E[slot, side, SLOT[number], place : place + 1, :] = D[
                        SLOT[number], plane, row : row + 1, :
                    ]

    def first(x, carry):
        for h in range(halves):
            field = [F[number, x, pl.ds(ROWS * h, ROWS), :] for number in range(COUNT)]
            values = collide(field)
            for number in range(COUNT):
                A[SLOT[number], x + 1, pl.ds(LOW + ROWS * h, ROWS), :] = values[number]
            for side, edge in ((0, 0), (1, ROWS - 1)):
                if h != (0 if side == 0 else halves - 1):
                    continue
                near = 1 if side == 0 else ROWS - 2
                for number in range(COUNT):
                    if lattice_velocities[number][1] == 0:
                        E[0, side, SLOT[number], pl.ds(ROWS + x, 1), :] = values[number][
                            edge : edge + 1
                        ]
                for j, number in enumerate(outward[side]):
                    SY[side, j, pl.ds(ROWS + x, 1), :] = values[number][edge : edge + 1]
                    E[0, side, SLOT[number], pl.ds(ROWS + x, 1), :] = values[number][
                        near : near + 1
                    ]
        return carry

    for c in range(chunks):
        loads[c].wait()
        lax.fori_loop(c * step_x, (c + 1) * step_x, first, 0)

    pl.semaphore_wait(barrier, everyone - 1)
    shares = [
        remote(PC.at[i], PC.at[i], pa_s.at[o], pa_r.at[o], to(0, o)) for o in range(1, ni)
    ]
    copies = exchange(A, 0)
    for copy in shares:
        copy.start()

    source, target = A, B
    for turn in range(1, STEPS):

        def middle(x, carry, source=source, target=target, turn=turn):
            update(source, target, turn % 2, x)
            return carry

        lax.fori_loop(1, X - 1, middle, 0)
        finish(copies, source, turn - 1)
        for side in range(2):
            for x in range(0, X, ROWS):
                put_edges(target, turn % 2, side, x, collide(edge_streamed((turn - 1) % 2, side, x)))
        copies = exchange(target, turn, middle)
        source, target = target, source

    def flow_of(field):
        density, momentum = moments(field)
        inverse = 1.0 / density
        return [momentum[axis] * inverse for axis in (1, 2, 0)]

    def last(x, carry):
        for start in starts:
            field = streamed(source, x, start)
            for number in range(COUNT):
                F[number, x, pl.ds(start, ROWS), :] = field[number]
            for place, value in enumerate(flow_of(field)):
                U[place, x + 1, pl.ds(LOW + start, ROWS), :] = value
        return carry

    def expand(m, carry):
        for block in range(PA.shape[1] // 8):
            line = lax.broadcasted_iota(jnp.int32, (8, NZ), 0) + 8 * block
            chosen = jnp.where(lane == line, jnp.broadcast_to(PC[m], (8, NZ)), 0.0)
            value = jnp.sum(chosen, axis=1, keepdims=True)
            PA[m, pl.ds(8 * block, 8), :] = jnp.broadcast_to(value, (8, NZ))
        return carry

    for copy in shares:
        copy.wait()
    lax.fori_loop(0, ni, expand, 0, unroll=2)
    lax.fori_loop(1, X - 1, last, 0)
    finish(copies, source, STEPS - 1)
    for x in (0, X - 1):
        last(x, 0)
    for side in range(2):
        row = edge_rows[side]
        for x in range(0, X, ROWS):
            field = edge_streamed((STEPS - 1) % 2, side, x)
            for place, value in enumerate(flow_of(field)):
                for r in range(ROWS):
                    U[place, x + r + 1, LOW + row : LOW + row + 1, :] = value[r : r + 1]
    ghosts(source, (STEPS - 1) % 2)

    def spin(x, carry):
        def across_x(place):
            return (U[place, x + 2, inner, :] - U[place, x, inner, :]) * 0.5

        def across_y(place):
            above = U[place, x + 1, pl.ds(LOW + 1, W), :]
            return (above - U[place, x + 1, pl.ds(LOW - 1, W), :]) * 0.5

        def across_z(place):
            value = U[place, x + 1, inner, :]
            return (pltpu.roll(value, NZ - 1, 1) - pltpu.roll(value, 1, 1)) * 0.5

        spin_x = across_y(1) - across_z(0)
        spin_y = across_z(2) - across_x(1)
        spin_z = across_x(0) - across_y(2)
        size = jnp.sqrt(spin_x * spin_x + spin_y * spin_y + spin_z * spin_z)
        rounded = size.astype(jnp.bfloat16)
        vort[x] = rounded
        value = rounded.astype(jnp.float32)
        level = (value / (value + level_offset)) * SCALE
        L[x] = level
        G[x] = jnp.exp2(-(level * level))
        return carry

    lax.fori_loop(0, X, spin, 0, unroll=2)

    owner = i // ratio
    mine = d * ratio + lax.rem(i, ratio)

    def row(m, r):
        return jnp.broadcast_to(PA[m, pl.ds(r, 1), :], (ROWS, NZ))

    def blend(backward, through, colors, local_through, local_colors):
        fade = jnp.where(backward, local_through, 1.0)
        lit = jnp.where(backward, 1.0, through)
        mixed = [color * fade + lit * local for color, local in zip(colors, local_colors)]
        return through * local_through, mixed

    def piece(o, m):
        return remote(
            PS.at[m],
            PR.at[mine],
            pr_s.at[o],
            pr_r.at[mine],
            {"depth": owner, "image": m},
        )

    def render(o, carry):
        m = lax.rem(i + 1 + o, ni)
        backward = row(m, 5 * bumps) > 0.5
        sign = jnp.where(backward, 1.0, -1.0)

        def along(x, state):
            new = []
            levels = [L[x, pl.ds(ROWS * h, ROWS), :] for h in range(halves)]
            totals = [[None] * 4 for h in range(halves)]
            for k in range(bumps):
                centre = row(m, k)
                shift = row(m, bumps + k)
                gains = [row(m, (1 + j) * bumps + k) for j in range(1, 4)]
                for h in range(halves):
                    bump = jnp.exp2(levels[h] * centre - shift)
                    for j in range(4):
                        term = gains[j - 1] * bump if j else bump
                        totals[h][j] = term if k == 0 else totals[h][j] + term
            for h in range(halves):
                signed, seen, *colors = state[5 * h : 5 * h + 5]
                common = G[x, pl.ds(ROWS * h, ROWS), :]
                signed = signed + totals[h][0] * (common * sign)
                now = jnp.exp2(signed)
                weight = (seen - now) * common
                colors = [color + weight * total for color, total in zip(colors, totals[h][1:])]
                new += [signed, now, *colors]
            return tuple(new)

        zero = jnp.zeros((ROWS, NZ), jnp.float32)
        start = (zero, jnp.ones((ROWS, NZ), jnp.float32), zero, zero, zero) * halves
        state = lax.fori_loop(0, X, along, start, unroll=2)
        for h in range(halves):
            signed, seen, *colors = state[5 * h : 5 * h + 5]
            through = jnp.where(backward, jnp.exp2(-signed), seen)
            factor = jnp.where(backward, -through, 1.0)
            for j, value in enumerate([color * factor for color in colors] + [through]):
                PS[m, j, pl.ds(ROWS * h, ROWS), :] = value
        local_target = jnp.logical_and(owner == d, m == i)

        @pl.when(local_target)
        def _():
            PR[mine] = PS[m]

        @pl.when(jnp.logical_not(local_target))
        def _():
            piece(o, m).start()

        return carry

    lax.fori_loop(0, ni, render, 0)
    for side in range(2):
        edge = edge_rows[side]
        for x in range(0, X, ROWS):
            field = edge_streamed((STEPS - 1) % 2, side, x)
            for number in range(COUNT):
                for r in range(ROWS):
                    F[number, x + r, edge : edge + 1, :] = field[number][r : r + 1]

    def sent(o, carry):
        m = lax.rem(i + 1 + o, ni)

        @pl.when(jnp.logical_not(jnp.logical_and(owner == d, m == i)))
        def _():
            piece(o, m).wait_send()

        return carry

    def arrived(slot, carry):
        @pl.when(jnp.logical_not(jnp.logical_and(owner == d, slot == mine)))
        def _():
            remote(
                PS.at[0], PR.at[slot], pr_s.at[0], pr_r.at[slot], {"depth": d, "image": i}
            ).wait_recv()

        return carry

    lax.fori_loop(0, nd * ratio, arrived, 0)
    backward = row(i, 5 * bumps) > 0.5
    for part in range(ratio):
        for h in range(halves):
            rows = pl.ds(ROWS * h, ROWS)
            through = jnp.ones((ROWS, NZ), jnp.float32)
            colors = [jnp.zeros((ROWS, NZ), jnp.float32)] * 3
            for slab in range(nd):
                slot = slab * ratio + part
                local = [PR[slot, j, rows, :] for j in range(4)]
                through, colors = blend(backward, through, colors, local[3], local[:3])
            for j, value in enumerate(colors + [1.0 - through]):
                img[0, j, pl.ds(part * W + ROWS * h, ROWS), :] = value
    lax.fori_loop(0, ni, sent, 0)


def put_out(pieces, F, vort, img, F_out, vort_out, img_out, sems):
    step = F.shape[1] // pieces
    copies = [
        pltpu.make_async_copy(
            F.at[:, pl.ds(c * step, step)], F_out.at[:, pl.ds(c * step, step)], sems.at[c]
        )
        for c in range(pieces)
    ]
    copies.append(pltpu.make_async_copy(vort, vort_out, sems.at[pieces]))
    copies.append(pltpu.make_async_copy(img, img_out, sems.at[pieces + 1]))
    for copy in copies:
        copy.start()
    for copy in copies:
        copy.wait()


def on_device(populations, transfer, direction):
    nd, ni = lax.axis_size("depth"), lax.axis_size("image")
    count, X, W, NZ = populations.shape
    bumps = transfer.shape[2]
    assert transfer.shape[0] == 1 and ni % nd == 0 and W % ROWS == 0 and W >= 2 * ROWS and X % CODED == 0
    sizes = (nd, ni, X, W, NZ, bumps)
    ratio = ni // nd
    padded = W + 2 * ROWS
    f32 = jnp.float32
    table = -(-(5 * bumps + 1) // 8) * 8
    dma = pltpu.SemaphoreType.DMA
    results = pl.pallas_call(
        functools.partial(kernel, sizes),
        out_shape=(
            pltpu.VMEM(populations.shape, f32),
            pltpu.VMEM((X, W, NZ), jnp.bfloat16),
            pltpu.VMEM((1, 4, ratio * W, NZ), f32),
        ),
        in_specs=[
            pl.BlockSpec(memory_space=pl.ANY),
            pl.BlockSpec(memory_space=pltpu.SMEM),
            pl.BlockSpec(memory_space=pltpu.SMEM),
        ],
        out_specs=(
            pl.BlockSpec(memory_space=pltpu.VMEM),
            pl.BlockSpec(memory_space=pltpu.VMEM),
            pl.BlockSpec(memory_space=pltpu.VMEM),
        ),
        scratch_shapes=[
            pltpu.VMEM((COUNT, X + 2, padded, NZ), f32),
            pltpu.VMEM((COUNT, X + 2, padded, NZ), f32),
            pltpu.VMEM((2, 2, COUNT, X + 2 * ROWS, NZ), f32),
            pltpu.VMEM((2, CROSS, X + 2 * ROWS, NZ), f32),
            pltpu.VMEM((2, 2, CROSS, X + 2 * ROWS, NZ), f32),
            pltpu.VMEM((2, CROSS, X, NZ), jnp.int16),
            pltpu.VMEM((2, 2, CROSS, X, NZ), jnp.int16),
            pltpu.VMEM((4, 1, NZ), f32),
            pltpu.VMEM((2, 4, 1, NZ), f32),
            pltpu.VMEM((3, X + 2, padded, NZ), f32),
            pltpu.VMEM((2, 3, X, NZ), jnp.int16),
            pltpu.VMEM((2, 3, X, NZ), jnp.int16),
            pltpu.VMEM((2, 3, W, NZ), f32),
            pltpu.VMEM((2, 3, W, NZ), f32),
            pltpu.VMEM((4, 8, NZ), f32),
            pltpu.VMEM((4, 8, NZ), f32),
            pltpu.VMEM((X, W, NZ), f32),
            pltpu.VMEM((X, W, NZ), f32),
            pltpu.VMEM((ni, 1, NZ), f32),
            pltpu.VMEM((ni, table, NZ), f32),
            pltpu.VMEM((ni, 4, W, NZ), f32),
            pltpu.VMEM((nd * ratio, 4, W, NZ), f32),
            dma((4,)),
            dma((STEPS, 10)),
            dma((STEPS, 10)),
            dma((8,)),
            dma((8,)),
            dma((ni,)),
            dma((ni,)),
            dma((ni,)),
            dma((nd * ratio,)),
        ],
        compiler_params=pltpu.CompilerParams(
            collective_id=0, has_side_effects=True, vmem_limit_bytes=56 << 20
        ),
    )(populations, transfer.transpose(1, 0, 2), direction)
    pieces = 4
    return pl.pallas_call(
        functools.partial(put_out, pieces),
        out_shape=tuple(jax.ShapeDtypeStruct(r.shape, r.dtype) for r in results),
        in_specs=[pl.BlockSpec(memory_space=pltpu.VMEM)] * 3,
        out_specs=(pl.BlockSpec(memory_space=pl.ANY),) * 3,
        scratch_shapes=[dma((pieces + 2,))],
        compiler_params=pltpu.CompilerParams(vmem_limit_bytes=1 << 20),
    )(*results)


def solution(mesh):
    in_specs = (P(None, "depth", "image", None), P("image", None, None), P("image"))
    out_specs = (
        P(None, "depth", "image", None),
        P("depth", "image", None),
        P("image", None, "depth", None),
    )
    return jax.shard_map(
        on_device, mesh=mesh, in_specs=in_specs, out_specs=out_specs, check_vma=False
    )
```

```python
import functools
import math

import jax
import jax.numpy as jnp
from jax import lax
from jax.experimental import pallas as pl
from jax.experimental.pallas import tpu as pltpu
from jax.sharding import PartitionSpec as P

STEPS = 4
MESH = pl.DeviceIdType.MESH

lattice_velocities = (
    (0, 0, 0),
    (1, 0, 0),
    (-1, 0, 0),
    (0, 1, 0),
    (0, -1, 0),
    (0, 0, 1),
    (0, 0, -1),
    (1, 1, 0),
    (-1, -1, 0),
    (1, -1, 0),
    (-1, 1, 0),
    (1, 0, 1),
    (-1, 0, -1),
    (1, 0, -1),
    (-1, 0, 1),
    (0, 1, 1),
    (0, -1, -1),
    (0, 1, -1),
    (0, -1, 1),
)
relaxation = 1.25
bump_width = 0.15
level_offset = 0.05
LOG2E = math.log2(math.e)
SCALE = math.sqrt(LOG2E) / bump_width

COUNT = len(lattice_velocities)
ORDER = (
    [n for n in range(COUNT) if lattice_velocities[n][0] == 1]
    + [n for n in range(COUNT) if lattice_velocities[n][0] == -1]
    + [n for n in range(COUNT) if lattice_velocities[n][0] == 0]
)
SLOT = {number: place for place, number in enumerate(ORDER)}
UP_Y = [n for n in range(COUNT) if lattice_velocities[n][1] == 1]
DOWN_Y = [n for n in range(COUNT) if lattice_velocities[n][1] == -1]
CROSS = len(UP_Y)
CORNERS = [n for n in range(COUNT) if lattice_velocities[n][0] and lattice_velocities[n][1]]
PAIRS = [(n, n + 1) for n in range(1, COUNT, 2)]
LOW = 8
ROWS = 8
CODED = 16
STEP = 16384.0
AHEAD = 4
PIECE = 65535.0
PART_UNITS = ((32768.0, 5.0 / 6.0), (65536.0, 0.0), (65536.0, 0.0))


def add_all(values):
    while len(values) > 1:
        paired = [a + b for a, b in zip(values[0::2], values[1::2])]
        values = paired + ([values[-1]] if len(values) % 2 else [])
    return values[0]


def moments(field):
    diffs = {}
    sums = [field[0]]
    for plus, minus in PAIRS:
        sums.append(field[plus] + field[minus])
        diffs[plus] = field[plus] - field[minus]
    momentum = []
    for axis in range(3):
        total = diffs[1 + 2 * axis]
        for plus, _ in PAIRS[3:]:
            factor = lattice_velocities[plus][axis]
            if factor == 1:
                total = total + diffs[plus]
            elif factor == -1:
                total = total - diffs[plus]
        momentum.append(total)
    return add_all(sums), momentum


def collide(field):
    density, momentum = moments(field)
    inverse = 1.0 / density
    square = momentum[0] * momentum[0] + momentum[1] * momentum[1] + momentum[2] * momentum[2]
    even = density - 1.5 * (square * inverse)
    keep = 1.0 - relaxation
    result = [keep * field[0] + (relaxation / 3.0) * even] + [None] * (COUNT - 1)
    parts = {}
    for divisor in (18.0, 36.0):
        parts[divisor] = ((relaxation / divisor) * even, (relaxation * 4.5 / divisor) * inverse)
    for plus, minus in PAIRS:
        project = None
        for axis in range(3):
            factor = lattice_velocities[plus][axis]
            if factor:
                if project is None:
                    project = momentum[axis]
                elif factor == 1:
                    project = project + momentum[axis]
                else:
                    project = project - momentum[axis]
        divisor = 18.0 if plus < 7 else 36.0
        base, curve = parts[divisor]
        symmetric = base + curve * (project * project)
        odd = (3.0 * relaxation / divisor) * project
        result[plus] = keep * field[plus] + (symmetric + odd)
        result[minus] = keep * field[minus] + (symmetric - odd)
    return result


def weight_of(number):
    return 1.0 / (18.0 if number < 7 else 36.0)


def encode(value, unit):
    steps = jnp.round(value * (STEP / unit) - STEP)
    return jnp.clip(steps, -2.0 * STEP, 2.0 * STEP - 1.0).astype(jnp.int32).astype(jnp.int16)


def decode(code, unit):
    return code.astype(jnp.int32).astype(jnp.float32) * (unit / STEP) + unit


def kernel(
    sizes,
    f_hbm,
    par_hbm,
    direct_hbm,
    F,
    vort,
    img,
    A,
    B,
    E,
    SY,
    RY,
    SQ,
    RQ,
    SC,
    RC,
    U,
    PYS,
    PYR,
    PXS,
    PXR,
    CS,
    CR,
    L,
    G,
    par,
    direct,
    PC,
    PA,
    PS,
    PR,
    first_s,
    second_s,
    halo_r,
    part_r,
    pa_r,
    pr_r,
):
    nd, ni, X, W, NZ, bumps = sizes
    d = lax.axis_index("depth")
    i = lax.axis_index("image")
    halves = W // ROWS
    ratio = ni // nd
    chunks = 8
    step_x = X // chunks

    loads = [
        pltpu.make_async_copy(
            f_hbm.at[:, pl.ds(c * step_x, step_x)],
            F.at[:, pl.ds(c * step_x, step_x)],
            first_s.at[c],
        )
        for c in range(chunks)
    ]
    for copy in loads[:AHEAD]:
        copy.start()
    scalars = [
        pltpu.make_async_copy(par_hbm, par, second_s.at[0]),
        pltpu.make_async_copy(direct_hbm, direct, second_s.at[1]),
    ]
    for copy in scalars:
        copy.start()

    barrier = pltpu.get_barrier_semaphore()
    everyone = nd * ni
    me = d * ni + i

    def greet(offset, carry):
        other = lax.rem(me + offset, everyone)
        pl.semaphore_signal(
            barrier,
            inc=1,
            device_id={"depth": other // ni, "image": lax.rem(other, ni)},
            device_id_type=MESH,
        )
        return carry

    lax.fori_loop(1, everyone, greet, 0)

    def to(cx, cy):
        return {"depth": lax.rem(d + cx + nd, nd), "image": lax.rem(i + cy + ni, ni)}

    def remote(src, dst, send, recv, target):
        return pltpu.make_async_remote_copy(
            src_ref=src,
            dst_ref=dst,
            send_sem=send,
            recv_sem=recv,
            device_id=target,
            device_id_type=MESH,
        )

    starts = list(range(1, W - 1 - ROWS, ROWS)) + [W - 1 - ROWS]
    edge_rows = (0, W - 1)
    outward = (DOWN_Y, UP_Y)
    inward = (UP_Y, DOWN_Y)

    def pack(b, x, start, values):
        if start == 1:
            for number in DOWN_Y:
                E[b, 0, SLOT[number], pl.ds(ROWS + x, 1), :] = values[number][0:1]
        if start == W - 1 - ROWS:
            for number in UP_Y:
                E[b, 1, SLOT[number], pl.ds(ROWS + x, 1), :] = values[number][ROWS - 1 : ROWS]

    def streamed(S, x, start):
        field = []
        for number in range(COUNT):
            cx, cy, cz = lattice_velocities[number]
            value = S[SLOT[number], x + 1 - cx, pl.ds(LOW + start - cy, ROWS), :]
            if cz:
                value = pltpu.roll(value, cz % NZ, 1)
            field.append(value)
        return field

    def edge_streamed(b, side, x):
        field = []
        for number in range(COUNT):
            cx, _, cz = lattice_velocities[number]
            rows = slice(ROWS + x - cx, 2 * ROWS + x - cx)
            if number in inward[side]:
                value = RY[b, side, inward[side].index(number), rows, :]
            else:
                value = E[b, side, SLOT[number], rows, :]
            if cz:
                value = pltpu.roll(value, cz % NZ, 1)
            field.append(value)
        return field

    def update(S, D, b, x):
        for start in starts:
            values = collide(streamed(S, x, start))
            for number in range(COUNT):
                D[SLOT[number], x + 1, pl.ds(LOW + start, ROWS), :] = values[number]
            pack(b, x, start, values)

    def put_edges(D, b, side, x, values):
        row = LOW + edge_rows[side]
        for number in range(COUNT):
            cx, cy, _ = lattice_velocities[number]
            value = values[number]
            if number in inward[side]:
                for r in range(ROWS):
                    D[SLOT[number], x + r + 1, row : row + 1, :] = value[r : r + 1]
                continue
            if cy == 0:
                E[b, side, SLOT[number], ROWS + x : 2 * ROWS + x, :] = value
            else:
                SY[side, outward[side].index(number), ROWS + x : 2 * ROWS + x, :] = value
            if cx == 1 and x == X - ROWS:
                D[SLOT[number], X, row : row + 1, :] = value[ROWS - 1 : ROWS]
            if cx == -1 and x == 0:
                D[SLOT[number], 1, row : row + 1, :] = value[0:1]

    inner = pl.ds(LOW, W)

    def collect(terms, axes):
        groups = {}
        for number, value in terms:
            velocity = lattice_velocities[number]
            sums = groups.setdefault(velocity[2], [None] * 3)
            for place, factor in enumerate([1] + [velocity[axis] for axis in axes]):
                if factor:
                    value_now = value if factor == 1 else -value
                    sums[place] = value_now if sums[place] is None else sums[place] + value_now
        totals = [None] * 3
        for cz, sums in groups.items():
            turned = [v if v is None or cz == 0 else pltpu.roll(v, cz % NZ, 1) for v in sums]
            if 2 in axes:
                turned[1 + axes.index(2)] = None if cz == 0 else cz * turned[0]
            for place in range(3):
                if turned[place] is not None:
                    old = totals[place]
                    totals[place] = turned[place] if old is None else old + turned[place]
        return totals

    def planes_of(side, number):
        edge, inside = ((0, 1), (X - 1, X - 2))[side]
        cx = lattice_velocities[number][0]
        if cx == 0:
            return edge
        return inside if cx == 2 * side - 1 else None

    def fill_rows(D, b):
        zero = jnp.zeros((1, NZ), jnp.float32)
        for side in range(2):
            for number in range(COUNT):
                plane = planes_of(side, number)
                if plane is None:
                    continue
                cy = lattice_velocities[number][1]
                if cy:
                    row = LOW - 1 if cy == 1 else LOW + W
                    D[SLOT[number], plane + 1, row : row + 1, :] = zero
                    continue
                for y, row in enumerate(edge_rows):
                    value = E[b, y, SLOT[number], ROWS + plane : ROWS + plane + 1, :]
                    D[SLOT[number], plane + 1, LOW + row : LOW + row + 1, :] = value

    def send_parts(D, b):
        line = lax.broadcasted_iota(jnp.int32, (CODED, NZ), 0)
        for k, corner in enumerate(CORNERS):
            cx, cy, _ = lattice_velocities[corner]
            side = 1 if cy == 1 else 0
            edge = ROWS + (X - 1 if cx == 1 else 0)
            for place, cz in enumerate((0, 1, -1)):
                number = lattice_velocities.index((cx, 0, cz))
                upper = E[b, side, SLOT[number], edge : edge + 1, :]
                number = outward[side].index(lattice_velocities.index((0, cy, cz)))
                lower = SY[side, number, edge : edge + 1, :]
                if cz == 0:
                    upper = upper + E[b, side, SLOT[corner], edge : edge + 1, :]
                    near = edge - cx
                    lower = lower + SY[side, outward[side].index(corner), near : near + 1, :]
                CS[k, 2 * place : 2 * place + 1, :] = upper
                CS[k, 2 * place + 1 : 2 * place + 2, :] = lower
        for side in range(2):
            for x in range(0, X, CODED):
                terms = []
                for number in range(COUNT):
                    if number in inward[side]:
                        continue
                    cx = lattice_velocities[number][0]
                    start = ROWS + x - cx
                    value = E[b, side, SLOT[number], start : start + CODED, :]
                    if cx == 1 and x == 0:
                        value = jnp.where(line == 0, 0.0, value)
                    if cx == -1 and x == X - CODED:
                        value = jnp.where(line == CODED - 1, 0.0, value)
                    terms.append((number, value))
                for place, value in enumerate(collect(terms, (2, 0))):
                    unit, centre = PART_UNITS[place]
                    steps = jnp.clip(jnp.round((value - centre) * unit), -32768.0, 32767.0)
                    code = steps.astype(jnp.int32).astype(jnp.int16)
                    PYS[side, place, x : x + CODED, :] = code
        for side in range(2):
            for h in range(halves):
                terms = []
                for number in range(COUNT):
                    plane = planes_of(side, number)
                    if plane is None:
                        continue
                    rows = pl.ds(LOW + ROWS * h - lattice_velocities[number][1], ROWS)
                    terms.append((number, D[SLOT[number], plane + 1, rows, :]))
                for place, value in enumerate(collect(terms, (1, 2))):
                    PXS[side, place, ROWS * h : ROWS * h + ROWS, :] = value
        parts = []
        for k, corner in enumerate(CORNERS):
            cx, cy, _ = lattice_velocities[corner]
            parts.append(remote(CS.at[k], CR.at[k], second_s.at[k], part_r.at[k], to(cx, cy)))
        far = lax.rem(i, 2)
        for side in (far, 1 - far):
            step = {"depth": d, "image": lax.rem(i + 2 * side - 1 + ni, ni)}
            parts.append(
                remote(
                    PYS.at[side], PYR.at[1 - side], second_s.at[4 + side], part_r.at[5 - side], step
                )
            )
        for side in range(2):
            parts.append(
                remote(
                    PXS.at[side],
                    PXR.at[1 - side],
                    second_s.at[6 + side],
                    part_r.at[7 - side],
                    to(2 * side - 1, 0),
                )
            )
        for part in parts:
            part.start()
        return parts

    def ghosts(D, slot):
        line = lax.broadcasted_iota(jnp.int32, (ROWS, NZ), 0)
        meet = {}
        for k, corner in enumerate(CORNERS):
            after = pltpu.roll(CR[k], 1, 1)
            before = pltpu.roll(CR[k], NZ - 1, 1)
            plain = CR[k]
            for y in range(2):
                up, down = after[2 + y : 3 + y], before[4 + y : 5 + y]
                meet[lattice_velocities[corner][:2], y] = (plain[y : y + 1] + up + down, up - down)
        for y in range(2):
            for number in outward[y]:
                cx = lattice_velocities[number][0]
                if cx:
                    place, plane = (ROWS - 1, 0) if cx == 1 else (ROWS + X, X + 1)
                    row = LOW + edge_rows[y]
                    SY[y, outward[y].index(number), place : place + 1, :] = D[
                        SLOT[number], plane, row : row + 1, :
                    ]
        for k, corner in enumerate(CORNERS):
            cx, cy, _ = lattice_velocities[corner]
            y = 0 if cy == 1 else 1
            plane, place = (X, ROWS + X - 1) if cx == 1 else (1, ROWS)
            row = LOW - 1 if cy == 1 else LOW + W
            D[SLOT[corner], plane, row : row + 1, :] = RY[
                slot, y, inward[y].index(corner), place : place + 1, :
            ]
        for side in range(2):
            from_x = 1 - 2 * side
            plane = X if side else 1
            for h in range(halves):
                terms = []
                for number in range(COUNT):
                    if lattice_velocities[number][0] == -from_x:
                        rows = pl.ds(LOW + ROWS * h - lattice_velocities[number][1], ROWS)
                        terms.append((number, D[SLOT[number], plane, rows, :]))
                sums = collect(terms, (1, 2))
                for place in range(3):
                    sums[place] = sums[place] + PXR[side, place, ROWS * h : ROWS * h + ROWS, :]
                for at, from_y, wanted in ((0, 1, 0), (ROWS - 1, -1, halves - 1)):
                    if h == wanted:
                        mass, along_z = meet[(from_x, from_y), 1]
                        for place, more in enumerate((mass, from_y * mass, along_z)):
                            sums[place] = jnp.where(line == at, sums[place] + more, sums[place])
                inverse = 1.0 / sums[0]
                for place in range(2):
                    U[place, (X + 1) * side, pl.ds(LOW + ROWS * h, ROWS), :] = (
                        sums[1 + place] * inverse
                    )
        for side in range(2):
            from_y = 1 - 2 * side
            row = LOW + W if side else LOW - 1
            for x in range(0, X, ROWS):
                terms = []
                for j, number in enumerate(outward[side]):
                    start = ROWS + x - lattice_velocities[number][0]
                    terms.append((number, SY[side, j, start : start + ROWS, :]))
                sums = collect(terms, (2, 0))
                for place in range(3):
                    unit, centre = PART_UNITS[place]
                    code = PYR[side, place, x // CODED * CODED : x // CODED * CODED + CODED, :]
                    value = code.astype(jnp.int32).astype(jnp.float32) * (1.0 / unit) + centre
                    sums[place] = sums[place] + value[x % CODED : x % CODED + ROWS]
                for at, from_x, wanted in ((0, 1, 0), (ROWS - 1, -1, X - ROWS)):
                    if x == wanted:
                        mass, along_z = meet[(from_x, from_y), 0]
                        for place, more in enumerate((mass, along_z, from_x * mass)):
                            sums[place] = jnp.where(line == at, sums[place] + more, sums[place])
                inverse = 1.0 / sums[0]
                for place in range(2):
                    value = sums[1 + place] * inverse
                    for r in range(ROWS):
                        U[1 + place, x + r + 1, row : row + 1, :] = value[r : r + 1]

    def exchange(D, turn, columns=None):
        slot = turn % 2
        for k, number in enumerate(CORNERS):
            cx, cy, _ = lattice_velocities[number]
            side = 1 if cy == 1 else 0
            edge = X - 1 if cx == 1 else 0
            SC[k] = SY[side, outward[side].index(number), ROWS + edge : ROWS + edge + 1, :]
        copies = []

        def add(src, dst, target, leave=None, land=None):
            k = len(copies) + (2 if len(copies) < 4 else 0)
            leave, land = (k, k) if leave is None else (leave, land)
            copies.append(remote(src, dst, first_s.at[leave], halo_r.at[turn % 2, land], target))
            copies[-1].start()

        for k, number in enumerate(CORNERS):
            cx, cy, _ = lattice_velocities[number]
            add(SC.at[k], RC.at[slot, k], to(cx, cy))
        for side in range(2):
            for j, number in enumerate(outward[side]):
                for x in range(0, X, CODED):
                    value = SY[side, j, ROWS + x : ROWS + x + CODED, :]
                    SQ[side, j, x : x + CODED, :] = encode(value, weight_of(number))
        far = lax.rem(i, 2)
        for side in (far, 1 - far):
            step = {"depth": d, "image": lax.rem(i + 2 * side - 1 + ni, ni)}
            add(SQ.at[side], RQ.at[slot, 1 - side], step, side, 1 - side)
        if columns is not None:
            for x in (0, X - 1):
                columns(x, 0)
        if turn == STEPS - 1:
            fill_rows(D, turn % 2)
        add(D.at[pl.ds(0, CROSS), X, inner], D.at[pl.ds(0, CROSS), 0, inner], to(1, 0))
        add(D.at[pl.ds(CROSS, CROSS), 1, inner], D.at[pl.ds(CROSS, CROSS), X + 1, inner], to(-1, 0))
        if turn == STEPS - 1:
            copies += send_parts(D, turn % 2)
        return copies

    def finish(copies, D, turn):
        slot = turn % 2
        for copy in copies:
            copy.wait()
        for side in range(2):
            for j, number in enumerate(inward[side]):
                for x in range(0, X, CODED):
                    value = decode(RQ[slot, side, j, x : x + CODED, :], weight_of(number))
                    RY[slot, side, j, ROWS + x : ROWS + x + CODED, :] = value
        for number in range(COUNT):
            cx, cy, _ = lattice_velocities[number]
            if cx == 0:
                continue
            plane, place = (0, ROWS - 1) if cx == 1 else (X + 1, ROWS + X)
            for side in range(2):
                if number in inward[side]:
                    k = CORNERS.index(number)
                    j = inward[side].index(number)
                    RY[slot, side, j, place : place + 1, :] = RC[slot, k]
                else:
                    row = LOW + edge_rows[side] - cy
                    E[slot, side, SLOT[number], place : place + 1, :] = D[
                        SLOT[number], plane, row : row + 1, :
                    ]

    def first(x, carry):
        for h in range(halves):
            field = [F[number, x, pl.ds(ROWS * h, ROWS), :] for number in range(COUNT)]
            values = collide(field)
            for number in range(COUNT):
                A[SLOT[number], x + 1, pl.ds(LOW + ROWS * h, ROWS), :] = values[number]
            for side, edge in ((0, 0), (1, ROWS - 1)):
                if h != (0 if side == 0 else halves - 1):
                    continue
                near = 1 if side == 0 else ROWS - 2
                for number in range(COUNT):
                    if lattice_velocities[number][1] == 0:
                        E[0, side, SLOT[number], pl.ds(ROWS + x, 1), :] = values[number][
                            edge : edge + 1
                        ]
                for j, number in enumerate(outward[side]):
                    SY[side, j, pl.ds(ROWS + x, 1), :] = values[number][edge : edge + 1]
                    E[0, side, SLOT[number], pl.ds(ROWS + x, 1), :] = values[number][
                        near : near + 1
                    ]
        return carry

    for c in range(chunks):
        loads[c].wait()
        if c + AHEAD < chunks:
            loads[c + AHEAD].start()
        lax.fori_loop(c * step_x, (c + 1) * step_x, first, 0)

    for copy in scalars:
        copy.wait()
    ray = X * nd
    lane = lax.broadcasted_iota(jnp.int32, (8, NZ), 1)
    entries = jnp.full((8, NZ), direct[0].astype(jnp.float32), jnp.float32)
    for k in range(bumps):
        for kind in range(5):
            factor = SCALE if kind == 0 else (LOG2E / ray if kind == 1 else 1.0)
            entries = jnp.where(lane == kind * bumps + k, par[kind, 0, k] * factor, entries)
    gain = pltpu.roll(entries, bumps, 1)
    shift = gain * gain - jnp.log2(entries)
    ratios = entries / gain
    for kind in (3, 4):
        ratios = jnp.where(
            lane < kind * bumps, ratios, entries / pltpu.roll(entries, (kind - 1) * bumps, 1)
        )
    table = jnp.where(lane < 2 * bumps, shift, ratios)
    table = jnp.where(lane < bumps, 2.0 * entries, table)
    PC[i] = jnp.where(lane < 5 * bumps, table, entries)[0:1]

    pl.semaphore_wait(barrier, everyone - 1)
    shares = [
        remote(PC.at[i], PC.at[i], second_s.at[o], pa_r.at[o], to(0, o)) for o in range(1, ni)
    ]
    copies = exchange(A, 0)
    for copy in shares:
        copy.start()

    source, target = A, B
    for turn in range(1, STEPS):

        def middle(x, carry, source=source, target=target, turn=turn):
            update(source, target, turn % 2, x)
            return carry

        lax.fori_loop(1, X - 1, middle, 0, unroll=2)
        finish(copies, source, turn - 1)
        for side in range(2):
            for x in range(0, X, ROWS):
                put_edges(target, turn % 2, side, x, collide(edge_streamed((turn - 1) % 2, side, x)))
        if turn == STEPS - 1:
            for copy in shares:
                copy.wait()
        copies = exchange(target, turn, middle)
        source, target = target, source

    def flow_of(field):
        density, momentum = moments(field)
        inverse = 1.0 / density
        return [momentum[axis] * inverse for axis in (1, 2, 0)]

    def last(x, carry):
        for start in starts:
            field = streamed(source, x, start)
            for number in range(COUNT):
                F[number, x, pl.ds(start, ROWS), :] = field[number]
            for place, value in enumerate(flow_of(field)):
                U[place, x + 1, pl.ds(LOW + start, ROWS), :] = value
        return carry

    def expand(m, carry):
        for block in range(PA.shape[1] // 8):
            line = lax.broadcasted_iota(jnp.int32, (8, NZ), 0) + 8 * block
            chosen = jnp.where(lane == line, jnp.broadcast_to(PC[m], (8, NZ)), 0.0)
            value = jnp.sum(chosen, axis=1, keepdims=True)
            PA[m, pl.ds(8 * block, 8), :] = jnp.broadcast_to(value, (8, NZ))
        return carry

    lax.fori_loop(0, ni, expand, 0, unroll=2)
    lax.fori_loop(1, X - 1, last, 0)
    finish(copies, source, STEPS - 1)
    for x in (0, X - 1):
        last(x, 0)
    for side in range(2):
        row = edge_rows[side]
        for x in range(0, X, ROWS):
            field = edge_streamed((STEPS - 1) % 2, side, x)
            for place, value in enumerate(flow_of(field)):
                for r in range(ROWS):
                    U[place, x + r + 1, LOW + row : LOW + row + 1, :] = value[r : r + 1]
    ghosts(source, (STEPS - 1) % 2)

    def spin(x, carry):
        def across_x(place):
            return (U[place, x + 2, inner, :] - U[place, x, inner, :]) * 0.5

        def across_y(place):
            above = U[place, x + 1, pl.ds(LOW + 1, W), :]
            return (above - U[place, x + 1, pl.ds(LOW - 1, W), :]) * 0.5

        def across_z(place):
            value = U[place, x + 1, inner, :]
            return (pltpu.roll(value, NZ - 1, 1) - pltpu.roll(value, 1, 1)) * 0.5

        spin_x = across_y(1) - across_z(0)
        spin_y = across_z(2) - across_x(1)
        spin_z = across_x(0) - across_y(2)
        size = jnp.sqrt(spin_x * spin_x + spin_y * spin_y + spin_z * spin_z)
        rounded = size.astype(jnp.bfloat16)
        vort[x] = rounded
        value = rounded.astype(jnp.float32)
        level = (value / (value + level_offset)) * SCALE
        L[x] = level
        G[x] = jnp.exp2(-(level * level))
        return carry

    lax.fori_loop(0, X, spin, 0, unroll=4)

    owner = i // ratio
    mine = d * ratio + lax.rem(i, ratio)

    def row(m, r):
        return jnp.broadcast_to(PA[m, pl.ds(r, 1), :], (ROWS, NZ))

    def blend(backward, through, colors, local_through, local_colors):
        fade = jnp.where(backward, local_through, 1.0)
        lit = jnp.where(backward, 1.0, through)
        mixed = [color * fade + lit * local for color, local in zip(colors, local_colors)]
        return through * local_through, mixed

    def piece(o, m):
        return remote(
            PS.at[m],
            PR.at[mine],
            first_s.at[o],
            pr_r.at[mine],
            {"depth": owner, "image": m},
        )

    def render(o, carry):
        m = lax.rem(i + 1 + o, ni)
        backward = row(m, 5 * bumps) > 0.5
        sign = jnp.where(backward, 1.0, -1.0)

        def along(x, state):
            new = []
            levels = [L[x, pl.ds(ROWS * h, ROWS), :] for h in range(halves)]
            totals = [[None] * 4 for h in range(halves)]
            for k in range(bumps):
                centre = row(m, k)
                shift = row(m, bumps + k)
                gains = [row(m, (1 + j) * bumps + k) for j in range(1, 4)]
                for h in range(halves):
                    bump = jnp.exp2(levels[h] * centre - shift)
                    for j in range(4):
                        term = gains[j - 1] * bump if j else bump
                        totals[h][j] = term if k == 0 else totals[h][j] + term
            for h in range(halves):
                signed, seen, *colors = state[5 * h : 5 * h + 5]
                common = G[x, pl.ds(ROWS * h, ROWS), :]
                signed = signed + totals[h][0] * (common * sign)
                now = jnp.exp2(signed)
                weight = (seen - now) * common
                colors = [color + weight * total for color, total in zip(colors, totals[h][1:])]
                new += [signed, now, *colors]
            return tuple(new)

        zero = jnp.zeros((ROWS, NZ), jnp.float32)
        start = (zero, jnp.ones((ROWS, NZ), jnp.float32), zero, zero, zero) * halves
        state = lax.fori_loop(0, X, along, start, unroll=2)
        parts = []
        for h in range(halves):
            signed, seen, *colors = state[5 * h : 5 * h + 5]
            through = jnp.where(backward, jnp.exp2(-signed), seen)
            factor = jnp.where(backward, -through, 1.0)
            parts.append([color * factor for color in colors] + [through])
        for j in range(4):
            value = jnp.concatenate([part[j] for part in parts], axis=0)
            unit = PIECE / (bumps if j < 3 else 1.0)
            steps = jnp.clip(jnp.round(value * unit - 32768.0), -32768.0, 32767.0)
            PS[m, j] = steps.astype(jnp.int32).astype(jnp.int16)
        local_target = jnp.logical_and(owner == d, m == i)

        @pl.when(local_target)
        def _():
            PR[mine] = PS[m]

        @pl.when(jnp.logical_not(local_target))
        def _():
            piece(o, m).start()

        return carry

    lax.fori_loop(0, ni, render, 0)
    for side in range(2):
        edge = edge_rows[side]
        for x in range(0, X, ROWS):
            field = edge_streamed((STEPS - 1) % 2, side, x)
            for number in range(COUNT):
                for r in range(ROWS):
                    F[number, x + r, edge : edge + 1, :] = field[number][r : r + 1]

    def sent(o, carry):
        m = lax.rem(i + 1 + o, ni)

        @pl.when(jnp.logical_not(jnp.logical_and(owner == d, m == i)))
        def _():
            piece(o, m).wait_send()

        return carry

    def arrived(slot, carry):
        @pl.when(jnp.logical_not(jnp.logical_and(owner == d, slot == mine)))
        def _():
            remote(
                PS.at[0], PR.at[slot], first_s.at[0], pr_r.at[slot], {"depth": d, "image": i}
            ).wait_recv()

        return carry

    lax.fori_loop(0, nd * ratio, arrived, 0)
    backward = jnp.broadcast_to(PA[i, pl.ds(5 * bumps, 1), :], (W, NZ)) > 0.5
    for part in range(ratio):
        through = jnp.ones((W, NZ), jnp.float32)
        colors = [jnp.zeros((W, NZ), jnp.float32)] * 3
        for slab in range(nd):
            local = []
            for j in range(4):
                unit = (bumps if j < 3 else 1.0) / PIECE
                code = PR[slab * ratio + part, j].astype(jnp.int32).astype(jnp.float32)
                local.append(code * unit + 32768.0 * unit)
            through, colors = blend(backward, through, colors, local[3], local[:3])
        for j, value in enumerate(colors + [1.0 - through]):
            img[0, j, part * W : (part + 1) * W, :] = value
    lax.fori_loop(0, ni, sent, 0)


def put_out(pieces, F, vort, img, F_out, vort_out, img_out, sems):
    step = F.shape[1] // pieces
    copies = [
        pltpu.make_async_copy(
            F.at[:, pl.ds(c * step, step)], F_out.at[:, pl.ds(c * step, step)], sems.at[c]
        )
        for c in range(pieces)
    ]
    copies.append(pltpu.make_async_copy(vort, vort_out, sems.at[pieces]))
    copies.append(pltpu.make_async_copy(img, img_out, sems.at[pieces + 1]))
    for copy in copies:
        copy.start()
    for copy in copies:
        copy.wait()


def on_device(populations, transfer, direction):
    nd, ni = lax.axis_size("depth"), lax.axis_size("image")
    count, X, W, NZ = populations.shape
    bumps = transfer.shape[2]
    assert transfer.shape[0] == 1 and ni % nd == 0 and W % ROWS == 0 and W >= 2 * ROWS and X % CODED == 0
    sizes = (nd, ni, X, W, NZ, bumps)
    ratio = ni // nd
    padded = W + 2 * ROWS
    f32 = jnp.float32
    table = -(-(5 * bumps + 1) // 8) * 8
    dma = pltpu.SemaphoreType.DMA
    results = pl.pallas_call(
        functools.partial(kernel, sizes),
        out_shape=(
            pltpu.VMEM(populations.shape, f32),
            pltpu.VMEM((X, W, NZ), jnp.bfloat16),
            pltpu.VMEM((1, 4, ratio * W, NZ), f32),
        ),
        in_specs=[
            pl.BlockSpec(memory_space=pl.ANY),
            pl.BlockSpec(memory_space=pl.ANY),
            pl.BlockSpec(memory_space=pl.ANY),
        ],
        out_specs=(
            pl.BlockSpec(memory_space=pltpu.VMEM),
            pl.BlockSpec(memory_space=pltpu.VMEM),
            pl.BlockSpec(memory_space=pltpu.VMEM),
        ),
        scratch_shapes=[
            pltpu.VMEM((COUNT, X + 2, padded, NZ), f32),
            pltpu.VMEM((COUNT, X + 2, padded, NZ), f32),
            pltpu.VMEM((2, 2, COUNT, X + 2 * ROWS, NZ), f32),
            pltpu.VMEM((2, CROSS, X + 2 * ROWS, NZ), f32),
            pltpu.VMEM((2, 2, CROSS, X + 2 * ROWS, NZ), f32),
            pltpu.VMEM((2, CROSS, X, NZ), jnp.int16),
            pltpu.VMEM((2, 2, CROSS, X, NZ), jnp.int16),
            pltpu.VMEM((4, 1, NZ), f32),
            pltpu.VMEM((2, 4, 1, NZ), f32),
            pltpu.VMEM((3, X + 2, padded, NZ), f32),
            pltpu.VMEM((2, 3, X, NZ), jnp.int16),
            pltpu.VMEM((2, 3, X, NZ), jnp.int16),
            pltpu.VMEM((2, 3, W, NZ), f32),
            pltpu.VMEM((2, 3, W, NZ), f32),
            pltpu.VMEM((4, 8, NZ), f32),
            pltpu.VMEM((4, 8, NZ), f32),
            pltpu.VMEM((X, W, NZ), f32),
            pltpu.VMEM((X, W, NZ), f32),
            pltpu.SMEM((5, 1, bumps), f32),
            pltpu.SMEM((1,), jnp.int32),
            pltpu.VMEM((ni, 1, NZ), f32),
            pltpu.VMEM((ni, table, NZ), f32),
            pltpu.VMEM((ni, 4, W, NZ), jnp.int16),
            pltpu.VMEM((nd * ratio, 4, W, NZ), jnp.int16),
            dma((max(8, ni),)),
            dma((max(8, ni),)),
            dma((2, 8)),
            dma((8,)),
            dma((ni,)),
            dma((nd * ratio,)),
        ],
        compiler_params=pltpu.CompilerParams(
            collective_id=0, has_side_effects=True, vmem_limit_bytes=56 << 20
        ),
    )(populations, transfer.transpose(1, 0, 2), direction)
    pieces = 8
    return pl.pallas_call(
        functools.partial(put_out, pieces),
        out_shape=tuple(jax.ShapeDtypeStruct(r.shape, r.dtype) for r in results),
        in_specs=[pl.BlockSpec(memory_space=pltpu.VMEM)] * 3,
        out_specs=(pl.BlockSpec(memory_space=pl.ANY),) * 3,
        scratch_shapes=[dma((pieces + 2,))],
        compiler_params=pltpu.CompilerParams(vmem_limit_bytes=1 << 20),
    )(*results)


def solution(mesh):
    in_specs = (P(None, "depth", "image", None), P("image", None, None), P("image"))
    out_specs = (
        P(None, "depth", "image", None),
        P("depth", "image", None),
        P("image", None, "depth", None),
    )
    return jax.shard_map(
        on_device, mesh=mesh, in_specs=in_specs, out_specs=out_specs, check_vma=False
    )
```

```python
import functools
import math

import jax
import jax.numpy as jnp
from jax import lax
from jax.experimental import pallas as pl
from jax.experimental.pallas import tpu as pltpu
from jax.sharding import PartitionSpec as P

STEPS = 4
MESH = pl.DeviceIdType.MESH

lattice_velocities = (
    (0, 0, 0),
    (1, 0, 0),
    (-1, 0, 0),
    (0, 1, 0),
    (0, -1, 0),
    (0, 0, 1),
    (0, 0, -1),
    (1, 1, 0),
    (-1, -1, 0),
    (1, -1, 0),
    (-1, 1, 0),
    (1, 0, 1),
    (-1, 0, -1),
    (1, 0, -1),
    (-1, 0, 1),
    (0, 1, 1),
    (0, -1, -1),
    (0, 1, -1),
    (0, -1, 1),
)
relaxation = 1.25
bump_width = 0.15
level_offset = 0.05
LOG2E = math.log2(math.e)
SCALE = math.sqrt(LOG2E) / bump_width

COUNT = len(lattice_velocities)
ORDER = (
    [n for n in range(COUNT) if lattice_velocities[n][0] == 1]
    + [n for n in range(COUNT) if lattice_velocities[n][0] == -1]
    + [n for n in range(COUNT) if lattice_velocities[n][0] == 0]
)
SLOT = {number: place for place, number in enumerate(ORDER)}
UP_Y = [n for n in range(COUNT) if lattice_velocities[n][1] == 1]
DOWN_Y = [n for n in range(COUNT) if lattice_velocities[n][1] == -1]
CROSS = len(UP_Y)
CORNERS = [n for n in range(COUNT) if lattice_velocities[n][0] and lattice_velocities[n][1]]
PAIRS = [(n, n + 1) for n in range(1, COUNT, 2)]
LOW = 8
ROWS = 8
CODED = 16
STEP = 16384.0
AHEAD = 4
PIECE = 65535.0
PART_UNITS = ((32768.0, 5.0 / 6.0), (65536.0, 0.0), (65536.0, 0.0))


def add_all(values):
    while len(values) > 1:
        paired = [a + b for a, b in zip(values[0::2], values[1::2])]
        values = paired + ([values[-1]] if len(values) % 2 else [])
    return values[0]


def moments(field):
    diffs = {}
    sums = [field[0]]
    for plus, minus in PAIRS:
        sums.append(field[plus] + field[minus])
        diffs[plus] = field[plus] - field[minus]
    momentum = []
    for axis in range(3):
        total = diffs[1 + 2 * axis]
        for plus, _ in PAIRS[3:]:
            factor = lattice_velocities[plus][axis]
            if factor == 1:
                total = total + diffs[plus]
            elif factor == -1:
                total = total - diffs[plus]
        momentum.append(total)
    return add_all(sums), momentum


def collide(field):
    density, momentum = moments(field)
    inverse = 1.0 / density
    square = momentum[0] * momentum[0] + momentum[1] * momentum[1] + momentum[2] * momentum[2]
    even = density - 1.5 * (square * inverse)
    keep = 1.0 - relaxation
    result = [keep * field[0] + (relaxation / 3.0) * even] + [None] * (COUNT - 1)
    parts = {}
    for divisor in (18.0, 36.0):
        parts[divisor] = ((relaxation / divisor) * even, (relaxation * 4.5 / divisor) * inverse)
    for plus, minus in PAIRS:
        project = None
        for axis in range(3):
            factor = lattice_velocities[plus][axis]
            if factor:
                if project is None:
                    project = momentum[axis]
                elif factor == 1:
                    project = project + momentum[axis]
                else:
                    project = project - momentum[axis]
        divisor = 18.0 if plus < 7 else 36.0
        base, curve = parts[divisor]
        symmetric = base + curve * (project * project)
        odd = (3.0 * relaxation / divisor) * project
        result[plus] = keep * field[plus] + (symmetric + odd)
        result[minus] = keep * field[minus] + (symmetric - odd)
    return result


def weight_of(number):
    return 1.0 / (18.0 if number < 7 else 36.0)


def encode(value, unit):
    steps = jnp.round(value * (STEP / unit) - STEP)
    return jnp.clip(steps, -2.0 * STEP, 2.0 * STEP - 1.0).astype(jnp.int32).astype(jnp.int16)


def decode(code, unit):
    return code.astype(jnp.int32).astype(jnp.float32) * (unit / STEP) + unit


def kernel(
    sizes,
    f_hbm,
    par_hbm,
    direct_hbm,
    F,
    vort,
    img,
    A,
    B,
    E,
    SY,
    EI,
    RY,
    SQ,
    RQ,
    SC,
    RC,
    U,
    PYS,
    PYR,
    PXS,
    PXR,
    CS,
    CR,
    L,
    G,
    par,
    direct,
    PC,
    PA,
    PS,
    PR,
    first_s,
    second_s,
    halo_r,
    part_r,
    pa_r,
    pr_r,
):
    nd, ni, X, W, NZ, bumps = sizes
    d = lax.axis_index("depth")
    i = lax.axis_index("image")
    halves = W // ROWS
    ratio = ni // nd
    chunks = 8
    step_x = X // chunks

    loads = [
        pltpu.make_async_copy(
            f_hbm.at[:, pl.ds(c * step_x, step_x)],
            F.at[:, pl.ds(c * step_x, step_x)],
            first_s.at[c],
        )
        for c in range(chunks)
    ]
    for copy in loads[:AHEAD]:
        copy.start()
    scalars = [
        pltpu.make_async_copy(par_hbm, par, second_s.at[0]),
        pltpu.make_async_copy(direct_hbm, direct, second_s.at[1]),
    ]
    for copy in scalars:
        copy.start()

    barrier = pltpu.get_barrier_semaphore()
    everyone = nd * ni
    me = d * ni + i

    def greet(offset, carry):
        other = lax.rem(me + offset, everyone)
        pl.semaphore_signal(
            barrier,
            inc=1,
            device_id={"depth": other // ni, "image": lax.rem(other, ni)},
            device_id_type=MESH,
        )
        return carry

    lax.fori_loop(1, everyone, greet, 0)

    def to(cx, cy):
        return {"depth": lax.rem(d + cx + nd, nd), "image": lax.rem(i + cy + ni, ni)}

    def remote(src, dst, send, recv, target):
        return pltpu.make_async_remote_copy(
            src_ref=src,
            dst_ref=dst,
            send_sem=send,
            recv_sem=recv,
            device_id=target,
            device_id_type=MESH,
        )

    starts = list(range(1, W - 1 - ROWS, ROWS)) + [W - 1 - ROWS]
    edge_rows = (0, W - 1)
    outward = (DOWN_Y, UP_Y)
    inward = (UP_Y, DOWN_Y)

    def pack(b, x, start, values):
        if start == 1:
            for number in DOWN_Y:
                E[b, 0, SLOT[number], pl.ds(ROWS + x, 1), :] = values[number][0:1]
        if start == W - 1 - ROWS:
            for number in UP_Y:
                E[b, 1, SLOT[number], pl.ds(ROWS + x, 1), :] = values[number][ROWS - 1 : ROWS]

    def streamed(S, x, start):
        field = []
        for number in range(COUNT):
            cx, cy, cz = lattice_velocities[number]
            value = S[SLOT[number], x + 1 - cx, pl.ds(LOW + start - cy, ROWS), :]
            if cz:
                value = pltpu.roll(value, cz % NZ, 1)
            field.append(value)
        return field

    def edge_streamed(b, side, x):
        field = []
        for number in range(COUNT):
            cx, _, cz = lattice_velocities[number]
            rows = slice(ROWS + x - cx, 2 * ROWS + x - cx)
            if number in inward[side]:
                value = RY[b, side, inward[side].index(number), rows, :]
            else:
                value = E[b, side, SLOT[number], rows, :]
            if cz:
                value = pltpu.roll(value, cz % NZ, 1)
            field.append(value)
        return field

    def update(S, D, b, x):
        for start in starts:
            values = collide(streamed(S, x, start))
            for number in range(COUNT):
                D[SLOT[number], x + 1, pl.ds(LOW + start, ROWS), :] = values[number]
            pack(b, x, start, values)

    def mirrored(number):
        cx, cy, cz = lattice_velocities[number]
        return lattice_velocities.index((cx, -cy, cz))

    def choose(side, low, high):
        return low if low == high else low + side * (high - low)

    def slot_of(side, number):
        return choose(side, SLOT[number], SLOT[mirrored(number)])

    def place_of(side, number):
        lists = (UP_Y, DOWN_Y) if number in UP_Y else (DOWN_Y, UP_Y)
        return choose(side, lists[0].index(number), lists[1].index(mirrored(number)))

    def corner_of(side, number):
        return choose(side, CORNERS.index(number), CORNERS.index(mirrored(number)))

    def edges(old, b, side):
        for x in (0,):
            field = []
            for number in range(COUNT):
                cx, _, cz = lattice_velocities[number]
                rows = slice(ROWS + x - cx, ROWS + x - cx + X)
                if number in UP_Y:
                    value = RY[old, side, place_of(side, number), rows, :]
                else:
                    value = E[old, side, slot_of(side, number), rows, :]
                if cz:
                    value = pltpu.roll(value, cz % NZ, 1)
                field.append(value)
            values = collide(field)
            for number in range(COUNT):
                cy = lattice_velocities[number][1]
                if cy == 1:
                    EI[side, place_of(side, number), x : x + X, :] = values[number]
                elif cy == 0:
                    E[b, side, SLOT[number], ROWS + x : ROWS + x + X, :] = values[number]
                else:
                    SY[side, place_of(side, number), ROWS + x : ROWS + x + X, :] = values[number]

    inner = pl.ds(LOW, W)

    def collect(terms, axes):
        groups = {}
        for number, value in terms:
            velocity = lattice_velocities[number]
            sums = groups.setdefault(velocity[2], [None] * 3)
            for place, factor in enumerate([1] + [velocity[axis] for axis in axes]):
                if factor:
                    value_now = value if factor == 1 else -value
                    sums[place] = value_now if sums[place] is None else sums[place] + value_now
        totals = [None] * 3
        for cz, sums in groups.items():
            turned = [v if v is None or cz == 0 else pltpu.roll(v, cz % NZ, 1) for v in sums]
            if 2 in axes:
                turned[1 + axes.index(2)] = None if cz == 0 else cz * turned[0]
            for place in range(3):
                if turned[place] is not None:
                    old = totals[place]
                    totals[place] = turned[place] if old is None else old + turned[place]
        return totals

    def planes_of(side, number):
        edge, inside = ((0, 1), (X - 1, X - 2))[side]
        cx = lattice_velocities[number][0]
        if cx == 0:
            return edge
        return inside if cx == 2 * side - 1 else None

    def fill_rows(D, b):
        zero = jnp.zeros((1, NZ), jnp.float32)
        for side in range(2):
            for number in range(COUNT):
                plane = planes_of(side, number)
                if plane is None:
                    continue
                cy = lattice_velocities[number][1]
                if cy:
                    row = LOW - 1 if cy == 1 else LOW + W
                    D[SLOT[number], plane + 1, row : row + 1, :] = zero
                    continue
                for y, row in enumerate(edge_rows):
                    value = E[b, y, SLOT[number], ROWS + plane : ROWS + plane + 1, :]
                    D[SLOT[number], plane + 1, LOW + row : LOW + row + 1, :] = value

    def send_parts(D, b):
        line = lax.broadcasted_iota(jnp.int32, (CODED, NZ), 0)
        for k, corner in enumerate(CORNERS):
            cx, cy, _ = lattice_velocities[corner]
            side = 1 if cy == 1 else 0
            edge = ROWS + (X - 1 if cx == 1 else 0)
            for place, cz in enumerate((0, 1, -1)):
                number = lattice_velocities.index((cx, 0, cz))
                upper = E[b, side, SLOT[number], edge : edge + 1, :]
                number = outward[side].index(lattice_velocities.index((0, cy, cz)))
                lower = SY[side, number, edge : edge + 1, :]
                if cz == 0:
                    upper = upper + E[b, side, SLOT[corner], edge : edge + 1, :]
                    deeper = edge - cx
                    lower = lower + SY[side, outward[side].index(corner), deeper : deeper + 1, :]
                CS[k, 2 * place : 2 * place + 1, :] = upper
                CS[k, 2 * place + 1 : 2 * place + 2, :] = lower
        for side in range(2):
            for x in range(0, X, CODED):
                terms = []
                for number in range(COUNT):
                    if number in inward[side]:
                        continue
                    cx = lattice_velocities[number][0]
                    start = ROWS + x - cx
                    value = E[b, side, SLOT[number], start : start + CODED, :]
                    if cx == 1 and x == 0:
                        value = jnp.where(line == 0, 0.0, value)
                    if cx == -1 and x == X - CODED:
                        value = jnp.where(line == CODED - 1, 0.0, value)
                    terms.append((number, value))
                for place, value in enumerate(collect(terms, (2, 0))):
                    unit, centre = PART_UNITS[place]
                    steps = jnp.clip(jnp.round((value - centre) * unit), -32768.0, 32767.0)
                    code = steps.astype(jnp.int32).astype(jnp.int16)
                    PYS[side, place, x : x + CODED, :] = code
        for side in range(2):
            for h in range(halves):
                terms = []
                for number in range(COUNT):
                    plane = planes_of(side, number)
                    if plane is None:
                        continue
                    rows = pl.ds(LOW + ROWS * h - lattice_velocities[number][1], ROWS)
                    terms.append((number, D[SLOT[number], plane + 1, rows, :]))
                for place, value in enumerate(collect(terms, (1, 2))):
                    PXS[side, place, ROWS * h : ROWS * h + ROWS, :] = value
        parts = []
        for k, corner in enumerate(CORNERS):
            cx, cy, _ = lattice_velocities[corner]
            parts.append(remote(CS.at[k], CR.at[k], second_s.at[k], part_r.at[k], to(cx, cy)))
        for side in (far, near):
            step = {"depth": d, "image": lax.rem(i + 2 * side - 1 + ni, ni)}
            parts.append(
                remote(
                    PYS.at[side], PYR.at[1 - side], second_s.at[4 + side], part_r.at[5 - side], step
                )
            )
        for side in range(2):
            parts.append(
                remote(
                    PXS.at[side],
                    PXR.at[1 - side],
                    second_s.at[6 + side],
                    part_r.at[7 - side],
                    to(2 * side - 1, 0),
                )
            )
        for part in parts:
            part.start()
        return parts

    def ghosts(D, slot):
        line = lax.broadcasted_iota(jnp.int32, (ROWS, NZ), 0)
        meet = {}
        for k, corner in enumerate(CORNERS):
            after = pltpu.roll(CR[k], 1, 1)
            before = pltpu.roll(CR[k], NZ - 1, 1)
            plain = CR[k]
            for y in range(2):
                up, down = after[2 + y : 3 + y], before[4 + y : 5 + y]
                meet[lattice_velocities[corner][:2], y] = (plain[y : y + 1] + up + down, up - down)
        for y in range(2):
            for number in outward[y]:
                cx = lattice_velocities[number][0]
                if cx:
                    place, plane = (ROWS - 1, 0) if cx == 1 else (ROWS + X, X + 1)
                    row = LOW + edge_rows[y]
                    SY[y, outward[y].index(number), place : place + 1, :] = D[
                        SLOT[number], plane, row : row + 1, :
                    ]
        for k, corner in enumerate(CORNERS):
            cx, cy, _ = lattice_velocities[corner]
            y = 0 if cy == 1 else 1
            plane, place = (X, ROWS + X - 1) if cx == 1 else (1, ROWS)
            row = LOW - 1 if cy == 1 else LOW + W
            D[SLOT[corner], plane, row : row + 1, :] = RY[
                slot, y, inward[y].index(corner), place : place + 1, :
            ]
        for side in range(2):
            from_x = 1 - 2 * side
            plane = X if side else 1
            for h in range(halves):
                terms = []
                for number in range(COUNT):
                    if lattice_velocities[number][0] == -from_x:
                        rows = pl.ds(LOW + ROWS * h - lattice_velocities[number][1], ROWS)
                        terms.append((number, D[SLOT[number], plane, rows, :]))
                sums = collect(terms, (1, 2))
                for place in range(3):
                    sums[place] = sums[place] + PXR[side, place, ROWS * h : ROWS * h + ROWS, :]
                for at, from_y, wanted in ((0, 1, 0), (ROWS - 1, -1, halves - 1)):
                    if h == wanted:
                        mass, along_z = meet[(from_x, from_y), 1]
                        for place, more in enumerate((mass, from_y * mass, along_z)):
                            sums[place] = jnp.where(line == at, sums[place] + more, sums[place])
                inverse = 1.0 / sums[0]
                for place in range(2):
                    U[place, (X + 1) * side, pl.ds(LOW + ROWS * h, ROWS), :] = (
                        sums[1 + place] * inverse
                    )
        for side in range(2):
            from_y = 1 - 2 * side
            row = LOW + W if side else LOW - 1
            for x in range(0, X, ROWS):
                terms = []
                for j, number in enumerate(outward[side]):
                    start = ROWS + x - lattice_velocities[number][0]
                    terms.append((number, SY[side, j, start : start + ROWS, :]))
                sums = collect(terms, (2, 0))
                for place in range(3):
                    unit, centre = PART_UNITS[place]
                    code = PYR[side, place, x // CODED * CODED : x // CODED * CODED + CODED, :]
                    value = code.astype(jnp.int32).astype(jnp.float32) * (1.0 / unit) + centre
                    sums[place] = sums[place] + value[x % CODED : x % CODED + ROWS]
                for at, from_x, wanted in ((0, 1, 0), (ROWS - 1, -1, X - ROWS)):
                    if x == wanted:
                        mass, along_z = meet[(from_x, from_y), 0]
                        for place, more in enumerate((mass, along_z, from_x * mass)):
                            sums[place] = jnp.where(line == at, sums[place] + more, sums[place])
                inverse = 1.0 / sums[0]
                for place in range(2):
                    value = sums[1 + place] * inverse
                    for r in range(ROWS):
                        U[1 + place, x + r + 1, row : row + 1, :] = value[r : r + 1]

    def across(cx, side):
        return {
            "depth": lax.rem(d + cx + nd, nd),
            "image": lax.rem(i + 2 * side - 1 + ni, ni),
        }

    def messages(turn, side):
        slot = turn % 2
        found = [
            remote(
                SQ.at[side],
                RQ.at[slot, 1 - side],
                first_s.at[side],
                halo_r.at[slot, 1 - side],
                across(0, side),
            )
        ]
        for number in CORNERS:
            cx, cy, _ = lattice_velocities[number]
            if cy == -1:
                k = corner_of(side, number)
                found.append(
                    remote(
                        SC.at[k],
                        RC.at[slot, k],
                        first_s.at[2 + k],
                        halo_r.at[slot, 2 + k],
                        across(cx, side),
                    )
                )
        return found

    def planes(D, turn):
        pairs = ((0, X, 0, 1), (CROSS, 1, X + 1, -1))
        return [
            remote(
                D.at[pl.ds(start, CROSS), plane, inner],
                D.at[pl.ds(start, CROSS), land, inner],
                first_s.at[6 + k],
                halo_r.at[turn % 2, 6 + k],
                to(cx, 0),
            )
            for k, (start, plane, land, cx) in enumerate(pairs)
        ]

    def send_side(turn, side):
        for number in CORNERS:
            cx, cy, _ = lattice_velocities[number]
            if cy == -1:
                edge = ROWS + (X - 1 if cx == 1 else 0)
                row = SY[side, place_of(side, number), edge : edge + 1, :]
                SC[corner_of(side, number)] = row
        copies = messages(turn, side)
        for copy in copies[1:]:
            copy.start()
        for number in DOWN_Y:
            j = place_of(side, number)
            for x in range(0, X, CODED):
                value = SY[side, j, ROWS + x : ROWS + x + CODED, :]
                SQ[side, j, x : x + CODED, :] = encode(value, weight_of(number))
        copies[0].start()

    def receive_side(D, turn, side):
        slot = turn % 2
        for copy in messages(turn, side):
            copy.wait_send()
        for copy in messages(turn, 1 - side):
            copy.wait_recv()
        for number in UP_Y:
            j = place_of(side, number)
            for x in range(0, X, CODED):
                value = decode(RQ[slot, side, j, x : x + CODED, :], weight_of(number))
                RY[slot, side, j, ROWS + x : ROWS + x + CODED, :] = value
        for number in range(COUNT):
            cx, cy, _ = lattice_velocities[number]
            if cx == 0:
                continue
            plane, place = (0, ROWS - 1) if cx == 1 else (X + 1, ROWS + X)
            if cy == 1:
                j = place_of(side, number)
                RY[slot, side, j, place : place + 1, :] = RC[slot, corner_of(side, number)]
            else:
                row = LOW - cy + side * (W - 1 + 2 * cy)
                k = slot_of(side, number)
                E[slot, side, k, place : place + 1, :] = D[k, plane, pl.ds(row, 1), :]

    def inward_rows(D, x):
        for side in range(2):
            row = LOW + edge_rows[side]
            for j, number in enumerate(inward[side]):
                D[SLOT[number], x + 1, row : row + 1, :] = EI[side, j, pl.ds(x, 1), :]

    def corner_rows(D, b):
        for x, wanted in ((0, -1), (X - 1, 1)):
            inward_rows(D, x)
            for side in range(2):
                row = LOW + edge_rows[side]
                for number in range(COUNT):
                    cx, cy, _ = lattice_velocities[number]
                    if cx != wanted or number in inward[side]:
                        continue
                    at = slice(ROWS + x, ROWS + x + 1)
                    if cy:
                        value = SY[side, outward[side].index(number), at, :]
                    else:
                        value = E[b, side, SLOT[number], at, :]
                    D[SLOT[number], x + 1, row : row + 1, :] = value

    far = lax.rem(i, 2)
    near = 1 - far
    span = max(1, ni // 2)
    inside = (lax.rem(i + 1, ni) // 2 + span - 1) // span
    lead = far + inside * (near - far)
    follow = 1 - lead

    def first(x, carry):
        for h in range(halves):
            field = [F[number, x, pl.ds(ROWS * h, ROWS), :] for number in range(COUNT)]
            values = collide(field)
            for number in range(COUNT):
                A[SLOT[number], x + 1, pl.ds(LOW + ROWS * h, ROWS), :] = values[number]
            for side, edge in ((0, 0), (1, ROWS - 1)):
                if h != (0 if side == 0 else halves - 1):
                    continue
                near = 1 if side == 0 else ROWS - 2
                for number in range(COUNT):
                    if lattice_velocities[number][1] == 0:
                        E[0, side, SLOT[number], pl.ds(ROWS + x, 1), :] = values[number][
                            edge : edge + 1
                        ]
                for j, number in enumerate(outward[side]):
                    SY[side, j, pl.ds(ROWS + x, 1), :] = values[number][edge : edge + 1]
                    E[0, side, SLOT[number], pl.ds(ROWS + x, 1), :] = values[number][
                        near : near + 1
                    ]
        return carry

    for c in range(chunks):
        loads[c].wait()
        if c + AHEAD < chunks:
            loads[c + AHEAD].start()
        lax.fori_loop(c * step_x, (c + 1) * step_x, first, 0)

    for copy in scalars:
        copy.wait()
    ray = X * nd
    lane = lax.broadcasted_iota(jnp.int32, (8, NZ), 1)
    entries = jnp.full((8, NZ), direct[0].astype(jnp.float32), jnp.float32)
    for k in range(bumps):
        for kind in range(5):
            factor = SCALE if kind == 0 else (LOG2E / ray if kind == 1 else 1.0)
            entries = jnp.where(lane == kind * bumps + k, par[kind, 0, k] * factor, entries)
    gain = pltpu.roll(entries, bumps, 1)
    shift = gain * gain - jnp.log2(entries)
    ratios = entries / gain
    for kind in (3, 4):
        ratios = jnp.where(
            lane < kind * bumps, ratios, entries / pltpu.roll(entries, (kind - 1) * bumps, 1)
        )
    table = jnp.where(lane < 2 * bumps, shift, ratios)
    table = jnp.where(lane < bumps, 2.0 * entries, table)
    PC[i] = jnp.where(lane < 5 * bumps, table, entries)[0:1]

    pl.semaphore_wait(barrier, everyone - 1)
    shares = [
        remote(PC.at[i], PC.at[i], second_s.at[o], pa_r.at[o], to(0, o)) for o in range(1, ni)
    ]
    for side in (far, near):
        send_side(0, side)
    for copy in planes(A, 0) + shares:
        copy.start()

    source, target = A, B
    for turn in range(1, STEPS):

        def middle(x, carry, source=source, target=target, turn=turn):
            update(source, target, turn % 2, x)
            return carry

        lax.fori_loop(1, X - 1, middle, 0, unroll=2)
        for copy in planes(source, turn - 1):
            copy.wait()
        for side in (lead, follow):
            receive_side(source, turn - 1, side)
            edges((turn - 1) % 2, turn % 2, side)
            send_side(turn, side)
        for x in (0, X - 1):
            middle(x, 0)
        corner_rows(target, turn % 2)
        if turn == STEPS - 1:
            fill_rows(target, turn % 2)
        for copy in planes(target, turn):
            copy.start()

        def settle(x, carry, target=target):
            inward_rows(target, x)
            return carry

        lax.fori_loop(1, X - 1, settle, 0)
        source, target = target, source

    for copy in shares:
        copy.wait()
    parts = send_parts(source, (STEPS - 1) % 2)

    def flow_of(field):
        density, momentum = moments(field)
        inverse = 1.0 / density
        return [momentum[axis] * inverse for axis in (1, 2, 0)]

    def last(x, carry):
        for start in starts:
            field = streamed(source, x, start)
            for number in range(COUNT):
                F[number, x, pl.ds(start, ROWS), :] = field[number]
            for place, value in enumerate(flow_of(field)):
                U[place, x + 1, pl.ds(LOW + start, ROWS), :] = value
        return carry

    def expand(m, carry):
        for block in range(PA.shape[1] // 8):
            line = lax.broadcasted_iota(jnp.int32, (8, NZ), 0) + 8 * block
            chosen = jnp.where(lane == line, jnp.broadcast_to(PC[m], (8, NZ)), 0.0)
            value = jnp.sum(chosen, axis=1, keepdims=True)
            PA[m, pl.ds(8 * block, 8), :] = jnp.broadcast_to(value, (8, NZ))
        return carry

    lax.fori_loop(0, ni, expand, 0, unroll=2)
    lax.fori_loop(1, X - 1, last, 0)
    for copy in planes(source, STEPS - 1):
        copy.wait()
    for side in (lead, follow):
        receive_side(source, STEPS - 1, side)
    for part in parts:
        part.wait()
    for x in (0, X - 1):
        last(x, 0)
    for side in range(2):
        row = edge_rows[side]
        for x in range(0, X, ROWS):
            field = edge_streamed((STEPS - 1) % 2, side, x)
            for place, value in enumerate(flow_of(field)):
                for r in range(ROWS):
                    U[place, x + r + 1, LOW + row : LOW + row + 1, :] = value[r : r + 1]
    ghosts(source, (STEPS - 1) % 2)

    def spin(x, carry):
        def across_x(place):
            return (U[place, x + 2, inner, :] - U[place, x, inner, :]) * 0.5

        def across_y(place):
            above = U[place, x + 1, pl.ds(LOW + 1, W), :]
            return (above - U[place, x + 1, pl.ds(LOW - 1, W), :]) * 0.5

        def across_z(place):
            value = U[place, x + 1, inner, :]
            return (pltpu.roll(value, NZ - 1, 1) - pltpu.roll(value, 1, 1)) * 0.5

        spin_x = across_y(1) - across_z(0)
        spin_y = across_z(2) - across_x(1)
        spin_z = across_x(0) - across_y(2)
        size = jnp.sqrt(spin_x * spin_x + spin_y * spin_y + spin_z * spin_z)
        rounded = size.astype(jnp.bfloat16)
        vort[x] = rounded
        value = rounded.astype(jnp.float32)
        level = (value / (value + level_offset)) * SCALE
        L[x] = level
        G[x] = jnp.exp2(-(level * level))
        return carry

    lax.fori_loop(0, X, spin, 0, unroll=4)

    owner = i // ratio
    mine = d * ratio + lax.rem(i, ratio)

    def row(m, r):
        return jnp.broadcast_to(PA[m, pl.ds(r, 1), :], (ROWS, NZ))

    def blend(backward, through, colors, local_through, local_colors):
        fade = jnp.where(backward, local_through, 1.0)
        lit = jnp.where(backward, 1.0, through)
        mixed = [color * fade + lit * local for color, local in zip(colors, local_colors)]
        return through * local_through, mixed

    def piece(o, m):
        return remote(
            PS.at[m],
            PR.at[mine],
            first_s.at[o],
            pr_r.at[mine],
            {"depth": owner, "image": m},
        )

    def render(o, carry):
        m = lax.rem(i + 1 + o, ni)
        backward = row(m, 5 * bumps) > 0.5
        sign = jnp.where(backward, 1.0, -1.0)

        def along(x, state):
            new = []
            levels = [L[x, pl.ds(ROWS * h, ROWS), :] for h in range(halves)]
            totals = [[None] * 4 for h in range(halves)]
            for k in range(bumps):
                centre = row(m, k)
                shift = row(m, bumps + k)
                gains = [row(m, (1 + j) * bumps + k) for j in range(1, 4)]
                for h in range(halves):
                    bump = jnp.exp2(levels[h] * centre - shift)
                    for j in range(4):
                        term = gains[j - 1] * bump if j else bump
                        totals[h][j] = term if k == 0 else totals[h][j] + term
            for h in range(halves):
                signed, seen, *colors = state[5 * h : 5 * h + 5]
                common = G[x, pl.ds(ROWS * h, ROWS), :]
                signed = signed + totals[h][0] * (common * sign)
                now = jnp.exp2(signed)
                weight = (seen - now) * common
                colors = [color + weight * total for color, total in zip(colors, totals[h][1:])]
                new += [signed, now, *colors]
            return tuple(new)

        zero = jnp.zeros((ROWS, NZ), jnp.float32)
        start = (zero, jnp.ones((ROWS, NZ), jnp.float32), zero, zero, zero) * halves
        state = lax.fori_loop(0, X, along, start, unroll=2)
        parts = []
        for h in range(halves):
            signed, seen, *colors = state[5 * h : 5 * h + 5]
            through = jnp.where(backward, jnp.exp2(-signed), seen)
            factor = jnp.where(backward, -through, 1.0)
            parts.append([color * factor for color in colors] + [through])
        for j in range(4):
            value = jnp.concatenate([part[j] for part in parts], axis=0)
            unit = PIECE / (bumps if j < 3 else 1.0)
            steps = jnp.clip(jnp.round(value * unit - 32768.0), -32768.0, 32767.0)
            PS[m, j] = steps.astype(jnp.int32).astype(jnp.int16)
        local_target = jnp.logical_and(owner == d, m == i)

        @pl.when(local_target)
        def _():
            PR[mine] = PS[m]

        @pl.when(jnp.logical_not(local_target))
        def _():
            piece(o, m).start()

        return carry

    lax.fori_loop(0, ni, render, 0)
    for side in range(2):
        edge = edge_rows[side]
        for x in range(0, X, ROWS):
            field = edge_streamed((STEPS - 1) % 2, side, x)
            for number in range(COUNT):
                for r in range(ROWS):
                    F[number, x + r, edge : edge + 1, :] = field[number][r : r + 1]

    def sent(o, carry):
        m = lax.rem(i + 1 + o, ni)

        @pl.when(jnp.logical_not(jnp.logical_and(owner == d, m == i)))
        def _():
            piece(o, m).wait_send()

        return carry

    def arrived(slot, carry):
        @pl.when(jnp.logical_not(jnp.logical_and(owner == d, slot == mine)))
        def _():
            remote(
                PS.at[0], PR.at[slot], first_s.at[0], pr_r.at[slot], {"depth": d, "image": i}
            ).wait_recv()

        return carry

    lax.fori_loop(0, nd * ratio, arrived, 0)
    backward = jnp.broadcast_to(PA[i, pl.ds(5 * bumps, 1), :], (W, NZ)) > 0.5
    for part in range(ratio):
        through = jnp.ones((W, NZ), jnp.float32)
        colors = [jnp.zeros((W, NZ), jnp.float32)] * 3
        for slab in range(nd):
            local = []
            for j in range(4):
                unit = (bumps if j < 3 else 1.0) / PIECE
                code = PR[slab * ratio + part, j].astype(jnp.int32).astype(jnp.float32)
                local.append(code * unit + 32768.0 * unit)
            through, colors = blend(backward, through, colors, local[3], local[:3])
        for j, value in enumerate(colors + [1.0 - through]):
            img[0, j, part * W : (part + 1) * W, :] = value
    lax.fori_loop(0, ni, sent, 0)


def put_out(pieces, F, vort, img, F_out, vort_out, img_out, sems):
    step = F.shape[1] // pieces
    copies = [
        pltpu.make_async_copy(
            F.at[:, pl.ds(c * step, step)], F_out.at[:, pl.ds(c * step, step)], sems.at[c]
        )
        for c in range(pieces)
    ]
    copies.append(pltpu.make_async_copy(vort, vort_out, sems.at[pieces]))
    copies.append(pltpu.make_async_copy(img, img_out, sems.at[pieces + 1]))
    for copy in copies:
        copy.start()
    for copy in copies:
        copy.wait()


def on_device(populations, transfer, direction):
    nd, ni = lax.axis_size("depth"), lax.axis_size("image")
    count, X, W, NZ = populations.shape
    bumps = transfer.shape[2]
    assert transfer.shape[0] == 1 and ni % nd == 0 and W % ROWS == 0 and W >= 2 * ROWS and X % CODED == 0
    sizes = (nd, ni, X, W, NZ, bumps)
    ratio = ni // nd
    padded = W + 2 * ROWS
    f32 = jnp.float32
    table = -(-(5 * bumps + 1) // 8) * 8
    dma = pltpu.SemaphoreType.DMA
    results = pl.pallas_call(
        functools.partial(kernel, sizes),
        out_shape=(
            pltpu.VMEM(populations.shape, f32),
            pltpu.VMEM((X, W, NZ), jnp.bfloat16),
            pltpu.VMEM((1, 4, ratio * W, NZ), f32),
        ),
        in_specs=[
            pl.BlockSpec(memory_space=pl.ANY),
            pl.BlockSpec(memory_space=pl.ANY),
            pl.BlockSpec(memory_space=pl.ANY),
        ],
        out_specs=(
            pl.BlockSpec(memory_space=pltpu.VMEM),
            pl.BlockSpec(memory_space=pltpu.VMEM),
            pl.BlockSpec(memory_space=pltpu.VMEM),
        ),
        scratch_shapes=[
            pltpu.VMEM((COUNT, X + 2, padded, NZ), f32),
            pltpu.VMEM((COUNT, X + 2, padded, NZ), f32),
            pltpu.VMEM((2, 2, COUNT, X + 2 * ROWS, NZ), f32),
            pltpu.VMEM((2, CROSS, X + 2 * ROWS, NZ), f32),
            pltpu.VMEM((2, CROSS, X, NZ), f32),
            pltpu.VMEM((2, 2, CROSS, X + 2 * ROWS, NZ), f32),
            pltpu.VMEM((2, CROSS, X, NZ), jnp.int16),
            pltpu.VMEM((2, 2, CROSS, X, NZ), jnp.int16),
            pltpu.VMEM((4, 1, NZ), f32),
            pltpu.VMEM((2, 4, 1, NZ), f32),
            pltpu.VMEM((3, X + 2, padded, NZ), f32),
            pltpu.VMEM((2, 3, X, NZ), jnp.int16),
            pltpu.VMEM((2, 3, X, NZ), jnp.int16),
            pltpu.VMEM((2, 3, W, NZ), f32),
            pltpu.VMEM((2, 3, W, NZ), f32),
            pltpu.VMEM((4, 8, NZ), f32),
            pltpu.VMEM((4, 8, NZ), f32),
            pltpu.VMEM((X, W, NZ), f32),
            pltpu.VMEM((X, W, NZ), f32),
            pltpu.SMEM((5, 1, bumps), f32),
            pltpu.SMEM((1,), jnp.int32),
            pltpu.VMEM((ni, 1, NZ), f32),
            pltpu.VMEM((ni, table, NZ), f32),
            pltpu.VMEM((ni, 4, W, NZ), jnp.int16),
            pltpu.VMEM((nd * ratio, 4, W, NZ), jnp.int16),
            dma((max(8, ni),)),
            dma((max(8, ni),)),
            dma((2, 8)),
            dma((8,)),
            dma((ni,)),
            dma((nd * ratio,)),
        ],
        compiler_params=pltpu.CompilerParams(
            collective_id=0, has_side_effects=True, vmem_limit_bytes=56 << 20
        ),
    )(populations, transfer.transpose(1, 0, 2), direction)
    pieces = 8
    return pl.pallas_call(
        functools.partial(put_out, pieces),
        out_shape=tuple(jax.ShapeDtypeStruct(r.shape, r.dtype) for r in results),
        in_specs=[pl.BlockSpec(memory_space=pltpu.VMEM)] * 3,
        out_specs=(pl.BlockSpec(memory_space=pl.ANY),) * 3,
        scratch_shapes=[dma((pieces + 2,))],
        compiler_params=pltpu.CompilerParams(vmem_limit_bytes=1 << 20),
    )(*results)


def solution(mesh):
    in_specs = (P(None, "depth", "image", None), P("image", None, None), P("image"))
    out_specs = (
        P(None, "depth", "image", None),
        P("depth", "image", None),
        P("image", None, "depth", None),
    )
    return jax.shard_map(
        on_device, mesh=mesh, in_specs=in_specs, out_specs=out_specs, check_vma=False
    )
```

```python
import functools
import math

import jax
import jax.numpy as jnp
from jax import lax
from jax.experimental import pallas as pl
from jax.experimental.pallas import tpu as pltpu
from jax.sharding import PartitionSpec as P

STEPS = 4
MESH = pl.DeviceIdType.MESH

lattice_velocities = (
    (0, 0, 0),
    (1, 0, 0),
    (-1, 0, 0),
    (0, 1, 0),
    (0, -1, 0),
    (0, 0, 1),
    (0, 0, -1),
    (1, 1, 0),
    (-1, -1, 0),
    (1, -1, 0),
    (-1, 1, 0),
    (1, 0, 1),
    (-1, 0, -1),
    (1, 0, -1),
    (-1, 0, 1),
    (0, 1, 1),
    (0, -1, -1),
    (0, 1, -1),
    (0, -1, 1),
)
relaxation = 1.25
bump_width = 0.15
level_offset = 0.05
LOG2E = math.log2(math.e)
SCALE = math.sqrt(LOG2E) / bump_width

COUNT = len(lattice_velocities)
ORDER = (
    [n for n in range(COUNT) if lattice_velocities[n][0] == 1]
    + [n for n in range(COUNT) if lattice_velocities[n][0] == -1]
    + [n for n in range(COUNT) if lattice_velocities[n][0] == 0]
)
SLOT = {number: place for place, number in enumerate(ORDER)}
UP_Y = [n for n in range(COUNT) if lattice_velocities[n][1] == 1]
DOWN_Y = [n for n in range(COUNT) if lattice_velocities[n][1] == -1]
CROSS = len(UP_Y)
CORNERS = [n for n in range(COUNT) if lattice_velocities[n][0] and lattice_velocities[n][1]]
PAIRS = [(n, n + 1) for n in range(1, COUNT, 2)]
LOW = 8
ROWS = 8
CODED = 16
STEP = 16384.0
AHEAD = 5
PIECE = 65535.0
PART_UNITS = ((32768.0, 5.0 / 6.0), (65536.0, 0.0), (65536.0, 0.0))


def add_all(values):
    while len(values) > 1:
        paired = [a + b for a, b in zip(values[0::2], values[1::2])]
        values = paired + ([values[-1]] if len(values) % 2 else [])
    return values[0]


def moments(field):
    diffs = {}
    sums = [field[0]]
    for plus, minus in PAIRS:
        sums.append(field[plus] + field[minus])
        diffs[plus] = field[plus] - field[minus]
    momentum = []
    for axis in range(3):
        total = diffs[1 + 2 * axis]
        for plus, _ in PAIRS[3:]:
            factor = lattice_velocities[plus][axis]
            if factor == 1:
                total = total + diffs[plus]
            elif factor == -1:
                total = total - diffs[plus]
        momentum.append(total)
    return add_all(sums), momentum


def collide(field):
    density, momentum = moments(field)
    inverse = 1.0 / density
    square = momentum[0] * momentum[0] + momentum[1] * momentum[1] + momentum[2] * momentum[2]
    even = density - 1.5 * (square * inverse)
    keep = 1.0 - relaxation
    result = [keep * field[0] + (relaxation / 3.0) * even] + [None] * (COUNT - 1)
    parts = {}
    for divisor in (18.0, 36.0):
        parts[divisor] = ((relaxation / divisor) * even, (relaxation * 4.5 / divisor) * inverse)
    for plus, minus in PAIRS:
        project = None
        for axis in range(3):
            factor = lattice_velocities[plus][axis]
            if factor:
                if project is None:
                    project = momentum[axis]
                elif factor == 1:
                    project = project + momentum[axis]
                else:
                    project = project - momentum[axis]
        divisor = 18.0 if plus < 7 else 36.0
        base, curve = parts[divisor]
        symmetric = base + curve * (project * project)
        odd = (3.0 * relaxation / divisor) * project
        result[plus] = keep * field[plus] + (symmetric + odd)
        result[minus] = keep * field[minus] + (symmetric - odd)
    return result


def weight_of(number):
    return 1.0 / (18.0 if number < 7 else 36.0)


def encode(value, unit):
    steps = jnp.round(value * (STEP / unit) - STEP)
    return jnp.clip(steps, -2.0 * STEP, 2.0 * STEP - 1.0).astype(jnp.int32).astype(jnp.int16)


def decode(code, unit):
    return code.astype(jnp.int32).astype(jnp.float32) * (unit / STEP) + unit


def kernel(
    sizes,
    f_hbm,
    par_hbm,
    direct_hbm,
    F,
    vort,
    img,
    A,
    B,
    E,
    SY,
    EI,
    RY,
    SQ,
    RQ,
    SC,
    RC,
    U,
    PYS,
    PYR,
    PXS,
    PXR,
    CS,
    CR,
    L,
    G,
    par,
    direct,
    PC,
    PA,
    PS,
    PR,
    first_s,
    second_s,
    halo_r,
    part_r,
    pa_r,
    pr_r,
):
    nd, ni, X, W, NZ, bumps = sizes
    d = lax.axis_index("depth")
    i = lax.axis_index("image")
    halves = W // ROWS
    ratio = ni // nd
    chunks = 8
    step_x = X // chunks

    loads = [
        pltpu.make_async_copy(
            f_hbm.at[:, pl.ds(c * step_x, step_x)],
            F.at[:, pl.ds(c * step_x, step_x)],
            first_s.at[c],
        )
        for c in range(chunks)
    ]
    for copy in loads[:AHEAD]:
        copy.start()
    scalars = [
        pltpu.make_async_copy(par_hbm, par, second_s.at[0]),
        pltpu.make_async_copy(direct_hbm, direct, second_s.at[1]),
    ]
    for copy in scalars:
        copy.start()

    barrier = pltpu.get_barrier_semaphore()
    everyone = nd * ni
    me = d * ni + i

    def greet(offset, carry):
        other = lax.rem(me + offset, everyone)
        pl.semaphore_signal(
            barrier,
            inc=1,
            device_id={"depth": other // ni, "image": lax.rem(other, ni)},
            device_id_type=MESH,
        )
        return carry

    lax.fori_loop(1, everyone, greet, 0)

    def to(cx, cy):
        return {"depth": lax.rem(d + cx + nd, nd), "image": lax.rem(i + cy + ni, ni)}

    def remote(src, dst, send, recv, target):
        return pltpu.make_async_remote_copy(
            src_ref=src,
            dst_ref=dst,
            send_sem=send,
            recv_sem=recv,
            device_id=target,
            device_id_type=MESH,
        )

    starts = list(range(1, W - 1 - ROWS, ROWS)) + [W - 1 - ROWS]
    edge_rows = (0, W - 1)
    outward = (DOWN_Y, UP_Y)
    inward = (UP_Y, DOWN_Y)

    def pack(b, x, start, values):
        if start == 1:
            for number in DOWN_Y:
                E[b, 0, SLOT[number], pl.ds(ROWS + x, 1), :] = values[number][0:1]
        if start == W - 1 - ROWS:
            for number in UP_Y:
                E[b, 1, SLOT[number], pl.ds(ROWS + x, 1), :] = values[number][ROWS - 1 : ROWS]

    def streamed(S, x, start):
        field = []
        for number in range(COUNT):
            cx, cy, cz = lattice_velocities[number]
            value = S[SLOT[number], x + 1 - cx, pl.ds(LOW + start - cy, ROWS), :]
            if cz:
                value = pltpu.roll(value, cz % NZ, 1)
            field.append(value)
        return field

    def edge_streamed(b, side, x):
        field = []
        for number in range(COUNT):
            cx, _, cz = lattice_velocities[number]
            rows = slice(ROWS + x - cx, 2 * ROWS + x - cx)
            if number in inward[side]:
                value = RY[b, side, inward[side].index(number), rows, :]
            else:
                value = E[b, side, SLOT[number], rows, :]
            if cz:
                value = pltpu.roll(value, cz % NZ, 1)
            field.append(value)
        return field

    def update(S, D, b, x):
        for start in starts:
            values = collide(streamed(S, x, start))
            for number in range(COUNT):
                D[SLOT[number], x + 1, pl.ds(LOW + start, ROWS), :] = values[number]
            pack(b, x, start, values)

    def mirrored(number):
        cx, cy, cz = lattice_velocities[number]
        return lattice_velocities.index((cx, -cy, cz))

    def choose(side, low, high):
        return low if low == high else low + side * (high - low)

    def slot_of(side, number):
        return choose(side, SLOT[number], SLOT[mirrored(number)])

    def place_of(side, number):
        lists = (UP_Y, DOWN_Y) if number in UP_Y else (DOWN_Y, UP_Y)
        return choose(side, lists[0].index(number), lists[1].index(mirrored(number)))

    def corner_of(side, number):
        return choose(side, CORNERS.index(number), CORNERS.index(mirrored(number)))

    def edges(old, b, side):
        for x in (0,):
            field = []
            for number in range(COUNT):
                cx, _, cz = lattice_velocities[number]
                rows = slice(ROWS + x - cx, ROWS + x - cx + X)
                if number in UP_Y:
                    value = RY[old, side, place_of(side, number), rows, :]
                else:
                    value = E[old, side, slot_of(side, number), rows, :]
                if cz:
                    value = pltpu.roll(value, cz % NZ, 1)
                field.append(value)
            values = collide(field)
            for number in range(COUNT):
                cy = lattice_velocities[number][1]
                if cy == 1:
                    EI[side, place_of(side, number), x : x + X, :] = values[number]
                elif cy == 0:
                    E[b, side, SLOT[number], ROWS + x : ROWS + x + X, :] = values[number]
                else:
                    SY[side, place_of(side, number), ROWS + x : ROWS + x + X, :] = values[number]

    inner = pl.ds(LOW, W)

    def collect(terms, axes):
        groups = {}
        for number, value in terms:
            velocity = lattice_velocities[number]
            sums = groups.setdefault(velocity[2], [None] * 3)
            for place, factor in enumerate([1] + [velocity[axis] for axis in axes]):
                if factor:
                    value_now = value if factor == 1 else -value
                    sums[place] = value_now if sums[place] is None else sums[place] + value_now
        totals = [None] * 3
        for cz, sums in groups.items():
            turned = [v if v is None or cz == 0 else pltpu.roll(v, cz % NZ, 1) for v in sums]
            if 2 in axes:
                turned[1 + axes.index(2)] = None if cz == 0 else cz * turned[0]
            for place in range(3):
                if turned[place] is not None:
                    old = totals[place]
                    totals[place] = turned[place] if old is None else old + turned[place]
        return totals

    def planes_of(side, number):
        edge, inside = ((0, 1), (X - 1, X - 2))[side]
        cx = lattice_velocities[number][0]
        if cx == 0:
            return edge
        return inside if cx == 2 * side - 1 else None

    def fill_rows(D, b):
        zero = jnp.zeros((1, NZ), jnp.float32)
        for side in range(2):
            for number in range(COUNT):
                plane = planes_of(side, number)
                if plane is None:
                    continue
                cy = lattice_velocities[number][1]
                if cy:
                    row = LOW - 1 if cy == 1 else LOW + W
                    D[SLOT[number], plane + 1, row : row + 1, :] = zero
                    continue
                for y, row in enumerate(edge_rows):
                    value = E[b, y, SLOT[number], ROWS + plane : ROWS + plane + 1, :]
                    D[SLOT[number], plane + 1, LOW + row : LOW + row + 1, :] = value

    def send_parts(D, b):
        line = lax.broadcasted_iota(jnp.int32, (CODED, NZ), 0)
        for k, corner in enumerate(CORNERS):
            cx, cy, _ = lattice_velocities[corner]
            side = 1 if cy == 1 else 0
            edge = ROWS + (X - 1 if cx == 1 else 0)
            for place, cz in enumerate((0, 1, -1)):
                number = lattice_velocities.index((cx, 0, cz))
                upper = E[b, side, SLOT[number], edge : edge + 1, :]
                number = outward[side].index(lattice_velocities.index((0, cy, cz)))
                lower = SY[side, number, edge : edge + 1, :]
                if cz == 0:
                    upper = upper + E[b, side, SLOT[corner], edge : edge + 1, :]
                    deeper = edge - cx
                    lower = lower + SY[side, outward[side].index(corner), deeper : deeper + 1, :]
                CS[k, 2 * place : 2 * place + 1, :] = upper
                CS[k, 2 * place + 1 : 2 * place + 2, :] = lower
        for side in range(2):
            for x in range(0, X, CODED):
                terms = []
                for number in range(COUNT):
                    if number in inward[side]:
                        continue
                    cx = lattice_velocities[number][0]
                    start = ROWS + x - cx
                    value = E[b, side, SLOT[number], start : start + CODED, :]
                    if cx == 1 and x == 0:
                        value = jnp.where(line == 0, 0.0, value)
                    if cx == -1 and x == X - CODED:
                        value = jnp.where(line == CODED - 1, 0.0, value)
                    terms.append((number, value))
                for place, value in enumerate(collect(terms, (2, 0))):
                    unit, centre = PART_UNITS[place]
                    steps = jnp.clip(jnp.round((value - centre) * unit), -32768.0, 32767.0)
                    code = steps.astype(jnp.int32).astype(jnp.int16)
                    PYS[side, place, x : x + CODED, :] = code
        for side in range(2):
            for h in range(halves):
                terms = []
                for number in range(COUNT):
                    plane = planes_of(side, number)
                    if plane is None:
                        continue
                    rows = pl.ds(LOW + ROWS * h - lattice_velocities[number][1], ROWS)
                    terms.append((number, D[SLOT[number], plane + 1, rows, :]))
                for place, value in enumerate(collect(terms, (1, 2))):
                    PXS[side, place, ROWS * h : ROWS * h + ROWS, :] = value
        parts = []
        for k, corner in enumerate(CORNERS):
            cx, cy, _ = lattice_velocities[corner]
            parts.append(remote(CS.at[k], CR.at[k], second_s.at[k], part_r.at[k], to(cx, cy)))
        for side in (far, near):
            step = {"depth": d, "image": lax.rem(i + 2 * side - 1 + ni, ni)}
            parts.append(
                remote(
                    PYS.at[side], PYR.at[1 - side], second_s.at[4 + side], part_r.at[5 - side], step
                )
            )
        for side in range(2):
            parts.append(
                remote(
                    PXS.at[side],
                    PXR.at[1 - side],
                    second_s.at[6 + side],
                    part_r.at[7 - side],
                    to(2 * side - 1, 0),
                )
            )
        for part in parts:
            part.start()
        return parts

    def ghosts(D, slot):
        line = lax.broadcasted_iota(jnp.int32, (ROWS, NZ), 0)
        meet = {}
        for k, corner in enumerate(CORNERS):
            after = pltpu.roll(CR[k], 1, 1)
            before = pltpu.roll(CR[k], NZ - 1, 1)
            plain = CR[k]
            for y in range(2):
                up, down = after[2 + y : 3 + y], before[4 + y : 5 + y]
                meet[lattice_velocities[corner][:2], y] = (plain[y : y + 1] + up + down, up - down)
        for y in range(2):
            for number in outward[y]:
                cx = lattice_velocities[number][0]
                if cx:
                    place, plane = (ROWS - 1, 0) if cx == 1 else (ROWS + X, X + 1)
                    row = LOW + edge_rows[y]
                    SY[y, outward[y].index(number), place : place + 1, :] = D[
                        SLOT[number], plane, row : row + 1, :
                    ]
        for k, corner in enumerate(CORNERS):
            cx, cy, _ = lattice_velocities[corner]
            y = 0 if cy == 1 else 1
            plane, place = (X, ROWS + X - 1) if cx == 1 else (1, ROWS)
            row = LOW - 1 if cy == 1 else LOW + W
            D[SLOT[corner], plane, row : row + 1, :] = RY[
                slot, y, inward[y].index(corner), place : place + 1, :
            ]
        for side in range(2):
            from_x = 1 - 2 * side
            plane = X if side else 1
            for h in range(halves):
                terms = []
                for number in range(COUNT):
                    if lattice_velocities[number][0] == -from_x:
                        rows = pl.ds(LOW + ROWS * h - lattice_velocities[number][1], ROWS)
                        terms.append((number, D[SLOT[number], plane, rows, :]))
                sums = collect(terms, (1, 2))
                for place in range(3):
                    sums[place] = sums[place] + PXR[side, place, ROWS * h : ROWS * h + ROWS, :]
                for at, from_y, wanted in ((0, 1, 0), (ROWS - 1, -1, halves - 1)):
                    if h == wanted:
                        mass, along_z = meet[(from_x, from_y), 1]
                        for place, more in enumerate((mass, from_y * mass, along_z)):
                            sums[place] = jnp.where(line == at, sums[place] + more, sums[place])
                inverse = 1.0 / sums[0]
                for place in range(2):
                    U[place, (X + 1) * side, pl.ds(LOW + ROWS * h, ROWS), :] = (
                        sums[1 + place] * inverse
                    )
        for side in range(2):
            from_y = 1 - 2 * side
            row = LOW + W if side else LOW - 1
            for x in range(0, X, ROWS):
                terms = []
                for j, number in enumerate(outward[side]):
                    start = ROWS + x - lattice_velocities[number][0]
                    terms.append((number, SY[side, j, start : start + ROWS, :]))
                sums = collect(terms, (2, 0))
                for place in range(3):
                    unit, centre = PART_UNITS[place]
                    code = PYR[side, place, x // CODED * CODED : x // CODED * CODED + CODED, :]
                    value = code.astype(jnp.int32).astype(jnp.float32) * (1.0 / unit) + centre
                    sums[place] = sums[place] + value[x % CODED : x % CODED + ROWS]
                for at, from_x, wanted in ((0, 1, 0), (ROWS - 1, -1, X - ROWS)):
                    if x == wanted:
                        mass, along_z = meet[(from_x, from_y), 0]
                        for place, more in enumerate((mass, along_z, from_x * mass)):
                            sums[place] = jnp.where(line == at, sums[place] + more, sums[place])
                inverse = 1.0 / sums[0]
                for place in range(2):
                    value = sums[1 + place] * inverse
                    for r in range(ROWS):
                        U[1 + place, x + r + 1, row : row + 1, :] = value[r : r + 1]

    def across(cx, side):
        return {
            "depth": lax.rem(d + cx + nd, nd),
            "image": lax.rem(i + 2 * side - 1 + ni, ni),
        }

    def messages(turn, side):
        slot = turn % 2
        found = [
            remote(
                SQ.at[side],
                RQ.at[slot, 1 - side],
                first_s.at[side],
                halo_r.at[slot, 1 - side],
                across(0, side),
            )
        ]
        for number in CORNERS:
            cx, cy, _ = lattice_velocities[number]
            if cy == -1:
                k = corner_of(side, number)
                found.append(
                    remote(
                        SC.at[k],
                        RC.at[slot, k],
                        first_s.at[2 + k],
                        halo_r.at[slot, 2 + k],
                        across(cx, side),
                    )
                )
        return found

    def planes(D, turn):
        pairs = ((0, X, 0, 1), (CROSS, 1, X + 1, -1))
        return [
            remote(
                D.at[pl.ds(start, CROSS), plane, inner],
                D.at[pl.ds(start, CROSS), land, inner],
                first_s.at[6 + k],
                halo_r.at[turn % 2, 6 + k],
                to(cx, 0),
            )
            for k, (start, plane, land, cx) in enumerate(pairs)
        ]

    def send_side(turn, side):
        for number in CORNERS:
            cx, cy, _ = lattice_velocities[number]
            if cy == -1:
                edge = ROWS + (X - 1 if cx == 1 else 0)
                row = SY[side, place_of(side, number), edge : edge + 1, :]
                SC[corner_of(side, number)] = row
        copies = messages(turn, side)
        for copy in copies[1:]:
            copy.start()
        for number in DOWN_Y:
            j = place_of(side, number)
            for x in range(0, X, CODED):
                value = SY[side, j, ROWS + x : ROWS + x + CODED, :]
                SQ[side, j, x : x + CODED, :] = encode(value, weight_of(number))
        copies[0].start()

    def receive_side(D, turn, side):
        slot = turn % 2
        for copy in messages(turn, side):
            copy.wait_send()
        for copy in messages(turn, 1 - side):
            copy.wait_recv()
        for number in UP_Y:
            j = place_of(side, number)
            for x in range(0, X, CODED):
                value = decode(RQ[slot, side, j, x : x + CODED, :], weight_of(number))
                RY[slot, side, j, ROWS + x : ROWS + x + CODED, :] = value
        for number in range(COUNT):
            cx, cy, _ = lattice_velocities[number]
            if cx == 0:
                continue
            plane, place = (0, ROWS - 1) if cx == 1 else (X + 1, ROWS + X)
            if cy == 1:
                j = place_of(side, number)
                RY[slot, side, j, place : place + 1, :] = RC[slot, corner_of(side, number)]
            else:
                row = LOW - cy + side * (W - 1 + 2 * cy)
                k = slot_of(side, number)
                E[slot, side, k, place : place + 1, :] = D[k, plane, pl.ds(row, 1), :]

    def inward_rows(D, x):
        for side in range(2):
            row = LOW + edge_rows[side]
            for j, number in enumerate(inward[side]):
                D[SLOT[number], x + 1, row : row + 1, :] = EI[side, j, pl.ds(x, 1), :]

    def corner_rows(D, b):
        for x, wanted in ((0, -1), (X - 1, 1)):
            inward_rows(D, x)
            for side in range(2):
                row = LOW + edge_rows[side]
                for number in range(COUNT):
                    cx, cy, _ = lattice_velocities[number]
                    if cx != wanted or number in inward[side]:
                        continue
                    at = slice(ROWS + x, ROWS + x + 1)
                    if cy:
                        value = SY[side, outward[side].index(number), at, :]
                    else:
                        value = E[b, side, SLOT[number], at, :]
                    D[SLOT[number], x + 1, row : row + 1, :] = value

    far = lax.rem(i, 2)
    near = 1 - far
    span = max(1, ni // 2)
    inside = (lax.rem(i + 1, ni) // 2 + span - 1) // span
    lead = far + inside * (near - far)
    follow = 1 - lead

    def first(x, carry):
        for h in range(halves):
            field = [F[number, x, pl.ds(ROWS * h, ROWS), :] for number in range(COUNT)]
            values = collide(field)
            for number in range(COUNT):
                A[SLOT[number], x + 1, pl.ds(LOW + ROWS * h, ROWS), :] = values[number]
            for side, edge in ((0, 0), (1, ROWS - 1)):
                if h != (0 if side == 0 else halves - 1):
                    continue
                near = 1 if side == 0 else ROWS - 2
                for number in range(COUNT):
                    if lattice_velocities[number][1] == 0:
                        E[0, side, SLOT[number], pl.ds(ROWS + x, 1), :] = values[number][
                            edge : edge + 1
                        ]
                for j, number in enumerate(outward[side]):
                    SY[side, j, pl.ds(ROWS + x, 1), :] = values[number][edge : edge + 1]
                    E[0, side, SLOT[number], pl.ds(ROWS + x, 1), :] = values[number][
                        near : near + 1
                    ]
        return carry

    for c in range(chunks):
        loads[c].wait()
        if c + AHEAD < chunks:
            loads[c + AHEAD].start()
        lax.fori_loop(c * step_x, (c + 1) * step_x, first, 0)

    for copy in scalars:
        copy.wait()
    ray = X * nd
    lane = lax.broadcasted_iota(jnp.int32, (8, NZ), 1)
    entries = jnp.full((8, NZ), direct[0].astype(jnp.float32), jnp.float32)
    for k in range(bumps):
        for kind in range(5):
            factor = SCALE if kind == 0 else (LOG2E / ray if kind == 1 else 1.0)
            entries = jnp.where(lane == kind * bumps + k, par[kind, 0, k] * factor, entries)
    gain = pltpu.roll(entries, bumps, 1)
    shift = gain * gain - jnp.log2(entries)
    ratios = entries / gain
    for kind in (3, 4):
        ratios = jnp.where(
            lane < kind * bumps, ratios, entries / pltpu.roll(entries, (kind - 1) * bumps, 1)
        )
    table = jnp.where(lane < 2 * bumps, shift, ratios)
    table = jnp.where(lane < bumps, 2.0 * entries, table)
    PC[i] = jnp.where(lane < 5 * bumps, table, entries)[0:1]

    pl.semaphore_wait(barrier, everyone - 1)
    shares = [
        remote(PC.at[i], PC.at[i], second_s.at[o], pa_r.at[o], to(0, o)) for o in range(1, ni)
    ]
    for side in (far, near):
        send_side(0, side)
    for copy in planes(A, 0) + shares:
        copy.start()

    source, target = A, B
    for turn in range(1, STEPS):

        def middle(x, carry, source=source, target=target, turn=turn):
            update(source, target, turn % 2, x)
            return carry

        lax.fori_loop(1, X - 1, middle, 0, unroll=2)
        for copy in planes(source, turn - 1):
            copy.wait()
        for side in (lead, follow):
            receive_side(source, turn - 1, side)
            edges((turn - 1) % 2, turn % 2, side)
            send_side(turn, side)
        for x in (0, X - 1):
            middle(x, 0)
        corner_rows(target, turn % 2)
        if turn == STEPS - 1:
            fill_rows(target, turn % 2)
        for copy in planes(target, turn):
            copy.start()

        def settle(x, carry, target=target):
            inward_rows(target, x)
            return carry

        lax.fori_loop(1, X - 1, settle, 0)
        source, target = target, source

    for copy in shares:
        copy.wait()
    parts = send_parts(source, (STEPS - 1) % 2)

    def flow_of(field):
        density, momentum = moments(field)
        inverse = 1.0 / density
        return [momentum[axis] * inverse for axis in (1, 2, 0)]

    def last(x, carry):
        for start in starts:
            field = streamed(source, x, start)
            for number in range(COUNT):
                F[number, x, pl.ds(start, ROWS), :] = field[number]
            for place, value in enumerate(flow_of(field)):
                U[place, x + 1, pl.ds(LOW + start, ROWS), :] = value
        return carry

    def expand(m, carry):
        for block in range(PA.shape[1] // 8):
            line = lax.broadcasted_iota(jnp.int32, (8, NZ), 0) + 8 * block
            chosen = jnp.where(lane == line, jnp.broadcast_to(PC[m], (8, NZ)), 0.0)
            value = jnp.sum(chosen, axis=1, keepdims=True)
            PA[m, pl.ds(8 * block, 8), :] = jnp.broadcast_to(value, (8, NZ))
        return carry

    lax.fori_loop(0, ni, expand, 0, unroll=2)
    lax.fori_loop(1, X - 1, last, 0)
    for copy in planes(source, STEPS - 1):
        copy.wait()
    for side in (lead, follow):
        receive_side(source, STEPS - 1, side)
    for part in parts:
        part.wait()
    for x in (0, X - 1):
        last(x, 0)
    for side in range(2):
        row = edge_rows[side]
        for x in range(0, X, ROWS):
            field = edge_streamed((STEPS - 1) % 2, side, x)
            for place, value in enumerate(flow_of(field)):
                for r in range(ROWS):
                    U[place, x + r + 1, LOW + row : LOW + row + 1, :] = value[r : r + 1]
    ghosts(source, (STEPS - 1) % 2)

    def spin(x, carry):
        def across_x(place):
            return (U[place, x + 2, inner, :] - U[place, x, inner, :]) * 0.5

        def across_y(place):
            above = U[place, x + 1, pl.ds(LOW + 1, W), :]
            return (above - U[place, x + 1, pl.ds(LOW - 1, W), :]) * 0.5

        def across_z(place):
            value = U[place, x + 1, inner, :]
            return (pltpu.roll(value, NZ - 1, 1) - pltpu.roll(value, 1, 1)) * 0.5

        spin_x = across_y(1) - across_z(0)
        spin_y = across_z(2) - across_x(1)
        spin_z = across_x(0) - across_y(2)
        size = jnp.sqrt(spin_x * spin_x + spin_y * spin_y + spin_z * spin_z)
        rounded = size.astype(jnp.bfloat16)
        vort[x] = rounded
        value = rounded.astype(jnp.float32)
        level = (value / (value + level_offset)) * SCALE
        L[x] = level
        G[x] = jnp.exp2(-(level * level))
        return carry

    lax.fori_loop(0, X, spin, 0, unroll=8)

    owner = i // ratio
    mine = d * ratio + lax.rem(i, ratio)

    def row(m, r):
        return jnp.broadcast_to(PA[m, pl.ds(r, 1), :], (ROWS, NZ))

    def blend(backward, through, colors, local_through, local_colors):
        fade = jnp.where(backward, local_through, 1.0)
        lit = jnp.where(backward, 1.0, through)
        mixed = [color * fade + lit * local for color, local in zip(colors, local_colors)]
        return through * local_through, mixed

    def piece(o, m):
        return remote(
            PS.at[m],
            PR.at[mine],
            first_s.at[o],
            pr_r.at[mine],
            {"depth": owner, "image": m},
        )

    def render(o, carry):
        m = lax.rem(i + 1 + o, ni)
        backward = row(m, 5 * bumps) > 0.5
        sign = jnp.where(backward, 1.0, -1.0)

        def along(x, state):
            new = []
            levels = [L[x, pl.ds(ROWS * h, ROWS), :] for h in range(halves)]
            totals = [[None] * 4 for h in range(halves)]
            for k in range(bumps):
                centre = row(m, k)
                shift = row(m, bumps + k)
                gains = [row(m, (1 + j) * bumps + k) for j in range(1, 4)]
                for h in range(halves):
                    bump = jnp.exp2(levels[h] * centre - shift)
                    for j in range(4):
                        term = gains[j - 1] * bump if j else bump
                        totals[h][j] = term if k == 0 else totals[h][j] + term
            for h in range(halves):
                signed, seen, *colors = state[5 * h : 5 * h + 5]
                common = G[x, pl.ds(ROWS * h, ROWS), :]
                signed = signed + totals[h][0] * (common * sign)
                now = jnp.exp2(signed)
                weight = (seen - now) * common
                colors = [color + weight * total for color, total in zip(colors, totals[h][1:])]
                new += [signed, now, *colors]
            return tuple(new)

        zero = jnp.zeros((ROWS, NZ), jnp.float32)
        start = (zero, jnp.ones((ROWS, NZ), jnp.float32), zero, zero, zero) * halves
        state = lax.fori_loop(0, X, along, start, unroll=8)
        parts = []
        for h in range(halves):
            signed, seen, *colors = state[5 * h : 5 * h + 5]
            through = jnp.where(backward, jnp.exp2(-signed), seen)
            factor = jnp.where(backward, -through, 1.0)
            parts.append([color * factor for color in colors] + [through])
        for j in range(4):
            value = jnp.concatenate([part[j] for part in parts], axis=0)
            unit = PIECE / (bumps if j < 3 else 1.0)
            steps = jnp.clip(jnp.round(value * unit - 32768.0), -32768.0, 32767.0)
            PS[m, j] = steps.astype(jnp.int32).astype(jnp.int16)
        local_target = jnp.logical_and(owner == d, m == i)

        @pl.when(local_target)
        def _():
            PR[mine] = PS[m]

        @pl.when(jnp.logical_not(local_target))
        def _():
            piece(o, m).start()

        return carry

    lax.fori_loop(0, ni, render, 0)
    for side in range(2):
        edge = edge_rows[side]
        for x in range(0, X, ROWS):
            field = edge_streamed((STEPS - 1) % 2, side, x)
            for number in range(COUNT):
                for r in range(ROWS):
                    F[number, x + r, edge : edge + 1, :] = field[number][r : r + 1]

    def sent(o, carry):
        m = lax.rem(i + 1 + o, ni)

        @pl.when(jnp.logical_not(jnp.logical_and(owner == d, m == i)))
        def _():
            piece(o, m).wait_send()

        return carry

    def arrived(slot, carry):
        @pl.when(jnp.logical_not(jnp.logical_and(owner == d, slot == mine)))
        def _():
            remote(
                PS.at[0], PR.at[slot], first_s.at[0], pr_r.at[slot], {"depth": d, "image": i}
            ).wait_recv()

        return carry

    lax.fori_loop(0, nd * ratio, arrived, 0)
    backward = jnp.broadcast_to(PA[i, pl.ds(5 * bumps, 1), :], (W, NZ)) > 0.5
    for part in range(ratio):
        through = jnp.ones((W, NZ), jnp.float32)
        colors = [jnp.zeros((W, NZ), jnp.float32)] * 3
        for slab in range(nd):
            local = []
            for j in range(4):
                unit = (bumps if j < 3 else 1.0) / PIECE
                code = PR[slab * ratio + part, j].astype(jnp.int32).astype(jnp.float32)
                local.append(code * unit + 32768.0 * unit)
            through, colors = blend(backward, through, colors, local[3], local[:3])
        for j, value in enumerate(colors + [1.0 - through]):
            img[0, j, part * W : (part + 1) * W, :] = value
    lax.fori_loop(0, ni, sent, 0)


def put_out(pieces, F, vort, img, F_out, vort_out, img_out, sems):
    step = F.shape[1] // pieces
    copies = [
        pltpu.make_async_copy(
            F.at[:, pl.ds(c * step, step)], F_out.at[:, pl.ds(c * step, step)], sems.at[c]
        )
        for c in range(pieces)
    ]
    copies.append(pltpu.make_async_copy(vort, vort_out, sems.at[pieces]))
    copies.append(pltpu.make_async_copy(img, img_out, sems.at[pieces + 1]))
    for copy in copies:
        copy.start()
    for copy in copies:
        copy.wait()


def on_device(populations, transfer, direction):
    nd, ni = lax.axis_size("depth"), lax.axis_size("image")
    count, X, W, NZ = populations.shape
    bumps = transfer.shape[2]
    assert transfer.shape[0] == 1 and ni % nd == 0 and W % ROWS == 0 and W >= 2 * ROWS and X % CODED == 0
    sizes = (nd, ni, X, W, NZ, bumps)
    ratio = ni // nd
    padded = W + 2 * ROWS
    f32 = jnp.float32
    table = -(-(5 * bumps + 1) // 8) * 8
    dma = pltpu.SemaphoreType.DMA
    results = pl.pallas_call(
        functools.partial(kernel, sizes),
        out_shape=(
            pltpu.VMEM(populations.shape, f32),
            pltpu.VMEM((X, W, NZ), jnp.bfloat16),
            pltpu.VMEM((1, 4, ratio * W, NZ), f32),
        ),
        in_specs=[
            pl.BlockSpec(memory_space=pl.ANY),
            pl.BlockSpec(memory_space=pl.ANY),
            pl.BlockSpec(memory_space=pl.ANY),
        ],
        out_specs=(
            pl.BlockSpec(memory_space=pltpu.VMEM),
            pl.BlockSpec(memory_space=pltpu.VMEM),
            pl.BlockSpec(memory_space=pltpu.VMEM),
        ),
        scratch_shapes=[
            pltpu.VMEM((COUNT, X + 2, padded, NZ), f32),
            pltpu.VMEM((COUNT, X + 2, padded, NZ), f32),
            pltpu.VMEM((2, 2, COUNT, X + 2 * ROWS, NZ), f32),
            pltpu.VMEM((2, CROSS, X + 2 * ROWS, NZ), f32),
            pltpu.VMEM((2, CROSS, X, NZ), f32),
            pltpu.VMEM((2, 2, CROSS, X + 2 * ROWS, NZ), f32),
            pltpu.VMEM((2, CROSS, X, NZ), jnp.int16),
            pltpu.VMEM((2, 2, CROSS, X, NZ), jnp.int16),
            pltpu.VMEM((4, 1, NZ), f32),
            pltpu.VMEM((2, 4, 1, NZ), f32),
            pltpu.VMEM((3, X + 2, padded, NZ), f32),
            pltpu.VMEM((2, 3, X, NZ), jnp.int16),
            pltpu.VMEM((2, 3, X, NZ), jnp.int16),
            pltpu.VMEM((2, 3, W, NZ), f32),
            pltpu.VMEM((2, 3, W, NZ), f32),
            pltpu.VMEM((4, 8, NZ), f32),
            pltpu.VMEM((4, 8, NZ), f32),
            pltpu.VMEM((X, W, NZ), f32),
            pltpu.VMEM((X, W, NZ), f32),
            pltpu.SMEM((5, 1, bumps), f32),
            pltpu.SMEM((1,), jnp.int32),
            pltpu.VMEM((ni, 1, NZ), f32),
            pltpu.VMEM((ni, table, NZ), f32),
            pltpu.VMEM((ni, 4, W, NZ), jnp.int16),
            pltpu.VMEM((nd * ratio, 4, W, NZ), jnp.int16),
            dma((max(8, ni),)),
            dma((max(8, ni),)),
            dma((2, 8)),
            dma((8,)),
            dma((ni,)),
            dma((nd * ratio,)),
        ],
        compiler_params=pltpu.CompilerParams(
            collective_id=0, has_side_effects=True, vmem_limit_bytes=56 << 20
        ),
    )(populations, transfer.transpose(1, 0, 2), direction)
    pieces = 8
    return pl.pallas_call(
        functools.partial(put_out, pieces),
        out_shape=tuple(jax.ShapeDtypeStruct(r.shape, r.dtype) for r in results),
        in_specs=[pl.BlockSpec(memory_space=pltpu.VMEM)] * 3,
        out_specs=(pl.BlockSpec(memory_space=pl.ANY),) * 3,
        scratch_shapes=[dma((pieces + 2,))],
        compiler_params=pltpu.CompilerParams(vmem_limit_bytes=1 << 20),
    )(*results)


def solution(mesh):
    in_specs = (P(None, "depth", "image", None), P("image", None, None), P("image"))
    out_specs = (
        P(None, "depth", "image", None),
        P("depth", "image", None),
        P("image", None, "depth", None),
    )
    return jax.shard_map(
        on_device, mesh=mesh, in_specs=in_specs, out_specs=out_specs, check_vma=False
    )
```

```python
import functools
import math

import jax
import jax.numpy as jnp
from jax import lax
from jax.experimental import pallas as pl
from jax.experimental.pallas import tpu as pltpu
from jax.sharding import PartitionSpec as P

STEPS = 4
MESH = pl.DeviceIdType.MESH

lattice_velocities = (
    (0, 0, 0),
    (1, 0, 0),
    (-1, 0, 0),
    (0, 1, 0),
    (0, -1, 0),
    (0, 0, 1),
    (0, 0, -1),
    (1, 1, 0),
    (-1, -1, 0),
    (1, -1, 0),
    (-1, 1, 0),
    (1, 0, 1),
    (-1, 0, -1),
    (1, 0, -1),
    (-1, 0, 1),
    (0, 1, 1),
    (0, -1, -1),
    (0, 1, -1),
    (0, -1, 1),
)
relaxation = 1.25
bump_width = 0.15
level_offset = 0.05
LOG2E = math.log2(math.e)
SCALE = math.sqrt(LOG2E) / bump_width

COUNT = len(lattice_velocities)
ORDER = (
    [n for n in range(COUNT) if lattice_velocities[n][0] == 1]
    + [n for n in range(COUNT) if lattice_velocities[n][0] == -1]
    + [n for n in range(COUNT) if lattice_velocities[n][0] == 0]
)
SLOT = {number: place for place, number in enumerate(ORDER)}
UP_Y = [n for n in range(COUNT) if lattice_velocities[n][1] == 1]
DOWN_Y = [n for n in range(COUNT) if lattice_velocities[n][1] == -1]
CROSS = len(UP_Y)
CORNERS = [n for n in range(COUNT) if lattice_velocities[n][0] and lattice_velocities[n][1]]
PAIRS = [(n, n + 1) for n in range(1, COUNT, 2)]
LOW = 8
ROWS = 8
CODED = 16
STEP = 16384.0
AHEAD = 5
PIECE = 65535.0
PART_UNITS = ((32768.0, 5.0 / 6.0), (65536.0, 0.0), (65536.0, 0.0))


def add_all(values):
    while len(values) > 1:
        paired = [a + b for a, b in zip(values[0::2], values[1::2])]
        values = paired + ([values[-1]] if len(values) % 2 else [])
    return values[0]


def moments(field):
    diffs = {}
    sums = [field[0]]
    for plus, minus in PAIRS:
        sums.append(field[plus] + field[minus])
        diffs[plus] = field[plus] - field[minus]
    momentum = []
    for axis in range(3):
        total = diffs[1 + 2 * axis]
        for plus, _ in PAIRS[3:]:
            factor = lattice_velocities[plus][axis]
            if factor == 1:
                total = total + diffs[plus]
            elif factor == -1:
                total = total - diffs[plus]
        momentum.append(total)
    return add_all(sums), momentum


def collide(field):
    density, momentum = moments(field)
    inverse = 1.0 / density
    square = momentum[0] * momentum[0] + momentum[1] * momentum[1] + momentum[2] * momentum[2]
    even = density - 1.5 * (square * inverse)
    keep = 1.0 - relaxation
    result = [keep * field[0] + (relaxation / 3.0) * even] + [None] * (COUNT - 1)
    parts = {}
    for divisor in (18.0, 36.0):
        parts[divisor] = ((relaxation / divisor) * even, (relaxation * 4.5 / divisor) * inverse)
    for plus, minus in PAIRS:
        project = None
        for axis in range(3):
            factor = lattice_velocities[plus][axis]
            if factor:
                if project is None:
                    project = momentum[axis]
                elif factor == 1:
                    project = project + momentum[axis]
                else:
                    project = project - momentum[axis]
        divisor = 18.0 if plus < 7 else 36.0
        base, curve = parts[divisor]
        symmetric = base + curve * (project * project)
        odd = (3.0 * relaxation / divisor) * project
        result[plus] = keep * field[plus] + (symmetric + odd)
        result[minus] = keep * field[minus] + (symmetric - odd)
    return result


def weight_of(number):
    return 1.0 / (18.0 if number < 7 else 36.0)


def encode(value, unit):
    steps = jnp.round(value * (STEP / unit) - STEP)
    return jnp.clip(steps, -2.0 * STEP, 2.0 * STEP - 1.0).astype(jnp.int32).astype(jnp.int16)


def decode(code, unit):
    return code.astype(jnp.int32).astype(jnp.float32) * (unit / STEP) + unit


def kernel(
    sizes,
    f_hbm,
    par_hbm,
    direct_hbm,
    F,
    vort,
    img,
    A,
    B,
    E,
    SY,
    EI,
    RY,
    SQ,
    RQ,
    SC,
    RC,
    U,
    PYS,
    PYR,
    PXS,
    PXR,
    CS,
    CR,
    L,
    G,
    par,
    direct,
    PC,
    PA,
    PS,
    PR,
    first_s,
    second_s,
    halo_r,
    part_r,
    pa_r,
    pr_r,
):
    nd, ni, X, W, NZ, bumps = sizes
    d = lax.axis_index("depth")
    i = lax.axis_index("image")
    halves = W // ROWS
    ratio = ni // nd
    chunks = 8
    step_x = X // chunks

    loads = [
        pltpu.make_async_copy(
            f_hbm.at[:, pl.ds(c * step_x, step_x)],
            F.at[:, pl.ds(c * step_x, step_x)],
            first_s.at[c],
        )
        for c in range(chunks)
    ]
    for copy in loads[:AHEAD]:
        copy.start()
    scalars = [
        pltpu.make_async_copy(par_hbm, par, second_s.at[0]),
        pltpu.make_async_copy(direct_hbm, direct, second_s.at[1]),
    ]
    for copy in scalars:
        copy.start()

    barrier = pltpu.get_barrier_semaphore()
    everyone = nd * ni
    me = d * ni + i

    def greet(offset, carry):
        other = lax.rem(me + offset, everyone)
        pl.semaphore_signal(
            barrier,
            inc=1,
            device_id={"depth": other // ni, "image": lax.rem(other, ni)},
            device_id_type=MESH,
        )
        return carry

    lax.fori_loop(1, everyone, greet, 0)

    def to(cx, cy):
        return {"depth": lax.rem(d + cx + nd, nd), "image": lax.rem(i + cy + ni, ni)}

    def remote(src, dst, send, recv, target):
        return pltpu.make_async_remote_copy(
            src_ref=src,
            dst_ref=dst,
            send_sem=send,
            recv_sem=recv,
            device_id=target,
            device_id_type=MESH,
        )

    starts = list(range(1, W - 1 - ROWS, ROWS)) + [W - 1 - ROWS]
    edge_rows = (0, W - 1)
    outward = (DOWN_Y, UP_Y)
    inward = (UP_Y, DOWN_Y)

    def pack(b, x, start, values):
        if start == 1:
            for number in DOWN_Y:
                E[b, 0, SLOT[number], pl.ds(ROWS + x, 1), :] = values[number][0:1]
        if start == W - 1 - ROWS:
            for number in UP_Y:
                E[b, 1, SLOT[number], pl.ds(ROWS + x, 1), :] = values[number][ROWS - 1 : ROWS]

    def streamed(S, x, start):
        field = []
        for number in range(COUNT):
            cx, cy, cz = lattice_velocities[number]
            value = S[SLOT[number], x + 1 - cx, pl.ds(LOW + start - cy, ROWS), :]
            if cz:
                value = pltpu.roll(value, cz % NZ, 1)
            field.append(value)
        return field

    def edge_streamed(b, side, x):
        field = []
        for number in range(COUNT):
            cx, _, cz = lattice_velocities[number]
            rows = slice(ROWS + x - cx, 2 * ROWS + x - cx)
            if number in inward[side]:
                value = RY[b, side, inward[side].index(number), rows, :]
            else:
                value = E[b, side, SLOT[number], rows, :]
            if cz:
                value = pltpu.roll(value, cz % NZ, 1)
            field.append(value)
        return field

    def update(S, D, b, x):
        for start in starts:
            values = collide(streamed(S, x, start))
            for number in range(COUNT):
                D[SLOT[number], x + 1, pl.ds(LOW + start, ROWS), :] = values[number]
            pack(b, x, start, values)

    def mirrored(number):
        cx, cy, cz = lattice_velocities[number]
        return lattice_velocities.index((cx, -cy, cz))

    def choose(side, low, high):
        return low if low == high else low + side * (high - low)

    def slot_of(side, number):
        return choose(side, SLOT[number], SLOT[mirrored(number)])

    def place_of(side, number):
        lists = (UP_Y, DOWN_Y) if number in UP_Y else (DOWN_Y, UP_Y)
        return choose(side, lists[0].index(number), lists[1].index(mirrored(number)))

    def corner_of(side, number):
        return choose(side, CORNERS.index(number), CORNERS.index(mirrored(number)))

    def edges(old, b, side):
        for x in (0,):
            field = []
            for number in range(COUNT):
                cx, _, cz = lattice_velocities[number]
                rows = slice(ROWS + x - cx, ROWS + x - cx + X)
                if number in UP_Y:
                    value = RY[old, side, place_of(side, number), rows, :]
                else:
                    value = E[old, side, slot_of(side, number), rows, :]
                if cz:
                    value = pltpu.roll(value, cz % NZ, 1)
                field.append(value)
            values = collide(field)
            for number in range(COUNT):
                cy = lattice_velocities[number][1]
                if cy == 1:
                    EI[side, place_of(side, number), x : x + X, :] = values[number]
                elif cy == 0:
                    E[b, side, SLOT[number], ROWS + x : ROWS + x + X, :] = values[number]
                else:
                    SY[side, place_of(side, number), ROWS + x : ROWS + x + X, :] = values[number]

    inner = pl.ds(LOW, W)

    def collect(terms, axes):
        groups = {}
        for number, value in terms:
            velocity = lattice_velocities[number]
            sums = groups.setdefault(velocity[2], [None] * 3)
            for place, factor in enumerate([1] + [velocity[axis] for axis in axes]):
                if factor:
                    value_now = value if factor == 1 else -value
                    sums[place] = value_now if sums[place] is None else sums[place] + value_now
        totals = [None] * 3
        for cz, sums in groups.items():
            turned = [v if v is None or cz == 0 else pltpu.roll(v, cz % NZ, 1) for v in sums]
            if 2 in axes:
                turned[1 + axes.index(2)] = None if cz == 0 else cz * turned[0]
            for place in range(3):
                if turned[place] is not None:
                    old = totals[place]
                    totals[place] = turned[place] if old is None else old + turned[place]
        return totals

    def planes_of(side, number):
        edge, inside = ((0, 1), (X - 1, X - 2))[side]
        cx = lattice_velocities[number][0]
        if cx == 0:
            return edge
        return inside if cx == 2 * side - 1 else None

    def fill_rows(D, b):
        zero = jnp.zeros((1, NZ), jnp.float32)
        for side in range(2):
            for number in range(COUNT):
                plane = planes_of(side, number)
                if plane is None:
                    continue
                cy = lattice_velocities[number][1]
                if cy:
                    row = LOW - 1 if cy == 1 else LOW + W
                    D[SLOT[number], plane + 1, row : row + 1, :] = zero
                    continue
                for y, row in enumerate(edge_rows):
                    value = E[b, y, SLOT[number], ROWS + plane : ROWS + plane + 1, :]
                    D[SLOT[number], plane + 1, LOW + row : LOW + row + 1, :] = value

    def send_parts(D, b):
        line = lax.broadcasted_iota(jnp.int32, (CODED, NZ), 0)
        for k, corner in enumerate(CORNERS):
            cx, cy, _ = lattice_velocities[corner]
            side = 1 if cy == 1 else 0
            edge = ROWS + (X - 1 if cx == 1 else 0)
            for place, cz in enumerate((0, 1, -1)):
                number = lattice_velocities.index((cx, 0, cz))
                upper = E[b, side, SLOT[number], edge : edge + 1, :]
                number = outward[side].index(lattice_velocities.index((0, cy, cz)))
                lower = SY[side, number, edge : edge + 1, :]
                if cz == 0:
                    upper = upper + E[b, side, SLOT[corner], edge : edge + 1, :]
                    deeper = edge - cx
                    lower = lower + SY[side, outward[side].index(corner), deeper : deeper + 1, :]
                CS[k, 2 * place : 2 * place + 1, :] = upper
                CS[k, 2 * place + 1 : 2 * place + 2, :] = lower
        for side in range(2):
            for x in range(0, X, CODED):
                terms = []
                for number in range(COUNT):
                    if number in inward[side]:
                        continue
                    cx = lattice_velocities[number][0]
                    start = ROWS + x - cx
                    value = E[b, side, SLOT[number], start : start + CODED, :]
                    if cx == 1 and x == 0:
                        value = jnp.where(line == 0, 0.0, value)
                    if cx == -1 and x == X - CODED:
                        value = jnp.where(line == CODED - 1, 0.0, value)
                    terms.append((number, value))
                for place, value in enumerate(collect(terms, (2, 0))):
                    unit, centre = PART_UNITS[place]
                    steps = jnp.clip(jnp.round((value - centre) * unit), -32768.0, 32767.0)
                    code = steps.astype(jnp.int32).astype(jnp.int16)
                    PYS[side, place, x : x + CODED, :] = code
        for side in range(2):
            for h in range(halves):
                terms = []
                for number in range(COUNT):
                    plane = planes_of(side, number)
                    if plane is None:
                        continue
                    rows = pl.ds(LOW + ROWS * h - lattice_velocities[number][1], ROWS)
                    terms.append((number, D[SLOT[number], plane + 1, rows, :]))
                for place, value in enumerate(collect(terms, (1, 2))):
                    PXS[side, place, ROWS * h : ROWS * h + ROWS, :] = value
        parts = []
        for k, corner in enumerate(CORNERS):
            cx, cy, _ = lattice_velocities[corner]
            parts.append(remote(CS.at[k], CR.at[k], second_s.at[k], part_r.at[k], to(cx, cy)))
        for side in (far, near):
            step = {"depth": d, "image": lax.rem(i + 2 * side - 1 + ni, ni)}
            parts.append(
                remote(
                    PYS.at[side], PYR.at[1 - side], second_s.at[4 + side], part_r.at[5 - side], step
                )
            )
        for side in range(2):
            parts.append(
                remote(
                    PXS.at[side],
                    PXR.at[1 - side],
                    second_s.at[6 + side],
                    part_r.at[7 - side],
                    to(2 * side - 1, 0),
                )
            )
        for part in parts:
            part.start()
        return parts

    def ghosts(D, slot):
        line = lax.broadcasted_iota(jnp.int32, (ROWS, NZ), 0)
        meet = {}
        for k, corner in enumerate(CORNERS):
            after = pltpu.roll(CR[k], 1, 1)
            before = pltpu.roll(CR[k], NZ - 1, 1)
            plain = CR[k]
            for y in range(2):
                up, down = after[2 + y : 3 + y], before[4 + y : 5 + y]
                meet[lattice_velocities[corner][:2], y] = (plain[y : y + 1] + up + down, up - down)
        for y in range(2):
            for number in outward[y]:
                cx = lattice_velocities[number][0]
                if cx:
                    place, plane = (ROWS - 1, 0) if cx == 1 else (ROWS + X, X + 1)
                    row = LOW + edge_rows[y]
                    SY[y, outward[y].index(number), place : place + 1, :] = D[
                        SLOT[number], plane, row : row + 1, :
                    ]
        for k, corner in enumerate(CORNERS):
            cx, cy, _ = lattice_velocities[corner]
            y = 0 if cy == 1 else 1
            plane, place = (X, ROWS + X - 1) if cx == 1 else (1, ROWS)
            row = LOW - 1 if cy == 1 else LOW + W
            D[SLOT[corner], plane, row : row + 1, :] = RY[
                slot, y, inward[y].index(corner), place : place + 1, :
            ]
        for side in range(2):
            from_x = 1 - 2 * side
            plane = X if side else 1
            for h in range(halves):
                terms = []
                for number in range(COUNT):
                    if lattice_velocities[number][0] == -from_x:
                        rows = pl.ds(LOW + ROWS * h - lattice_velocities[number][1], ROWS)
                        terms.append((number, D[SLOT[number], plane, rows, :]))
                sums = collect(terms, (1, 2))
                for place in range(3):
                    sums[place] = sums[place] + PXR[side, place, ROWS * h : ROWS * h + ROWS, :]
                for at, from_y, wanted in ((0, 1, 0), (ROWS - 1, -1, halves - 1)):
                    if h == wanted:
                        mass, along_z = meet[(from_x, from_y), 1]
                        for place, more in enumerate((mass, from_y * mass, along_z)):
                            sums[place] = jnp.where(line == at, sums[place] + more, sums[place])
                inverse = 1.0 / sums[0]
                for place in range(2):
                    U[place, (X + 1) * side, pl.ds(LOW + ROWS * h, ROWS), :] = (
                        sums[1 + place] * inverse
                    )
        for side in range(2):
            from_y = 1 - 2 * side
            row = LOW + W if side else LOW - 1
            for x in range(0, X, ROWS):
                terms = []
                for j, number in enumerate(outward[side]):
                    start = ROWS + x - lattice_velocities[number][0]
                    terms.append((number, SY[side, j, start : start + ROWS, :]))
                sums = collect(terms, (2, 0))
                for place in range(3):
                    unit, centre = PART_UNITS[place]
                    code = PYR[side, place, x // CODED * CODED : x // CODED * CODED + CODED, :]
                    value = code.astype(jnp.int32).astype(jnp.float32) * (1.0 / unit) + centre
                    sums[place] = sums[place] + value[x % CODED : x % CODED + ROWS]
                for at, from_x, wanted in ((0, 1, 0), (ROWS - 1, -1, X - ROWS)):
                    if x == wanted:
                        mass, along_z = meet[(from_x, from_y), 0]
                        for place, more in enumerate((mass, along_z, from_x * mass)):
                            sums[place] = jnp.where(line == at, sums[place] + more, sums[place])
                inverse = 1.0 / sums[0]
                for place in range(2):
                    value = sums[1 + place] * inverse
                    for r in range(ROWS):
                        U[1 + place, x + r + 1, row : row + 1, :] = value[r : r + 1]

    def across(cx, side):
        return {
            "depth": lax.rem(d + cx + nd, nd),
            "image": lax.rem(i + 2 * side - 1 + ni, ni),
        }

    def messages(turn, side):
        slot = turn % 2
        found = [
            remote(
                SQ.at[side],
                RQ.at[slot, 1 - side],
                first_s.at[side],
                halo_r.at[slot, 1 - side],
                across(0, side),
            )
        ]
        for number in CORNERS:
            cx, cy, _ = lattice_velocities[number]
            if cy == -1:
                k = corner_of(side, number)
                found.append(
                    remote(
                        SC.at[k],
                        RC.at[slot, k],
                        first_s.at[2 + k],
                        halo_r.at[slot, 2 + k],
                        across(cx, side),
                    )
                )
        return found

    def planes(D, turn):
        pairs = ((0, X, 0, 1), (CROSS, 1, X + 1, -1))
        return [
            remote(
                D.at[pl.ds(start, CROSS), plane, inner],
                D.at[pl.ds(start, CROSS), land, inner],
                first_s.at[6 + k],
                halo_r.at[turn % 2, 6 + k],
                to(cx, 0),
            )
            for k, (start, plane, land, cx) in enumerate(pairs)
        ]

    def send_side(turn, side):
        for number in CORNERS:
            cx, cy, _ = lattice_velocities[number]
            if cy == -1:
                edge = ROWS + (X - 1 if cx == 1 else 0)
                row = SY[side, place_of(side, number), edge : edge + 1, :]
                SC[corner_of(side, number)] = row
        copies = messages(turn, side)
        for copy in copies[1:]:
            copy.start()
        for number in DOWN_Y:
            j = place_of(side, number)
            for x in range(0, X, CODED):
                value = SY[side, j, ROWS + x : ROWS + x + CODED, :]
                SQ[side, j, x : x + CODED, :] = encode(value, weight_of(number))
        copies[0].start()

    def receive_side(D, turn, side):
        slot = turn % 2
        for copy in messages(turn, side):
            copy.wait_send()
        for copy in messages(turn, 1 - side):
            copy.wait_recv()
        for number in UP_Y:
            j = place_of(side, number)
            for x in range(0, X, CODED):
                value = decode(RQ[slot, side, j, x : x + CODED, :], weight_of(number))
                RY[slot, side, j, ROWS + x : ROWS + x + CODED, :] = value
        for number in range(COUNT):
            cx, cy, _ = lattice_velocities[number]
            if cx == 0:
                continue
            plane, place = (0, ROWS - 1) if cx == 1 else (X + 1, ROWS + X)
            if cy == 1:
                j = place_of(side, number)
                RY[slot, side, j, place : place + 1, :] = RC[slot, corner_of(side, number)]
            else:
                row = LOW - cy + side * (W - 1 + 2 * cy)
                k = slot_of(side, number)
                E[slot, side, k, place : place + 1, :] = D[k, plane, pl.ds(row, 1), :]

    def inward_rows(D, x):
        for side in range(2):
            row = LOW + edge_rows[side]
            for j, number in enumerate(inward[side]):
                D[SLOT[number], x + 1, row : row + 1, :] = EI[side, j, pl.ds(x, 1), :]

    def corner_rows(D, b):
        for x, wanted in ((0, -1), (X - 1, 1)):
            inward_rows(D, x)
            for side in range(2):
                row = LOW + edge_rows[side]
                for number in range(COUNT):
                    cx, cy, _ = lattice_velocities[number]
                    if cx != wanted or number in inward[side]:
                        continue
                    at = slice(ROWS + x, ROWS + x + 1)
                    if cy:
                        value = SY[side, outward[side].index(number), at, :]
                    else:
                        value = E[b, side, SLOT[number], at, :]
                    D[SLOT[number], x + 1, row : row + 1, :] = value

    far = lax.rem(i, 2)
    near = 1 - far
    span = max(1, ni // 2)
    inside = (lax.rem(i + 1, ni) // 2 + span - 1) // span
    lead = far + inside * (near - far)
    follow = 1 - lead

    def first(x, carry):
        for h in range(halves):
            field = [F[number, x, pl.ds(ROWS * h, ROWS), :] for number in range(COUNT)]
            values = collide(field)
            for number in range(COUNT):
                A[SLOT[number], x + 1, pl.ds(LOW + ROWS * h, ROWS), :] = values[number]
            for side, edge in ((0, 0), (1, ROWS - 1)):
                if h != (0 if side == 0 else halves - 1):
                    continue
                near = 1 if side == 0 else ROWS - 2
                for number in range(COUNT):
                    if lattice_velocities[number][1] == 0:
                        E[0, side, SLOT[number], pl.ds(ROWS + x, 1), :] = values[number][
                            edge : edge + 1
                        ]
                for j, number in enumerate(outward[side]):
                    SY[side, j, pl.ds(ROWS + x, 1), :] = values[number][edge : edge + 1]
                    E[0, side, SLOT[number], pl.ds(ROWS + x, 1), :] = values[number][
                        near : near + 1
                    ]
        return carry

    for c in range(chunks):
        loads[c].wait()
        if c + AHEAD < chunks:
            loads[c + AHEAD].start()
        lax.fori_loop(c * step_x, (c + 1) * step_x, first, 0)

    for copy in scalars:
        copy.wait()
    ray = X * nd
    lane = lax.broadcasted_iota(jnp.int32, (8, NZ), 1)
    entries = jnp.full((8, NZ), direct[0].astype(jnp.float32), jnp.float32)
    for k in range(bumps):
        for kind in range(5):
            factor = SCALE if kind == 0 else (LOG2E / ray if kind == 1 else 1.0)
            entries = jnp.where(lane == kind * bumps + k, par[kind, 0, k] * factor, entries)
    gain = pltpu.roll(entries, bumps, 1)
    shift = gain * gain - jnp.log2(entries)
    ratios = entries / gain
    for kind in (3, 4):
        ratios = jnp.where(
            lane < kind * bumps, ratios, entries / pltpu.roll(entries, (kind - 1) * bumps, 1)
        )
    table = jnp.where(lane < 2 * bumps, shift, ratios)
    table = jnp.where(lane < bumps, 2.0 * entries, table)
    PC[i] = jnp.where(lane < 5 * bumps, table, entries)[0:1]

    pl.semaphore_wait(barrier, everyone - 1)
    shares = [
        remote(PC.at[i], PC.at[i], second_s.at[o], pa_r.at[o], to(0, o)) for o in range(1, ni)
    ]
    for side in (far, near):
        send_side(0, side)
    for copy in planes(A, 0) + shares:
        copy.start()

    source, target = A, B
    for turn in range(1, STEPS):

        def middle(x, carry, source=source, target=target, turn=turn):
            update(source, target, turn % 2, x)
            return carry

        lax.fori_loop(1, X - 1, middle, 0, unroll=2)
        for copy in planes(source, turn - 1):
            copy.wait()
        for side in (lead, follow):
            receive_side(source, turn - 1, side)
            edges((turn - 1) % 2, turn % 2, side)
            send_side(turn, side)
        for x in (0, X - 1):
            middle(x, 0)
        corner_rows(target, turn % 2)
        if turn == STEPS - 1:
            fill_rows(target, turn % 2)
        for copy in planes(target, turn):
            copy.start()
        if turn == STEPS - 1:
            for x in (1, X - 2):
                inward_rows(target, x)
            for copy in shares:
                copy.wait()
            parts = send_parts(target, turn % 2)

        def settle(x, carry, target=target):
            inward_rows(target, x)
            return carry

        lax.fori_loop(1, X - 1, settle, 0)
        source, target = target, source

    def flow_of(field):
        density, momentum = moments(field)
        inverse = 1.0 / density
        return [momentum[axis] * inverse for axis in (1, 2, 0)]

    def last(x, carry):
        for start in starts:
            field = streamed(source, x, start)
            for number in range(COUNT):
                F[number, x, pl.ds(start, ROWS), :] = field[number]
            for place, value in enumerate(flow_of(field)):
                U[place, x + 1, pl.ds(LOW + start, ROWS), :] = value
        return carry

    def expand(m, carry):
        for block in range(PA.shape[1] // 8):
            line = lax.broadcasted_iota(jnp.int32, (8, NZ), 0) + 8 * block
            chosen = jnp.where(lane == line, jnp.broadcast_to(PC[m], (8, NZ)), 0.0)
            value = jnp.sum(chosen, axis=1, keepdims=True)
            PA[m, pl.ds(8 * block, 8), :] = jnp.broadcast_to(value, (8, NZ))
        return carry

    lax.fori_loop(0, ni, expand, 0, unroll=2)
    lax.fori_loop(1, X - 1, last, 0)
    for copy in planes(source, STEPS - 1):
        copy.wait()
    for x in (0, X - 1):
        last(x, 0)
    for side in (lead, follow):
        receive_side(source, STEPS - 1, side)
    for part in parts:
        part.wait()
    for side in range(2):
        row = edge_rows[side]
        for x in range(0, X, ROWS):
            field = edge_streamed((STEPS - 1) % 2, side, x)
            for place, value in enumerate(flow_of(field)):
                for r in range(ROWS):
                    U[place, x + r + 1, LOW + row : LOW + row + 1, :] = value[r : r + 1]
    ghosts(source, (STEPS - 1) % 2)

    def spin(x, carry):
        def across_x(place):
            return (U[place, x + 2, inner, :] - U[place, x, inner, :]) * 0.5

        def across_y(place):
            above = U[place, x + 1, pl.ds(LOW + 1, W), :]
            return (above - U[place, x + 1, pl.ds(LOW - 1, W), :]) * 0.5

        def across_z(place):
            value = U[place, x + 1, inner, :]
            return (pltpu.roll(value, NZ - 1, 1) - pltpu.roll(value, 1, 1)) * 0.5

        spin_x = across_y(1) - across_z(0)
        spin_y = across_z(2) - across_x(1)
        spin_z = across_x(0) - across_y(2)
        size = jnp.sqrt(spin_x * spin_x + spin_y * spin_y + spin_z * spin_z)
        rounded = size.astype(jnp.bfloat16)
        vort[x] = rounded
        value = rounded.astype(jnp.float32)
        level = (value / (value + level_offset)) * SCALE
        L[x] = level
        G[x] = jnp.exp2(-(level * level))
        return carry

    lax.fori_loop(0, X, spin, 0, unroll=8)

    owner = i // ratio
    mine = d * ratio + lax.rem(i, ratio)

    def row(m, r):
        return jnp.broadcast_to(PA[m, pl.ds(r, 1), :], (ROWS, NZ))

    def blend(backward, through, colors, local_through, local_colors):
        fade = jnp.where(backward, local_through, 1.0)
        lit = jnp.where(backward, 1.0, through)
        mixed = [color * fade + lit * local for color, local in zip(colors, local_colors)]
        return through * local_through, mixed

    def piece(o, m):
        return remote(
            PS.at[m],
            PR.at[mine],
            first_s.at[o],
            pr_r.at[mine],
            {"depth": owner, "image": m},
        )

    def render(o, carry):
        m = lax.rem(i + 1 + o, ni)
        backward = row(m, 5 * bumps) > 0.5
        sign = jnp.where(backward, 1.0, -1.0)

        def along(x, state):
            new = []
            levels = [L[x, pl.ds(ROWS * h, ROWS), :] for h in range(halves)]
            totals = [[None] * 4 for h in range(halves)]
            for k in range(bumps):
                centre = row(m, k)
                shift = row(m, bumps + k)
                gains = [row(m, (1 + j) * bumps + k) for j in range(1, 4)]
                for h in range(halves):
                    bump = jnp.exp2(levels[h] * centre - shift)
                    for j in range(4):
                        term = gains[j - 1] * bump if j else bump
                        totals[h][j] = term if k == 0 else totals[h][j] + term
            for h in range(halves):
                signed, seen, *colors = state[5 * h : 5 * h + 5]
                common = G[x, pl.ds(ROWS * h, ROWS), :]
                signed = signed + totals[h][0] * (common * sign)
                now = jnp.exp2(signed)
                weight = (seen - now) * common
                colors = [color + weight * total for color, total in zip(colors, totals[h][1:])]
                new += [signed, now, *colors]
            return tuple(new)

        zero = jnp.zeros((ROWS, NZ), jnp.float32)
        start = (zero, jnp.ones((ROWS, NZ), jnp.float32), zero, zero, zero) * halves
        state = lax.fori_loop(0, X, along, start, unroll=8)
        parts = []
        for h in range(halves):
            signed, seen, *colors = state[5 * h : 5 * h + 5]
            through = jnp.where(backward, jnp.exp2(-signed), seen)
            factor = jnp.where(backward, -through, 1.0)
            parts.append([color * factor for color in colors] + [through])
        for j in range(4):
            value = jnp.concatenate([part[j] for part in parts], axis=0)
            unit = PIECE / (bumps if j < 3 else 1.0)
            steps = jnp.clip(jnp.round(value * unit - 32768.0), -32768.0, 32767.0)
            PS[m, j] = steps.astype(jnp.int32).astype(jnp.int16)
        local_target = jnp.logical_and(owner == d, m == i)

        @pl.when(local_target)
        def _():
            PR[mine] = PS[m]

        @pl.when(jnp.logical_not(local_target))
        def _():
            piece(o, m).start()

        return carry

    lax.fori_loop(0, ni, render, 0)
    for side in range(2):
        edge = edge_rows[side]
        for x in range(0, X, ROWS):
            field = edge_streamed((STEPS - 1) % 2, side, x)
            for number in range(COUNT):
                for r in range(ROWS):
                    F[number, x + r, edge : edge + 1, :] = field[number][r : r + 1]

    def sent(o, carry):
        m = lax.rem(i + 1 + o, ni)

        @pl.when(jnp.logical_not(jnp.logical_and(owner == d, m == i)))
        def _():
            piece(o, m).wait_send()

        return carry

    def arrived(slot, carry):
        @pl.when(jnp.logical_not(jnp.logical_and(owner == d, slot == mine)))
        def _():
            remote(
                PS.at[0], PR.at[slot], first_s.at[0], pr_r.at[slot], {"depth": d, "image": i}
            ).wait_recv()

        return carry

    lax.fori_loop(0, nd * ratio, arrived, 0)
    backward = jnp.broadcast_to(PA[i, pl.ds(5 * bumps, 1), :], (W, NZ)) > 0.5
    for part in range(ratio):
        through = jnp.ones((W, NZ), jnp.float32)
        colors = [jnp.zeros((W, NZ), jnp.float32)] * 3
        for slab in range(nd):
            local = []
            for j in range(4):
                unit = (bumps if j < 3 else 1.0) / PIECE
                code = PR[slab * ratio + part, j].astype(jnp.int32).astype(jnp.float32)
                local.append(code * unit + 32768.0 * unit)
            through, colors = blend(backward, through, colors, local[3], local[:3])
        for j, value in enumerate(colors + [1.0 - through]):
            img[0, j, part * W : (part + 1) * W, :] = value
    lax.fori_loop(0, ni, sent, 0)


def put_out(pieces, F, vort, img, F_out, vort_out, img_out, sems):
    step = F.shape[1] // pieces
    copies = [
        pltpu.make_async_copy(
            F.at[:, pl.ds(c * step, step)], F_out.at[:, pl.ds(c * step, step)], sems.at[c]
        )
        for c in range(pieces)
    ]
    copies.append(pltpu.make_async_copy(vort, vort_out, sems.at[pieces]))
    copies.append(pltpu.make_async_copy(img, img_out, sems.at[pieces + 1]))
    for copy in copies:
        copy.start()
    for copy in copies:
        copy.wait()


def on_device(populations, transfer, direction):
    nd, ni = lax.axis_size("depth"), lax.axis_size("image")
    count, X, W, NZ = populations.shape
    bumps = transfer.shape[2]
    assert transfer.shape[0] == 1 and ni % nd == 0 and W % ROWS == 0 and W >= 2 * ROWS and X % CODED == 0
    sizes = (nd, ni, X, W, NZ, bumps)
    ratio = ni // nd
    padded = W + 2 * ROWS
    f32 = jnp.float32
    table = -(-(5 * bumps + 1) // 8) * 8
    dma = pltpu.SemaphoreType.DMA
    results = pl.pallas_call(
        functools.partial(kernel, sizes),
        out_shape=(
            pltpu.VMEM(populations.shape, f32),
            pltpu.VMEM((X, W, NZ), jnp.bfloat16),
            pltpu.VMEM((1, 4, ratio * W, NZ), f32),
        ),
        in_specs=[
            pl.BlockSpec(memory_space=pl.ANY),
            pl.BlockSpec(memory_space=pl.ANY),
            pl.BlockSpec(memory_space=pl.ANY),
        ],
        out_specs=(
            pl.BlockSpec(memory_space=pltpu.VMEM),
            pl.BlockSpec(memory_space=pltpu.VMEM),
            pl.BlockSpec(memory_space=pltpu.VMEM),
        ),
        scratch_shapes=[
            pltpu.VMEM((COUNT, X + 2, padded, NZ), f32),
            pltpu.VMEM((COUNT, X + 2, padded, NZ), f32),
            pltpu.VMEM((2, 2, COUNT, X + 2 * ROWS, NZ), f32),
            pltpu.VMEM((2, CROSS, X + 2 * ROWS, NZ), f32),
            pltpu.VMEM((2, CROSS, X, NZ), f32),
            pltpu.VMEM((2, 2, CROSS, X + 2 * ROWS, NZ), f32),
            pltpu.VMEM((2, CROSS, X, NZ), jnp.int16),
            pltpu.VMEM((2, 2, CROSS, X, NZ), jnp.int16),
            pltpu.VMEM((4, 1, NZ), f32),
            pltpu.VMEM((2, 4, 1, NZ), f32),
            pltpu.VMEM((3, X + 2, padded, NZ), f32),
            pltpu.VMEM((2, 3, X, NZ), jnp.int16),
            pltpu.VMEM((2, 3, X, NZ), jnp.int16),
            pltpu.VMEM((2, 3, W, NZ), f32),
            pltpu.VMEM((2, 3, W, NZ), f32),
            pltpu.VMEM((4, 8, NZ), f32),
            pltpu.VMEM((4, 8, NZ), f32),
            pltpu.VMEM((X, W, NZ), f32),
            pltpu.VMEM((X, W, NZ), f32),
            pltpu.SMEM((5, 1, bumps), f32),
            pltpu.SMEM((1,), jnp.int32),
            pltpu.VMEM((ni, 1, NZ), f32),
            pltpu.VMEM((ni, table, NZ), f32),
            pltpu.VMEM((ni, 4, W, NZ), jnp.int16),
            pltpu.VMEM((nd * ratio, 4, W, NZ), jnp.int16),
            dma((max(8, ni),)),
            dma((max(8, ni),)),
            dma((2, 8)),
            dma((8,)),
            dma((ni,)),
            dma((nd * ratio,)),
        ],
        compiler_params=pltpu.CompilerParams(
            collective_id=0, has_side_effects=True, vmem_limit_bytes=56 << 20
        ),
    )(populations, transfer.transpose(1, 0, 2), direction)
    pieces = 8
    return pl.pallas_call(
        functools.partial(put_out, pieces),
        out_shape=tuple(jax.ShapeDtypeStruct(r.shape, r.dtype) for r in results),
        in_specs=[pl.BlockSpec(memory_space=pltpu.VMEM)] * 3,
        out_specs=(pl.BlockSpec(memory_space=pl.ANY),) * 3,
        scratch_shapes=[dma((pieces + 2,))],
        compiler_params=pltpu.CompilerParams(vmem_limit_bytes=1 << 20),
    )(*results)


def solution(mesh):
    in_specs = (P(None, "depth", "image", None), P("image", None, None), P("image"))
    out_specs = (
        P(None, "depth", "image", None),
        P("depth", "image", None),
        P("image", None, "depth", None),
    )
    return jax.shard_map(
        on_device, mesh=mesh, in_specs=in_specs, out_specs=out_specs, check_vma=False
    )
```

```python
import functools
import math

import jax
import jax.numpy as jnp
from jax import lax
from jax.experimental import pallas as pl
from jax.experimental.pallas import tpu as pltpu
from jax.sharding import PartitionSpec as P

STEPS = 4
MESH = pl.DeviceIdType.MESH

lattice_velocities = (
    (0, 0, 0),
    (1, 0, 0),
    (-1, 0, 0),
    (0, 1, 0),
    (0, -1, 0),
    (0, 0, 1),
    (0, 0, -1),
    (1, 1, 0),
    (-1, -1, 0),
    (1, -1, 0),
    (-1, 1, 0),
    (1, 0, 1),
    (-1, 0, -1),
    (1, 0, -1),
    (-1, 0, 1),
    (0, 1, 1),
    (0, -1, -1),
    (0, 1, -1),
    (0, -1, 1),
)
relaxation = 1.25
bump_width = 0.15
level_offset = 0.05
LOG2E = math.log2(math.e)
SCALE = math.sqrt(LOG2E) / bump_width

COUNT = len(lattice_velocities)
ORDER = (
    [n for n in range(COUNT) if lattice_velocities[n][0] == 1]
    + [n for n in range(COUNT) if lattice_velocities[n][0] == -1]
    + [n for n in range(COUNT) if lattice_velocities[n][0] == 0]
)
SLOT = {number: place for place, number in enumerate(ORDER)}
UP_Y = [n for n in range(COUNT) if lattice_velocities[n][1] == 1]
DOWN_Y = [n for n in range(COUNT) if lattice_velocities[n][1] == -1]
CROSS = len(UP_Y)
CORNERS = [n for n in range(COUNT) if lattice_velocities[n][0] and lattice_velocities[n][1]]
PAIRS = [(n, n + 1) for n in range(1, COUNT, 2)]
LOW = 8
ROWS = 8
CODED = 16
STEP = 16384.0
AHEAD = 5
PIECE = 65535.0
PART_UNITS = ((32768.0, 5.0 / 6.0), (65536.0, 0.0), (65536.0, 0.0))


def add_all(values):
    while len(values) > 1:
        paired = [a + b for a, b in zip(values[0::2], values[1::2])]
        values = paired + ([values[-1]] if len(values) % 2 else [])
    return values[0]


def moments(field):
    diffs = {}
    sums = [field[0]]
    for plus, minus in PAIRS:
        sums.append(field[plus] + field[minus])
        diffs[plus] = field[plus] - field[minus]
    momentum = []
    for axis in range(3):
        total = diffs[1 + 2 * axis]
        for plus, _ in PAIRS[3:]:
            factor = lattice_velocities[plus][axis]
            if factor == 1:
                total = total + diffs[plus]
            elif factor == -1:
                total = total - diffs[plus]
        momentum.append(total)
    return add_all(sums), momentum


def collide(field):
    density, momentum = moments(field)
    inverse = 1.0 / density
    square = momentum[0] * momentum[0] + momentum[1] * momentum[1] + momentum[2] * momentum[2]
    even = density - 1.5 * (square * inverse)
    keep = 1.0 - relaxation
    result = [keep * field[0] + (relaxation / 3.0) * even] + [None] * (COUNT - 1)
    parts = {}
    for divisor in (18.0, 36.0):
        parts[divisor] = ((relaxation / divisor) * even, (relaxation * 4.5 / divisor) * inverse)
    for plus, minus in PAIRS:
        project = None
        for axis in range(3):
            factor = lattice_velocities[plus][axis]
            if factor:
                if project is None:
                    project = momentum[axis]
                elif factor == 1:
                    project = project + momentum[axis]
                else:
                    project = project - momentum[axis]
        divisor = 18.0 if plus < 7 else 36.0
        base, curve = parts[divisor]
        symmetric = base + curve * (project * project)
        odd = (3.0 * relaxation / divisor) * project
        result[plus] = keep * field[plus] + (symmetric + odd)
        result[minus] = keep * field[minus] + (symmetric - odd)
    return result


def weight_of(number):
    return 1.0 / (18.0 if number < 7 else 36.0)


def encode(value, unit):
    steps = jnp.round(value * (STEP / unit) - STEP)
    return jnp.clip(steps, -2.0 * STEP, 2.0 * STEP - 1.0).astype(jnp.int32).astype(jnp.int16)


def decode(code, unit):
    return code.astype(jnp.int32).astype(jnp.float32) * (unit / STEP) + unit


def kernel(
    sizes,
    f_hbm,
    par_hbm,
    direct_hbm,
    F,
    vort,
    img,
    A,
    B,
    E,
    SY,
    EI,
    RY,
    SQ,
    RQ,
    SC,
    RC,
    U,
    PYS,
    PYR,
    PXS,
    PXR,
    CS,
    CR,
    L,
    G,
    par,
    direct,
    PC,
    PA,
    PS,
    PR,
    first_s,
    second_s,
    halo_r,
    part_r,
    pa_r,
    pr_r,
):
    nd, ni, X, W, NZ, bumps = sizes
    d = lax.axis_index("depth")
    i = lax.axis_index("image")
    halves = W // ROWS
    ratio = ni // nd
    chunks = 8
    step_x = X // chunks

    loads = [
        pltpu.make_async_copy(
            f_hbm.at[:, pl.ds(c * step_x, step_x)],
            F.at[:, pl.ds(c * step_x, step_x)],
            first_s.at[c],
        )
        for c in range(chunks)
    ]
    for copy in loads[:AHEAD]:
        copy.start()
    scalars = [
        pltpu.make_async_copy(par_hbm, par, second_s.at[0]),
        pltpu.make_async_copy(direct_hbm, direct, second_s.at[1]),
    ]
    for copy in scalars:
        copy.start()

    barrier = pltpu.get_barrier_semaphore()
    everyone = nd * ni
    me = d * ni + i

    def greet(offset, carry):
        other = lax.rem(me + offset, everyone)
        pl.semaphore_signal(
            barrier,
            inc=1,
            device_id={"depth": other // ni, "image": lax.rem(other, ni)},
            device_id_type=MESH,
        )
        return carry

    lax.fori_loop(1, everyone, greet, 0)

    def to(cx, cy):
        return {"depth": lax.rem(d + cx + nd, nd), "image": lax.rem(i + cy + ni, ni)}

    def remote(src, dst, send, recv, target):
        return pltpu.make_async_remote_copy(
            src_ref=src,
            dst_ref=dst,
            send_sem=send,
            recv_sem=recv,
            device_id=target,
            device_id_type=MESH,
        )

    starts = list(range(1, W - 1 - ROWS, ROWS)) + [W - 1 - ROWS]
    edge_rows = (0, W - 1)
    outward = (DOWN_Y, UP_Y)
    inward = (UP_Y, DOWN_Y)

    def pack(b, x, start, values):
        if start == 1:
            for number in DOWN_Y:
                E[b, 0, SLOT[number], pl.ds(ROWS + x, 1), :] = values[number][0:1]
        if start == W - 1 - ROWS:
            for number in UP_Y:
                E[b, 1, SLOT[number], pl.ds(ROWS + x, 1), :] = values[number][ROWS - 1 : ROWS]

    def streamed(S, x, start):
        field = []
        for number in range(COUNT):
            cx, cy, cz = lattice_velocities[number]
            value = S[SLOT[number], x + 1 - cx, pl.ds(LOW + start - cy, ROWS), :]
            if cz:
                value = pltpu.roll(value, cz % NZ, 1)
            field.append(value)
        return field

    def edge_streamed(b, side, x):
        field = []
        for number in range(COUNT):
            cx, _, cz = lattice_velocities[number]
            rows = slice(ROWS + x - cx, 2 * ROWS + x - cx)
            if number in inward[side]:
                value = RY[b, side, inward[side].index(number), rows, :]
            else:
                value = E[b, side, SLOT[number], rows, :]
            if cz:
                value = pltpu.roll(value, cz % NZ, 1)
            field.append(value)
        return field

    def update(S, D, b, x):
        for start in starts:
            values = collide(streamed(S, x, start))
            for number in range(COUNT):
                D[SLOT[number], x + 1, pl.ds(LOW + start, ROWS), :] = values[number]
            pack(b, x, start, values)

    def mirrored(number):
        cx, cy, cz = lattice_velocities[number]
        return lattice_velocities.index((cx, -cy, cz))

    def choose(side, low, high):
        return low if low == high else low + side * (high - low)

    def slot_of(side, number):
        return choose(side, SLOT[number], SLOT[mirrored(number)])

    def place_of(side, number):
        lists = (UP_Y, DOWN_Y) if number in UP_Y else (DOWN_Y, UP_Y)
        return choose(side, lists[0].index(number), lists[1].index(mirrored(number)))

    def corner_of(side, number):
        return choose(side, CORNERS.index(number), CORNERS.index(mirrored(number)))

    def edges(old, b, side):
        for x in (0,):
            field = []
            for number in range(COUNT):
                cx, _, cz = lattice_velocities[number]
                rows = slice(ROWS + x - cx, ROWS + x - cx + X)
                if number in UP_Y:
                    value = RY[old, side, place_of(side, number), rows, :]
                else:
                    value = E[old, side, slot_of(side, number), rows, :]
                if cz:
                    value = pltpu.roll(value, cz % NZ, 1)
                field.append(value)
            values = collide(field)
            for number in range(COUNT):
                cy = lattice_velocities[number][1]
                if cy == 1:
                    EI[side, place_of(side, number), x : x + X, :] = values[number]
                elif cy == 0:
                    E[b, side, SLOT[number], ROWS + x : ROWS + x + X, :] = values[number]
                else:
                    SY[side, place_of(side, number), ROWS + x : ROWS + x + X, :] = values[number]

    inner = pl.ds(LOW, W)

    def collect(terms, axes):
        groups = {}
        for number, value in terms:
            velocity = lattice_velocities[number]
            sums = groups.setdefault(velocity[2], [None] * 3)
            for place, factor in enumerate([1] + [velocity[axis] for axis in axes]):
                if factor:
                    value_now = value if factor == 1 else -value
                    sums[place] = value_now if sums[place] is None else sums[place] + value_now
        totals = [None] * 3
        for cz, sums in groups.items():
            turned = [v if v is None or cz == 0 else pltpu.roll(v, cz % NZ, 1) for v in sums]
            if 2 in axes:
                turned[1 + axes.index(2)] = None if cz == 0 else cz * turned[0]
            for place in range(3):
                if turned[place] is not None:
                    old = totals[place]
                    totals[place] = turned[place] if old is None else old + turned[place]
        return totals

    def planes_of(side, number):
        edge, inside = ((0, 1), (X - 1, X - 2))[side]
        cx = lattice_velocities[number][0]
        if cx == 0:
            return edge
        return inside if cx == 2 * side - 1 else None

    def fill_rows(D, b):
        zero = jnp.zeros((1, NZ), jnp.float32)
        for side in range(2):
            for number in range(COUNT):
                plane = planes_of(side, number)
                if plane is None:
                    continue
                cy = lattice_velocities[number][1]
                if cy:
                    row = LOW - 1 if cy == 1 else LOW + W
                    D[SLOT[number], plane + 1, row : row + 1, :] = zero
                    continue
                for y, row in enumerate(edge_rows):
                    value = E[b, y, SLOT[number], ROWS + plane : ROWS + plane + 1, :]
                    D[SLOT[number], plane + 1, LOW + row : LOW + row + 1, :] = value

    def send_parts(D, b):
        line = lax.broadcasted_iota(jnp.int32, (CODED, NZ), 0)
        for k, corner in enumerate(CORNERS):
            cx, cy, _ = lattice_velocities[corner]
            side = 1 if cy == 1 else 0
            edge = ROWS + (X - 1 if cx == 1 else 0)
            for place, cz in enumerate((0, 1, -1)):
                number = lattice_velocities.index((cx, 0, cz))
                upper = E[b, side, SLOT[number], edge : edge + 1, :]
                number = outward[side].index(lattice_velocities.index((0, cy, cz)))
                lower = SY[side, number, edge : edge + 1, :]
                if cz == 0:
                    upper = upper + E[b, side, SLOT[corner], edge : edge + 1, :]
                    deeper = edge - cx
                    lower = lower + SY[side, outward[side].index(corner), deeper : deeper + 1, :]
                CS[k, 2 * place : 2 * place + 1, :] = upper
                CS[k, 2 * place + 1 : 2 * place + 2, :] = lower
        for side in range(2):
            for x in range(0, X, CODED):
                terms = []
                for number in range(COUNT):
                    if number in inward[side]:
                        continue
                    cx = lattice_velocities[number][0]
                    start = ROWS + x - cx
                    value = E[b, side, SLOT[number], start : start + CODED, :]
                    if cx == 1 and x == 0:
                        value = jnp.where(line == 0, 0.0, value)
                    if cx == -1 and x == X - CODED:
                        value = jnp.where(line == CODED - 1, 0.0, value)
                    terms.append((number, value))
                for place, value in enumerate(collect(terms, (2, 0))):
                    unit, centre = PART_UNITS[place]
                    steps = jnp.clip(jnp.round((value - centre) * unit), -32768.0, 32767.0)
                    code = steps.astype(jnp.int32).astype(jnp.int16)
                    PYS[side, place, x : x + CODED, :] = code
        for side in range(2):
            for h in range(halves):
                terms = []
                for number in range(COUNT):
                    plane = planes_of(side, number)
                    if plane is None:
                        continue
                    rows = pl.ds(LOW + ROWS * h - lattice_velocities[number][1], ROWS)
                    terms.append((number, D[SLOT[number], plane + 1, rows, :]))
                for place, value in enumerate(collect(terms, (1, 2))):
                    PXS[side, place, ROWS * h : ROWS * h + ROWS, :] = value
        parts = []
        for k, corner in enumerate(CORNERS):
            cx, cy, _ = lattice_velocities[corner]
            parts.append(remote(CS.at[k], CR.at[k], second_s.at[k], part_r.at[k], to(cx, cy)))
        for side in (far, near):
            step = {"depth": d, "image": lax.rem(i + 2 * side - 1 + ni, ni)}
            parts.append(
                remote(
                    PYS.at[side], PYR.at[1 - side], second_s.at[4 + side], part_r.at[5 - side], step
                )
            )
        for side in range(2):
            parts.append(
                remote(
                    PXS.at[side],
                    PXR.at[1 - side],
                    second_s.at[6 + side],
                    part_r.at[7 - side],
                    to(2 * side - 1, 0),
                )
            )
        for part in parts:
            part.start()
        return parts

    def ghosts(D, slot):
        line = lax.broadcasted_iota(jnp.int32, (ROWS, NZ), 0)
        meet = {}
        for k, corner in enumerate(CORNERS):
            after = pltpu.roll(CR[k], 1, 1)
            before = pltpu.roll(CR[k], NZ - 1, 1)
            plain = CR[k]
            for y in range(2):
                up, down = after[2 + y : 3 + y], before[4 + y : 5 + y]
                meet[lattice_velocities[corner][:2], y] = (plain[y : y + 1] + up + down, up - down)
        for y in range(2):
            for number in outward[y]:
                cx = lattice_velocities[number][0]
                if cx:
                    place, plane = (ROWS - 1, 0) if cx == 1 else (ROWS + X, X + 1)
                    row = LOW + edge_rows[y]
                    SY[y, outward[y].index(number), place : place + 1, :] = D[
                        SLOT[number], plane, row : row + 1, :
                    ]
        for k, corner in enumerate(CORNERS):
            cx, cy, _ = lattice_velocities[corner]
            y = 0 if cy == 1 else 1
            plane, place = (X, ROWS + X - 1) if cx == 1 else (1, ROWS)
            row = LOW - 1 if cy == 1 else LOW + W
            D[SLOT[corner], plane, row : row + 1, :] = RY[
                slot, y, inward[y].index(corner), place : place + 1, :
            ]
        for side in range(2):
            from_x = 1 - 2 * side
            plane = X if side else 1
            for h in range(halves):
                terms = []
                for number in range(COUNT):
                    if lattice_velocities[number][0] == -from_x:
                        rows = pl.ds(LOW + ROWS * h - lattice_velocities[number][1], ROWS)
                        terms.append((number, D[SLOT[number], plane, rows, :]))
                sums = collect(terms, (1, 2))
                for place in range(3):
                    sums[place] = sums[place] + PXR[side, place, ROWS * h : ROWS * h + ROWS, :]
                for at, from_y, wanted in ((0, 1, 0), (ROWS - 1, -1, halves - 1)):
                    if h == wanted:
                        mass, along_z = meet[(from_x, from_y), 1]
                        for place, more in enumerate((mass, from_y * mass, along_z)):
                            sums[place] = jnp.where(line == at, sums[place] + more, sums[place])
                inverse = 1.0 / sums[0]
                for place in range(2):
                    U[place, (X + 1) * side, pl.ds(LOW + ROWS * h, ROWS), :] = (
                        sums[1 + place] * inverse
                    )
        for side in range(2):
            from_y = 1 - 2 * side
            row = LOW + W if side else LOW - 1
            for x in range(0, X, ROWS):
                terms = []
                for j, number in enumerate(outward[side]):
                    start = ROWS + x - lattice_velocities[number][0]
                    terms.append((number, SY[side, j, start : start + ROWS, :]))
                sums = collect(terms, (2, 0))
                for place in range(3):
                    unit, centre = PART_UNITS[place]
                    code = PYR[side, place, x // CODED * CODED : x // CODED * CODED + CODED, :]
                    value = code.astype(jnp.int32).astype(jnp.float32) * (1.0 / unit) + centre
                    sums[place] = sums[place] + value[x % CODED : x % CODED + ROWS]
                for at, from_x, wanted in ((0, 1, 0), (ROWS - 1, -1, X - ROWS)):
                    if x == wanted:
                        mass, along_z = meet[(from_x, from_y), 0]
                        for place, more in enumerate((mass, along_z, from_x * mass)):
                            sums[place] = jnp.where(line == at, sums[place] + more, sums[place])
                inverse = 1.0 / sums[0]
                for place in range(2):
                    value = sums[1 + place] * inverse
                    for r in range(ROWS):
                        U[1 + place, x + r + 1, row : row + 1, :] = value[r : r + 1]

    def across(cx, side):
        return {
            "depth": lax.rem(d + cx + nd, nd),
            "image": lax.rem(i + 2 * side - 1 + ni, ni),
        }

    def messages(turn, side):
        slot = turn % 2
        found = [
            remote(
                SQ.at[side],
                RQ.at[slot, 1 - side],
                first_s.at[side],
                halo_r.at[slot, 1 - side],
                across(0, side),
            )
        ]
        for number in CORNERS:
            cx, cy, _ = lattice_velocities[number]
            if cy == -1:
                k = corner_of(side, number)
                found.append(
                    remote(
                        SC.at[k],
                        RC.at[slot, k],
                        first_s.at[2 + k],
                        halo_r.at[slot, 2 + k],
                        across(cx, side),
                    )
                )
        return found

    def planes(D, turn):
        pairs = ((0, X, 0, 1), (CROSS, 1, X + 1, -1))
        return [
            remote(
                D.at[pl.ds(start, CROSS), plane, inner],
                D.at[pl.ds(start, CROSS), land, inner],
                first_s.at[6 + k],
                halo_r.at[turn % 2, 6 + k],
                to(cx, 0),
            )
            for k, (start, plane, land, cx) in enumerate(pairs)
        ]

    def send_side(turn, side):
        for number in CORNERS:
            cx, cy, _ = lattice_velocities[number]
            if cy == -1:
                edge = ROWS + (X - 1 if cx == 1 else 0)
                row = SY[side, place_of(side, number), edge : edge + 1, :]
                SC[corner_of(side, number)] = row
        copies = messages(turn, side)
        for copy in copies[1:]:
            copy.start()
        for number in DOWN_Y:
            j = place_of(side, number)
            for x in range(0, X, CODED):
                value = SY[side, j, ROWS + x : ROWS + x + CODED, :]
                SQ[side, j, x : x + CODED, :] = encode(value, weight_of(number))
        copies[0].start()

    def receive_side(D, turn, side):
        slot = turn % 2
        for copy in messages(turn, side):
            copy.wait_send()
        for copy in messages(turn, 1 - side):
            copy.wait_recv()
        for number in UP_Y:
            j = place_of(side, number)
            for x in range(0, X, CODED):
                value = decode(RQ[slot, side, j, x : x + CODED, :], weight_of(number))
                RY[slot, side, j, ROWS + x : ROWS + x + CODED, :] = value
        for number in range(COUNT):
            cx, cy, _ = lattice_velocities[number]
            if cx == 0:
                continue
            plane, place = (0, ROWS - 1) if cx == 1 else (X + 1, ROWS + X)
            if cy == 1:
                j = place_of(side, number)
                RY[slot, side, j, place : place + 1, :] = RC[slot, corner_of(side, number)]
            else:
                row = LOW - cy + side * (W - 1 + 2 * cy)
                k = slot_of(side, number)
                E[slot, side, k, place : place + 1, :] = D[k, plane, pl.ds(row, 1), :]

    def inward_rows(D, x):
        for side in range(2):
            row = LOW + edge_rows[side]
            for j, number in enumerate(inward[side]):
                D[SLOT[number], x + 1, row : row + 1, :] = EI[side, j, pl.ds(x, 1), :]

    def corner_rows(D, b):
        for x, wanted in ((0, -1), (X - 1, 1)):
            inward_rows(D, x)
            for side in range(2):
                row = LOW + edge_rows[side]
                for number in range(COUNT):
                    cx, cy, _ = lattice_velocities[number]
                    if cx != wanted or number in inward[side]:
                        continue
                    at = slice(ROWS + x, ROWS + x + 1)
                    if cy:
                        value = SY[side, outward[side].index(number), at, :]
                    else:
                        value = E[b, side, SLOT[number], at, :]
                    D[SLOT[number], x + 1, row : row + 1, :] = value

    far = lax.rem(i, 2)
    near = 1 - far
    span = max(1, ni // 2)
    inside = (lax.rem(i + 1, ni) // 2 + span - 1) // span
    lead = far + inside * (near - far)
    follow = 1 - lead

    def first(x, carry):
        for h in range(halves):
            field = [F[number, x, pl.ds(ROWS * h, ROWS), :] for number in range(COUNT)]
            values = collide(field)
            for number in range(COUNT):
                A[SLOT[number], x + 1, pl.ds(LOW + ROWS * h, ROWS), :] = values[number]
            for side, edge in ((0, 0), (1, ROWS - 1)):
                if h != (0 if side == 0 else halves - 1):
                    continue
                near = 1 if side == 0 else ROWS - 2
                for number in range(COUNT):
                    if lattice_velocities[number][1] == 0:
                        E[0, side, SLOT[number], pl.ds(ROWS + x, 1), :] = values[number][
                            edge : edge + 1
                        ]
                for j, number in enumerate(outward[side]):
                    SY[side, j, pl.ds(ROWS + x, 1), :] = values[number][edge : edge + 1]
                    E[0, side, SLOT[number], pl.ds(ROWS + x, 1), :] = values[number][
                        near : near + 1
                    ]
        return carry

    for c in range(chunks):
        loads[c].wait()
        if c + AHEAD < chunks:
            loads[c + AHEAD].start()
        lax.fori_loop(c * step_x, (c + 1) * step_x, first, 0)

    for copy in scalars:
        copy.wait()
    ray = X * nd
    lane = lax.broadcasted_iota(jnp.int32, (8, NZ), 1)
    entries = jnp.full((8, NZ), direct[0].astype(jnp.float32), jnp.float32)
    for k in range(bumps):
        for kind in range(5):
            factor = SCALE if kind == 0 else (LOG2E / ray if kind == 1 else 1.0)
            entries = jnp.where(lane == kind * bumps + k, par[kind, 0, k] * factor, entries)
    gain = pltpu.roll(entries, bumps, 1)
    shift = gain * gain - jnp.log2(entries)
    ratios = entries / gain
    for kind in (3, 4):
        ratios = jnp.where(
            lane < kind * bumps, ratios, entries / pltpu.roll(entries, (kind - 1) * bumps, 1)
        )
    table = jnp.where(lane < 2 * bumps, shift, ratios)
    table = jnp.where(lane < bumps, 2.0 * entries, table)
    PC[i] = jnp.where(lane < 5 * bumps, table, entries)[0:1]

    pl.semaphore_wait(barrier, everyone - 1)
    shares = [
        remote(PC.at[i], PC.at[i], second_s.at[o], pa_r.at[o], to(0, o)) for o in range(1, ni)
    ]
    for side in (far, near):
        send_side(0, side)
    for copy in planes(A, 0) + shares:
        copy.start()

    source, target = A, B
    for turn in range(1, STEPS):

        def middle(x, carry, source=source, target=target, turn=turn):
            update(source, target, turn % 2, x)
            return carry

        lax.fori_loop(1, X - 1, middle, 0, unroll=2)
        for copy in planes(source, turn - 1):
            copy.wait()
        for side in (lead, follow):
            receive_side(source, turn - 1, side)
            edges((turn - 1) % 2, turn % 2, side)
            send_side(turn, side)
        for x in (0, X - 1):
            middle(x, 0)
        corner_rows(target, turn % 2)
        if turn == STEPS - 1:
            fill_rows(target, turn % 2)
        for copy in planes(target, turn):
            copy.start()
        if turn == STEPS - 1:
            for x in (1, X - 2):
                inward_rows(target, x)
            for copy in shares:
                copy.wait()
            parts = send_parts(target, turn % 2)

        def settle(x, carry, target=target):
            inward_rows(target, x)
            return carry

        lax.fori_loop(1, X - 1, settle, 0)
        source, target = target, source

    def flow_of(field):
        density, momentum = moments(field)
        inverse = 1.0 / density
        return [momentum[axis] * inverse for axis in (1, 2, 0)]

    def last(x, carry):
        for start in starts:
            field = streamed(source, x, start)
            for number in range(COUNT):
                F[number, x, pl.ds(start, ROWS), :] = field[number]
            for place, value in enumerate(flow_of(field)):
                U[place, x + 1, pl.ds(LOW + start, ROWS), :] = value
        return carry

    def expand(m, carry):
        for block in range(PA.shape[1] // 8):
            line = lax.broadcasted_iota(jnp.int32, (8, NZ), 0) + 8 * block
            chosen = jnp.where(lane == line, jnp.broadcast_to(PC[m], (8, NZ)), 0.0)
            value = jnp.sum(chosen, axis=1, keepdims=True)
            PA[m, pl.ds(8 * block, 8), :] = jnp.broadcast_to(value, (8, NZ))
        return carry

    lax.fori_loop(0, ni, expand, 0, unroll=2)
    lax.fori_loop(1, X - 1, last, 0, unroll=2)
    for copy in planes(source, STEPS - 1):
        copy.wait()
    for x in (0, X - 1):
        last(x, 0)
    for side in (lead, follow):
        receive_side(source, STEPS - 1, side)
    for part in parts:
        part.wait()
    for side in range(2):
        row = edge_rows[side]
        for x in range(0, X, ROWS):
            field = edge_streamed((STEPS - 1) % 2, side, x)
            for place, value in enumerate(flow_of(field)):
                for r in range(ROWS):
                    U[place, x + r + 1, LOW + row : LOW + row + 1, :] = value[r : r + 1]
    ghosts(source, (STEPS - 1) % 2)

    def spin(x, carry):
        def across_x(place):
            return (U[place, x + 2, inner, :] - U[place, x, inner, :]) * 0.5

        def across_y(place):
            above = U[place, x + 1, pl.ds(LOW + 1, W), :]
            return (above - U[place, x + 1, pl.ds(LOW - 1, W), :]) * 0.5

        def across_z(place):
            value = U[place, x + 1, inner, :]
            return (pltpu.roll(value, NZ - 1, 1) - pltpu.roll(value, 1, 1)) * 0.5

        spin_x = across_y(1) - across_z(0)
        spin_y = across_z(2) - across_x(1)
        spin_z = across_x(0) - across_y(2)
        size = jnp.sqrt(spin_x * spin_x + spin_y * spin_y + spin_z * spin_z)
        rounded = size.astype(jnp.bfloat16)
        vort[x] = rounded
        value = rounded.astype(jnp.float32)
        level = (value / (value + level_offset)) * SCALE
        L[x] = level
        G[x] = jnp.exp2(-(level * level))
        return carry

    lax.fori_loop(0, X, spin, 0, unroll=8)

    owner = i // ratio
    mine = d * ratio + lax.rem(i, ratio)

    def row(m, r):
        return jnp.broadcast_to(PA[m, pl.ds(r, 1), :], (ROWS, NZ))

    def blend(backward, through, colors, local_through, local_colors):
        fade = jnp.where(backward, local_through, 1.0)
        lit = jnp.where(backward, 1.0, through)
        mixed = [color * fade + lit * local for color, local in zip(colors, local_colors)]
        return through * local_through, mixed

    def piece(o, m):
        return remote(
            PS.at[m],
            PR.at[mine],
            first_s.at[o],
            pr_r.at[mine],
            {"depth": owner, "image": m},
        )

    def render(o, carry):
        m = lax.rem(i + 1 + o, ni)
        backward = row(m, 5 * bumps) > 0.5
        sign = jnp.where(backward, 1.0, -1.0)

        def along(x, state):
            new = []
            levels = [L[x, pl.ds(ROWS * h, ROWS), :] for h in range(halves)]
            totals = [[None] * 4 for h in range(halves)]
            for k in range(bumps):
                centre = row(m, k)
                shift = row(m, bumps + k)
                gains = [row(m, (1 + j) * bumps + k) for j in range(1, 4)]
                for h in range(halves):
                    bump = jnp.exp2(levels[h] * centre - shift)
                    for j in range(4):
                        term = gains[j - 1] * bump if j else bump
                        totals[h][j] = term if k == 0 else totals[h][j] + term
            for h in range(halves):
                signed, seen, *colors = state[5 * h : 5 * h + 5]
                common = G[x, pl.ds(ROWS * h, ROWS), :]
                signed = signed + totals[h][0] * (common * sign)
                now = jnp.exp2(signed)
                weight = (seen - now) * common
                colors = [color + weight * total for color, total in zip(colors, totals[h][1:])]
                new += [signed, now, *colors]
            return tuple(new)

        zero = jnp.zeros((ROWS, NZ), jnp.float32)
        start = (zero, jnp.ones((ROWS, NZ), jnp.float32), zero, zero, zero) * halves
        state = lax.fori_loop(0, X, along, start, unroll=8)
        parts = []
        for h in range(halves):
            signed, seen, *colors = state[5 * h : 5 * h + 5]
            through = jnp.where(backward, jnp.exp2(-signed), seen)
            factor = jnp.where(backward, -through, 1.0)
            parts.append([color * factor for color in colors] + [through])
        for j in range(4):
            value = jnp.concatenate([part[j] for part in parts], axis=0)
            unit = PIECE / (bumps if j < 3 else 1.0)
            steps = jnp.clip(jnp.round(value * unit - 32768.0), -32768.0, 32767.0)
            PS[m, j] = steps.astype(jnp.int32).astype(jnp.int16)
        local_target = jnp.logical_and(owner == d, m == i)

        @pl.when(local_target)
        def _():
            PR[mine] = PS[m]

        @pl.when(jnp.logical_not(local_target))
        def _():
            piece(o, m).start()

        return carry

    lax.fori_loop(0, ni, render, 0)
    for side in range(2):
        edge = edge_rows[side]
        for x in range(0, X, ROWS):
            field = edge_streamed((STEPS - 1) % 2, side, x)
            for number in range(COUNT):
                for r in range(ROWS):
                    F[number, x + r, edge : edge + 1, :] = field[number][r : r + 1]

    def sent(o, carry):
        m = lax.rem(i + 1 + o, ni)

        @pl.when(jnp.logical_not(jnp.logical_and(owner == d, m == i)))
        def _():
            piece(o, m).wait_send()

        return carry

    def arrived(slot, carry):
        @pl.when(jnp.logical_not(jnp.logical_and(owner == d, slot == mine)))
        def _():
            remote(
                PS.at[0], PR.at[slot], first_s.at[0], pr_r.at[slot], {"depth": d, "image": i}
            ).wait_recv()

        return carry

    lax.fori_loop(0, nd * ratio, arrived, 0)
    backward = jnp.broadcast_to(PA[i, pl.ds(5 * bumps, 1), :], (W, NZ)) > 0.5
    for part in range(ratio):
        through = jnp.ones((W, NZ), jnp.float32)
        colors = [jnp.zeros((W, NZ), jnp.float32)] * 3
        for slab in range(nd):
            local = []
            for j in range(4):
                unit = (bumps if j < 3 else 1.0) / PIECE
                code = PR[slab * ratio + part, j].astype(jnp.int32).astype(jnp.float32)
                local.append(code * unit + 32768.0 * unit)
            through, colors = blend(backward, through, colors, local[3], local[:3])
        for j, value in enumerate(colors + [1.0 - through]):
            img[0, j, part * W : (part + 1) * W, :] = value
    lax.fori_loop(0, ni, sent, 0)


def put_out(pieces, F, vort, img, F_out, vort_out, img_out, sems):
    step = F.shape[1] // pieces
    copies = [
        pltpu.make_async_copy(
            F.at[:, pl.ds(c * step, step)], F_out.at[:, pl.ds(c * step, step)], sems.at[c]
        )
        for c in range(pieces)
    ]
    copies.append(pltpu.make_async_copy(vort, vort_out, sems.at[pieces]))
    copies.append(pltpu.make_async_copy(img, img_out, sems.at[pieces + 1]))
    for copy in copies:
        copy.start()
    for copy in copies:
        copy.wait()


def on_device(populations, transfer, direction):
    nd, ni = lax.axis_size("depth"), lax.axis_size("image")
    count, X, W, NZ = populations.shape
    bumps = transfer.shape[2]
    assert transfer.shape[0] == 1 and ni % nd == 0 and W % ROWS == 0 and W >= 2 * ROWS and X % CODED == 0
    sizes = (nd, ni, X, W, NZ, bumps)
    ratio = ni // nd
    padded = W + 2 * ROWS
    f32 = jnp.float32
    table = -(-(5 * bumps + 1) // 8) * 8
    dma = pltpu.SemaphoreType.DMA
    results = pl.pallas_call(
        functools.partial(kernel, sizes),
        out_shape=(
            pltpu.VMEM(populations.shape, f32),
            pltpu.VMEM((X, W, NZ), jnp.bfloat16),
            pltpu.VMEM((1, 4, ratio * W, NZ), f32),
        ),
        in_specs=[
            pl.BlockSpec(memory_space=pl.ANY),
            pl.BlockSpec(memory_space=pl.ANY),
            pl.BlockSpec(memory_space=pl.ANY),
        ],
        out_specs=(
            pl.BlockSpec(memory_space=pltpu.VMEM),
            pl.BlockSpec(memory_space=pltpu.VMEM),
            pl.BlockSpec(memory_space=pltpu.VMEM),
        ),
        scratch_shapes=[
            pltpu.VMEM((COUNT, X + 2, padded, NZ), f32),
            pltpu.VMEM((COUNT, X + 2, padded, NZ), f32),
            pltpu.VMEM((2, 2, COUNT, X + 2 * ROWS, NZ), f32),
            pltpu.VMEM((2, CROSS, X + 2 * ROWS, NZ), f32),
            pltpu.VMEM((2, CROSS, X, NZ), f32),
            pltpu.VMEM((2, 2, CROSS, X + 2 * ROWS, NZ), f32),
            pltpu.VMEM((2, CROSS, X, NZ), jnp.int16),
            pltpu.VMEM((2, 2, CROSS, X, NZ), jnp.int16),
            pltpu.VMEM((4, 1, NZ), f32),
            pltpu.VMEM((2, 4, 1, NZ), f32),
            pltpu.VMEM((3, X + 2, padded, NZ), f32),
            pltpu.VMEM((2, 3, X, NZ), jnp.int16),
            pltpu.VMEM((2, 3, X, NZ), jnp.int16),
            pltpu.VMEM((2, 3, W, NZ), f32),
            pltpu.VMEM((2, 3, W, NZ), f32),
            pltpu.VMEM((4, 8, NZ), f32),
            pltpu.VMEM((4, 8, NZ), f32),
            pltpu.VMEM((X, W, NZ), f32),
            pltpu.VMEM((X, W, NZ), f32),
            pltpu.SMEM((5, 1, bumps), f32),
            pltpu.SMEM((1,), jnp.int32),
            pltpu.VMEM((ni, 1, NZ), f32),
            pltpu.VMEM((ni, table, NZ), f32),
            pltpu.VMEM((ni, 4, W, NZ), jnp.int16),
            pltpu.VMEM((nd * ratio, 4, W, NZ), jnp.int16),
            dma((max(8, ni),)),
            dma((max(8, ni),)),
            dma((2, 8)),
            dma((8,)),
            dma((ni,)),
            dma((nd * ratio,)),
        ],
        compiler_params=pltpu.CompilerParams(
            collective_id=0, has_side_effects=True, vmem_limit_bytes=56 << 20
        ),
    )(populations, transfer.transpose(1, 0, 2), direction)
    pieces = 8
    return pl.pallas_call(
        functools.partial(put_out, pieces),
        out_shape=tuple(jax.ShapeDtypeStruct(r.shape, r.dtype) for r in results),
        in_specs=[pl.BlockSpec(memory_space=pltpu.VMEM)] * 3,
        out_specs=(pl.BlockSpec(memory_space=pl.ANY),) * 3,
        scratch_shapes=[dma((pieces + 2,))],
        compiler_params=pltpu.CompilerParams(vmem_limit_bytes=1 << 20),
    )(*results)


def solution(mesh):
    in_specs = (P(None, "depth", "image", None), P("image", None, None), P("image"))
    out_specs = (
        P(None, "depth", "image", None),
        P("depth", "image", None),
        P("image", None, "depth", None),
    )
    return jax.shard_map(
        on_device, mesh=mesh, in_specs=in_specs, out_specs=out_specs, check_vma=False
    )
```
